128 devices in a mesh: tile: 32 (over y, z, core), batch: 4 (over x).
Axes of the slice: x: 4, y: 4, z: 4, core: 2. Of those that a mesh axis runs over, the one named last changes fastest.
Arguments:
- states: bfloat16 [4, 256, 16, 16, 256], P('batch', 'tile'), may hold values from -6 to 6
- cotangent: bfloat16 [4, 256, 16, 16, 256], P('batch', 'tile'), may hold values from -6 to 6
- beside_slot: int32 [256, 8], replicated, may hold values from 0 to 255, as said below
- beside_code: int32 [256, 8], replicated, may hold values from 0 to 7
- mixers: bfloat16 [2, 256, 256], replicated, may hold values from -0.375 to 0.375
- stencils: float32 [2, 9, 256], replicated, may hold values from -2 to 2
- shifts: float32 [2, 256], replicated, may hold values from -3 to 3
Outputs:
- outcome: bfloat16 [4, 256, 16, 16, 256], P('batch', 'tile')
- state_grad: bfloat16 [4, 256, 16, 16, 256], P('batch', 'tile')
- mixer_grads: float32 [2, 256, 256], replicated
- stencil_grads: float32 [2, 9, 256], replicated
- shift_grads: float32 [2, 256], replicated
The draws below stay inside these ranges and needn't reach their ends.
Inputs may be any that keep to these rules, and one draw needn't show every extreme that they name: `beside_slot`: tiles are numbered by slot; the tiles of one aligned block of 8 slots have 8 * 8 entries, of which at most 2 name slots of any one other block, and in every block exactly 2 entries name one other block; how many entries of a block name other blocks varies from block to block.
All inputs are finite; a program needn't handle non-finite values.
Results may differ from the reference program's by a relative error of at most 0.009.
Values may be sent and summed in bfloat16 or wider, within the bound.
No kernel may reach another device: no remote copies, remote signals or barrier semaphores. Data moves between devices by JAX's collectives and lax.ppermute only.
A program may use at most 128 MiB of HBM per device.

```python
import math
import jax
import jax.numpy as jnp
from jax import lax

C = 256
P_SIZE = 16
TILE_DEV = 8
CAP = 2
NT = 256
SAMPLES = 4


def draw_beside_slot(key, part):
    groups = NT // TILE_DEV
    entries = 8 * TILE_DEV
    highest = min(entries, (groups - 1) * CAP)
    key_count, key_rank, key_peer, key_local = jax.random.split(key, 4)
    remote_count = jax.random.randint(key_count, (groups, 1), CAP, highest + 1)
    ranks = jax.vmap(lambda sub: jax.random.permutation(sub, entries))(jax.random.split(key_rank, groups))
    offsets = jax.vmap(lambda sub: jax.random.permutation(sub, groups - 1) + 1)(jax.random.split(key_peer, groups))
    which = jnp.minimum(ranks // CAP, groups - 2)
    shifted = jnp.take_along_axis(offsets, which, axis=1)
    home = jnp.arange(groups, dtype=jnp.int32)[:, None]
    owner = jnp.where(ranks < remote_count, (home + shifted) % groups, home)
    local = jax.random.randint(key_local, (groups, entries), 0, TILE_DEV)
    return (owner * TILE_DEV + local).reshape(NT, 8).astype(jnp.int32)


def with_ends(values, stream_key, least, top_value):
    dims = values.shape
    index_at = [jax.random.randint(jax.random.fold_in(stream_key, axis), (), 0, dims[axis]) for axis in range(len(dims))]
    values = values.at[tuple(index_at)].set(least)
    longest = dims.index(max(dims))
    index_at[longest] = (index_at[longest] + 1) % dims[longest]
    return values.at[tuple(index_at)].set(top_value)


def steps_of(stream_key, dims, cuts, least, high):
    level = 1.0
    for axis_at, shards_of in cuts:
        heights = jax.random.uniform(jax.random.fold_in(jax.random.fold_in(stream_key, 6), axis_at), (shards_of,), jnp.float32, least / len(cuts), high / len(cuts))
        level = level * jnp.repeat(jnp.exp(heights), dims[axis_at] // shards_of).reshape((-1,) + (1,) * (len(dims) - 1 - axis_at))
    return level


def gaussian(key, extent, spread, limit, cuts=(), held_as=jnp.bfloat16):
    array = spread * jax.random.normal(key, extent, jnp.float32)
    if cuts:
        array = array * steps_of(key, extent, cuts, -0.22, 0.18)
    return jnp.clip(array, -limit, limit).astype(held_as)


def setup_inputs(seed: int = 0) -> dict:
    key_of = jax.random.split(jax.random.key(seed), 8)
    states = gaussian(key_of[0], (SAMPLES, NT, P_SIZE, P_SIZE, C), 1.0, 6.0, ((0, 4), (1, 32)))
    cotangent = gaussian(key_of[1], (SAMPLES, NT, P_SIZE, P_SIZE, C), 1.0, 6.0, ((0, 4), (1, 32)))
    beside_slot = draw_beside_slot(jax.random.fold_in(key_of[7], 71), 0)
    beside_code = with_ends(jax.random.randint(key_of[3], (NT, 8), 0, 8), jax.random.fold_in(key_of[3], 1), 0, 7).astype(jnp.int32)
    mixers = gaussian(key_of[4], (2, C, C), C ** -0.5, 0.375)
    stencils = gaussian(key_of[5], (2, 9, C), 0.33, 2.0, (), jnp.float32)
    shifts = gaussian(key_of[6], (2, C), 0.5, 3.0, (), jnp.float32)
    return {"states": states, "cotangent": cotangent, "beside_slot": beside_slot, "beside_code": beside_code, "mixers": mixers, "stencils": stencils, "shifts": shifts}


SQRT_HALF = 0.7071067811865476
INV_ROOT_TAU = 0.3989422804014327

def gelu_exact(value):
    return 0.5 * value * (1.0 + lax.erf(value * SQRT_HALF))

def gelu_slope(value):
    return 0.5 * (1.0 + lax.erf(value * SQRT_HALF)) + value * jnp.exp(-0.5 * value * value) * INV_ROOT_TAU

def rim_rows(field):
    return jnp.stack([field[:, :, 0], field[:, :, :, -1], field[:, :, -1], field[:, :, :, 0]], axis=2)

def assemble(field, panels, flip_bits):
    turned = jnp.where(flip_bits[None, :, :, None, None] == 1, panels[:, :, :, ::-1], panels)
    corners = turned[:, :, 4:, 0]
    top_row = jnp.concatenate([corners[:, :, 3:4], turned[:, :, 0], corners[:, :, 0:1]], axis=2)
    bottom = jnp.concatenate([corners[:, :, 2:3], turned[:, :, 2], corners[:, :, 1:2]], axis=2)
    middle = jnp.concatenate([turned[:, :, 3][:, :, :, None], field, turned[:, :, 1][:, :, :, None]], axis=3)
    return jnp.concatenate([top_row[:, :, None], middle, bottom[:, :, None]], axis=2)

def stencil_apply(padded, kernel):
    side_len = padded.shape[2] - 2
    running = jnp.zeros(padded.shape[:2] + (side_len, side_len, padded.shape[4]), jnp.float32)
    for row_at in range(3):
        for col_at in range(3):
            window = padded[:, :, row_at:row_at + side_len, col_at:col_at + side_len]
            running = running + kernel[3 * row_at + col_at] * window.astype(jnp.float32)
    return running

def stencil_back(grad, kernel):
    widened = grad.astype(jnp.float32)
    running = jnp.zeros(grad.shape[:2] + (grad.shape[2] + 2, grad.shape[3] + 2, grad.shape[4]), jnp.float32)
    for row_at in range(3):
        for col_at in range(3):
            running = running + jnp.pad(kernel[3 * row_at + col_at] * widened, ((0, 0), (0, 0), (row_at, 2 - row_at), (col_at, 2 - col_at), (0, 0)))
    return running

def stencil_grad(grad, padded):
    side_len = grad.shape[2]
    widened = grad.astype(jnp.float32)
    terms = []
    for row_at in range(3):
        for col_at in range(3):
            window = padded[:, :, row_at:row_at + side_len, col_at:col_at + side_len].astype(jnp.float32)
            terms.append(lax.optimization_barrier(jnp.sum(widened * window, axis=(0, 1, 2, 3))))
    return jnp.stack(terms)

def halo_parts(padded_grad, flip_bits):
    side_len = padded_grad.shape[2] - 2
    side_parts = jnp.stack([padded_grad[:, :, 0, 1:-1], padded_grad[:, :, 1:-1, -1], padded_grad[:, :, -1, 1:-1], padded_grad[:, :, 1:-1, 0]], axis=2)
    corner_vals = jnp.stack([padded_grad[:, :, 0, -1], padded_grad[:, :, -1, -1], padded_grad[:, :, -1, 0], padded_grad[:, :, 0, 0]], axis=2)
    flip_wide = flip_bits[None, :, :, None, None]
    side_parts = jnp.where(flip_wide[:, :, :4] == 1, side_parts[:, :, :, ::-1], side_parts)
    positions = jnp.arange(side_len)
    first_spot = (positions == 0).astype(jnp.float32)[:, None]
    last_spot = (positions == side_len - 1).astype(jnp.float32)[:, None]
    corner_spot = jnp.where(flip_wide[:, :, 4:] == 1, last_spot, first_spot)
    return jnp.concatenate([side_parts, corner_spot * corner_vals[:, :, :, None]], axis=2)

def add_rims(inner, rim_grad):
    inner = inner.at[:, :, 0].add(rim_grad[:, :, 0])
    inner = inner.at[:, :, :, -1].add(rim_grad[:, :, 1])
    inner = inner.at[:, :, -1].add(rim_grad[:, :, 2])
    inner = inner.at[:, :, :, 0].add(rim_grad[:, :, 3])
    return inner

def keep_same(group):
    return group

def block_pass(states, cotangent, panel_fetch, send_back, flip_bits, mixers, stencils, shifts, early):
    shape = states.shape
    channels = shape[4]
    padded_in = assemble(states, panel_fetch(states), flip_bits)
    conv_first = stencil_apply(padded_in, stencils[0]).astype(jnp.bfloat16)
    flat_first = conv_first.reshape(-1, channels)
    hidden = jnp.dot(flat_first, mixers[0], preferred_element_type=jnp.float32) + shifts[0]
    active = gelu_exact(hidden).astype(jnp.bfloat16).reshape(shape)
    padded_mid = assemble(active, panel_fetch(active), flip_bits)
    conv_second = stencil_apply(padded_mid, stencils[1]).astype(jnp.bfloat16)
    flat_second = conv_second.reshape(-1, channels)
    outcome = (states.reshape(-1, channels).astype(jnp.float32) + jnp.dot(flat_second, mixers[1], preferred_element_type=jnp.float32) + shifts[1]).astype(jnp.bfloat16)
    upstream = cotangent.reshape(-1, channels)
    mixer_second = lax.dot_general(flat_second, upstream, (((0,), (0,)), ((), ())), preferred_element_type=jnp.float32)
    shift_second = lax.optimization_barrier(jnp.sum(upstream.astype(jnp.float32), axis=0))
    grad_second = lax.dot_general(upstream, mixers[1], (((1,), (1,)), ((), ())), preferred_element_type=jnp.float32).astype(jnp.bfloat16).reshape(shape)
    stencil_second = stencil_grad(grad_second, padded_mid)
    later = early((mixer_second, stencil_second, shift_second))
    grad_active = send_back(stencil_back(grad_second, stencils[1]))
    grad_hidden = (grad_active.reshape(-1, channels) * gelu_slope(hidden)).astype(jnp.bfloat16)
    mixer_first = lax.dot_general(flat_first, grad_hidden, (((0,), (0,)), ((), ())), preferred_element_type=jnp.float32)
    shift_first = lax.optimization_barrier(jnp.sum(grad_hidden.astype(jnp.float32), axis=0))
    grad_conv = lax.dot_general(grad_hidden, mixers[0], (((1,), (1,)), ((), ())), preferred_element_type=jnp.float32).astype(jnp.bfloat16).reshape(shape)
    stencil_first = stencil_grad(grad_conv, padded_in)
    state_grad = (cotangent.astype(jnp.float32) + send_back(stencil_back(grad_conv, stencils[0]))).astype(jnp.bfloat16)
    return (outcome.reshape(shape), state_grad, (mixer_first, stencil_first, shift_first), later)

def reference(states, cotangent, beside_slot, beside_code, mixers, stencils, shifts):
    tile_total = beside_slot.shape[0]
    side_len = states.shape[2]
    channels = states.shape[4]
    flip_bits = beside_code % 2
    source = (beside_slot * 4 + beside_code // 2).reshape(-1).astype(jnp.int32)

    def panel_fetch(field):
        rims = rim_rows(field).reshape(1, tile_total * 4, side_len, channels)
        return rims[:, source].reshape(1, tile_total, 8, side_len, channels)

    def send_back(padded_grad):
        parts = halo_parts(padded_grad, flip_bits).reshape(tile_total * 8, side_len, channels)
        rim_grad = jnp.zeros((tile_total * 4, side_len, channels), jnp.float32).at[source].add(parts)
        return add_rims(padded_grad[:, :, 1:-1, 1:-1], rim_grad.reshape(1, tile_total, 4, side_len, channels))

    def one_sample(carry, pair):
        outcome, state_grad, first, second = block_pass(pair[0][None], pair[1][None], panel_fetch, send_back, flip_bits, mixers, stencils, shifts, keep_same)
        carry = jax.tree.map(lambda held, term: held + term, carry, (first, second))
        return (carry, (outcome[0], state_grad[0]))
    zero_set = (jnp.zeros((channels, channels), jnp.float32), jnp.zeros((9, channels), jnp.float32), jnp.zeros((channels,), jnp.float32))
    sums, results = lax.scan(one_sample, (zero_set, zero_set), (states, cotangent))
    scale = 1.0 / math.sqrt(states.shape[0] * tile_total * side_len * side_len)
    first, second = sums
    mixer_grads = jnp.stack([first[0], second[0]]) * scale
    stencil_grads = jnp.stack([first[1], second[1]]) * scale
    shift_grads = jnp.stack([first[2], second[2]]) * scale
    return (results[0], results[1], mixer_grads, stencil_grads, shift_grads)
```

```python
import math

import jax
import jax.numpy as jnp
import numpy as np
from jax import lax
from jax.experimental import pallas as pl
from jax.experimental.pallas import tpu as pltpu
from jax.sharding import Mesh
from jax.sharding import PartitionSpec as P


TILE = ("tile_0", "tile_1", "tile_2")
SQRT_HALF = 0.7071067811865476
INV_ROOT_TAU = 0.3989422804014327

F32 = jnp.float32
BF16 = jnp.bfloat16
I32 = jnp.int32

S = 16
T = 8
CELLS = S * S
SIDE_TAPS = {0: (0, 1, 2), 1: (2, 5, 8), 2: (6, 7, 8), 3: (0, 3, 6)}
CORNER_TAP = {4: 2, 5: 8, 6: 6, 7: 0}
VMEM_LIMIT = 60 * 1024 * 1024


def line_cell(d, i):
    if d == 0:
        return i
    if d == 1:
        return S * i + S - 1
    if d == 2:
        return S * (S - 1) + i
    if d == 3:
        return S * i
    if i != 0:
        return None
    return {4: S - 1, 5: CELLS - 1, 6: S * (S - 1), 7: 0}[d]


def selection():
    sel = np.zeros((256, CELLS), np.float32)
    for d in range(8):
        for f in range(2):
            for i in range(S):
                cell = line_cell(d, S - 1 - i if f else i)
                if cell is not None:
                    sel[(2 * d + f) * S + i, cell] = 1.0
    return sel


def spreading():
    out = np.zeros((CELLS, 128), np.float32)
    for d in range(4):
        for i in range(S):
            out[line_cell(d, i), d * S + i] = 1.0
            out[line_cell(d, i), 64 + d * S + i] = 1.0
    return out


def shifting():
    out = np.zeros((512, CELLS), np.float32)
    for i in range(S):
        for j in range(S):
            if j > 0:
                out[S * i + j, S * i + j - 1] = 1.0
            if j < S - 1:
                out[256 + S * i + j, S * i + j + 1] = 1.0
    return out


def dot(a, b):
    return jnp.dot(a, b, preferred_element_type=F32)


def dot_t(a, b):
    return lax.dot_general(a, b, (((1,), (1,)), ((), ())), preferred_element_type=F32)


def t_dot(a, b):
    return lax.dot_general(a, b, (((0,), (0,)), ((), ())), preferred_element_type=F32)


def iota(shape, axis):
    return lax.broadcasted_iota(I32, shape, axis)


def neighbours(x):
    place = iota(x.shape, 0)
    before = jnp.where(place == 0, 0.0, pltpu.roll(x, 1, 0))
    after = jnp.where(place == S - 1, 0.0, pltpu.roll(x, S - 1, 0))
    return before, after


def down(x):
    return jnp.concatenate([jnp.zeros((S, x.shape[1]), x.dtype), x[: CELLS - S]], axis=0)


def up(x):
    return jnp.concatenate([x[S:], jnp.zeros((S, x.shape[1]), x.dtype)], axis=0)


def conv_inner(left, centre, right, w):
    rows = [w[3 * a] * left + w[3 * a + 1] * centre + w[3 * a + 2] * right for a in range(3)]
    return rows[1] + down(rows[0]) + up(rows[2])


def back_inner(left, centre, right, w):
    rows = [w[3 * a] * right + w[3 * a + 1] * centre + w[3 * a + 2] * left for a in range(3)]
    return rows[1] + up(rows[0]) + down(rows[2])


def tap_rows(ref, layer):
    return [ref[layer, k : k + 1, :] for k in range(9)]


def fill_tap_sets(taps_ref, stencil_ref, layer):
    w = tap_rows(stencil_ref, layer)
    zero = jnp.zeros_like(w[0])
    for d in range(8):
        if d < 4:
            three = [w[k] for k in SIDE_TAPS[d]]
        else:
            three = [zero, w[CORNER_TAP[d]], zero]
        for f in range(2):
            for m, row in enumerate(three[::-1] if f else three):
                taps_ref[2 * d + f, m : m + 1, :] = row


def tile_of(ref, t):
    return ref[pl.ds(pl.multiple_of(t * CELLS, CELLS), CELLS), :]


def put_tile(ref, t, value):
    ref[pl.ds(pl.multiple_of(t * CELLS, CELLS), CELLS), :] = value


def split_store(ref, t, first, value):
    high = value.astype(BF16)
    ref[t, pl.ds(first, value.shape[0]), :] = high
    ref[t, pl.ds(64 + first, value.shape[0]), :] = (value - high.astype(F32)).astype(BF16)


def forward_lines(split_ref, buf_ref, tab_ref, w):
    place = None

    def one(t, carry):
        corner = {}
        for d in range(4, 8):
            row = buf_ref[tab_ref[0, t * 8 + d]][:8, :].astype(F32)[:1, :]
            corner[d] = w[CORNER_TAP[d]] * row
        for d in range(4):
            x = buf_ref[tab_ref[0, t * 8 + d]].astype(F32)
            before, after = neighbours(x)
            a, b, c = SIDE_TAPS[d]
            line = w[a] * before + w[b] * x + w[c] * after
            at = iota(line.shape, 0)
            if d == 0:
                line = line + jnp.where(at == 0, corner[7], 0.0)
                line = line + jnp.where(at == S - 1, corner[4], 0.0)
            if d == 2:
                line = line + jnp.where(at == 0, corner[6], 0.0)
                line = line + jnp.where(at == S - 1, corner[5], 0.0)
            split_store(split_ref, t, d * S, line)
        return carry

    del place
    lax.fori_loop(0, T, one, 0)


def rim_gradients(split_ref, rim_ref, lines_ref, tab_ref, taps_ref):
    rim_ref[...] = jnp.zeros_like(rim_ref)

    def one(i, carry):
        x = lines_ref[i].astype(F32)
        before, after = neighbours(x)
        u = taps_ref[tab_ref[3, i]]
        rim = tab_ref[2, i] >> 1
        rim_ref[rim] += u[0:1] * after + u[1:2] * x + u[2:3] * before
        return carry

    lax.fori_loop(0, 128, one, 0, unroll=8)

    def split(t, carry):
        for e in range(4):
            split_store(split_ref, t, e * S, rim_ref[t * 4 + e])
        return carry

    lax.fori_loop(0, T, split, 0)


def live_lines(dst_ref, own_ref, in_ref, tab_ref):
    def own(i, carry):
        dst_ref[i] = jnp.where(tab_ref[4, i] > 0, own_ref[i], jnp.zeros((S, 256), BF16))
        j = i + 64
        dst_ref[j] = jnp.where(tab_ref[4, j] > 0, in_ref[i, S : 2 * S], jnp.zeros((S, 256), BF16))
        return carry

    lax.fori_loop(0, 64, own, 0, unroll=8)


def gather_out(out_ref, own_ref, rims_ref, lines_ref, tab_ref):
    def one(s, carry):
        out_ref[s, 0:S] = rims_ref[tab_ref[2, 64 + s]]
        out_ref[s, S : 2 * S] = lines_ref[tab_ref[1, s]]
        own_ref[s] = lines_ref[tab_ref[5, s]]
        return carry

    lax.fori_loop(0, 64, one, 0, unroll=8)


def banks(rims_ref, lines_ref, rim_field, line_field, sel_ref):
    def one(t, carry):
        rims = dot(sel_ref[0:128, :], tile_of(rim_field, t)).astype(BF16)
        rims_ref[pl.ds(t * 8, 8)] = rims.reshape(8, S, 256)
        lines = dot(sel_ref[...], tile_of(line_field, t)).astype(BF16)
        lines_ref[pl.ds(t * 16, 16)] = lines.reshape(16, S, 256)
        return carry

    lax.fori_loop(0, T, one, 0)


def own_position():
    a, b, c = (lax.axis_index(name) for name in TILE)
    return (a * lax.axis_size(TILE[1]) + b) * lax.axis_size(TILE[2]) + c


def first_kernel(
    comb_ref, states_ref, cot_ref, sel_ref, tab_ref, out_ref, rims_ref, own_ref, lines_ref, smem, sem
):
    me = own_position()
    comb = comb_ref[...]
    groups = comb.shape[0]
    lane = iota(comb.shape, 1)
    home = iota(comb.shape, 0)
    slot = comb >> 3
    wanted = (lane < 64) & ((slot >> 3) == me) & (home != me)
    wanted_f = wanted.astype(F32)
    before = (iota((128, 128), 0) < iota((128, 128), 1)).astype(F32).astype(BF16)
    place = dot(wanted_f.astype(BF16), before)
    code = comb & 7
    rim_code = (slot & 7) * 8 + code
    tap_set = (lane & 7) * 2 + (code & 1)
    packed = (rim_code * 16 + tap_set + 1024).astype(F32)
    asked = jnp.zeros((1, 128), F32)
    for k in range(2):
        value = jnp.sum(
            jnp.where(wanted & (place == k), packed, 0.0), axis=1, keepdims=True
        )
        at = (lane >= 64) & (((lane - 64) >> 1) == home) & ((lane & 1) == k)
        asked = asked + jnp.sum(jnp.where(at, value, 0.0), axis=0, keepdims=True)
    asked = asked.astype(I32)

    own = comb_ref[pl.ds(me, 1), :]
    sub2 = iota((128, 128), 0)
    lane2 = iota((128, 128), 1)
    own_wide = jnp.broadcast_to(own, (128, 128))
    own_col = jnp.sum(
        jnp.where(sub2 == lane2, own_wide, 0).astype(F32), axis=1, keepdims=True
    ).astype(I32)
    owner_col = own_col >> 6
    owner_row = own >> 6
    same = (owner_col == owner_row) & (sub2 < 64) & (lane2 < 64)
    place_col = jnp.sum((same & (lane2 < sub2)).astype(F32), axis=1, keepdims=True).astype(I32)
    place_row = jnp.sum((same & (sub2 < lane2)).astype(F32), axis=0, keepdims=True).astype(I32)
    lane1 = iota((1, 128), 1)
    sub1 = iota((128, 1), 0)
    remote_row = owner_row != me
    slot_col = jnp.where((owner_col != me) & (sub1 < 64), owner_col * 2 + place_col, -1)
    line_col = (sub1 * 2 + (own_col & 1)).astype(F32)
    sent = jnp.sum(jnp.where(slot_col == lane2, line_col, 0.0), axis=0, keepdims=True).astype(I32)
    own_rim = (own & 511)
    own_rim = ((own_rim >> 3) & 7) * 8 + (own_rim & 7)
    in_own = lane1 < 64
    panel = jnp.where(remote_row, 64 + owner_row * 2 + place_row, own_rim)
    tab_ref[...] = jnp.zeros_like(tab_ref)
    tab_ref[0:1, :] = jnp.where(in_own, panel, 0)
    tab_ref[1:2, :] = jnp.where(in_own, sent, 0)
    tab_ref[2:3, :] = jnp.where(in_own, own_rim, (asked & 1023) >> 4)
    tab_ref[3:4, :] = jnp.where(in_own, (lane1 & 7) * 2 + (own & 1), asked & 15)
    tab_ref[4:5, :] = jnp.where(in_own, (~remote_row).astype(I32), asked >> 10)
    tab_ref[5:6, :] = jnp.where(in_own, lane1 * 2 + (own & 1), 0)
    del groups
    copy = pltpu.make_async_copy(tab_ref, smem, sem)
    copy.start()
    banks(rims_ref, lines_ref, states_ref, cot_ref, sel_ref)
    copy.wait()
    gather_out(out_ref, own_ref, rims_ref, lines_ref, smem)


def inner_kernel(states_ref, cot_ref, mixers_ref, stencils_ref, shift_ref, conv_ref, back_ref, g_ref):
    w0 = tap_rows(stencils_ref, 0)
    w1 = tap_rows(stencils_ref, 1)

    def one(t, carry):
        x = tile_of(states_ref, t)
        moved = dot(shift_ref[...], x)
        put_tile(conv_ref, t, conv_inner(moved[:CELLS], x.astype(F32), moved[CELLS:], w0))
        g = dot_t(tile_of(cot_ref, t), mixers_ref[1]).astype(BF16)
        put_tile(g_ref, t, g)
        moved = dot(shift_ref[...], g)
        put_tile(back_ref, t, back_inner(moved[:CELLS], g.astype(F32), moved[CELLS:], w1))
        return carry

    lax.fori_loop(0, T, one, 0)


def middle_kernel(
    tab_ref, in_ref, rims_in_ref, own_in_ref, conv_ref, back_ref, mixers_ref, stencils_ref,
    shifts_ref, sel_ref, spread_ref,
    active_ref, first_ref, gh_ref, gc_ref, rims_ref, lines_ref, out_ref, own_ref, c_ref, g_ref,
    buf_ref, split_ref, split2_ref, rim_ref, taps_ref,
):
    w0 = tap_rows(stencils_ref, 0)
    buf_ref[0:64] = rims_in_ref[...]
    buf_ref[64:128] = in_ref[:, 0:S, :]
    forward_lines(split_ref, buf_ref, tab_ref, w0)
    fill_tap_sets(taps_ref, stencils_ref, 1)
    live_lines(c_ref, own_in_ref, in_ref, tab_ref)

    def line_grads(b, carry):
        part = c_ref[pl.ds(b * 16, 16)].reshape(256, 256)
        g_ref[pl.ds(b * 16, 16)] = dot_t(part, mixers_ref[1]).astype(BF16).reshape(16, S, 256)
        return carry

    lax.fori_loop(0, 8, line_grads, 0)
    rim_gradients(split2_ref, rim_ref, g_ref, tab_ref, taps_ref)

    def one(t, carry):
        first = (tile_of(conv_ref, t) + dot(spread_ref[...], split_ref[t])).astype(BF16)
        put_tile(first_ref, t, first)
        hidden = dot(first, mixers_ref[0]) + shifts_ref[0:1, :]
        cdf = 0.5 * (1.0 + lax.erf(hidden * SQRT_HALF))
        active = (hidden * cdf).astype(BF16)
        put_tile(active_ref, t, active)
        slope = cdf + hidden * jnp.exp(-0.5 * hidden * hidden) * INV_ROOT_TAU
        grad = tile_of(back_ref, t) + dot(spread_ref[...], split2_ref[t])
        gh = (grad * slope).astype(BF16)
        put_tile(gh_ref, t, gh)
        put_tile(gc_ref, t, dot_t(gh, mixers_ref[0]).astype(BF16))
        return carry

    lax.fori_loop(0, T, one, 0)
    banks(rims_ref, lines_ref, active_ref, gc_ref, sel_ref)
    gather_out(out_ref, own_ref, rims_ref, lines_ref, tab_ref)


def weight_kernel(
    tab_ref, states_ref, cot_ref, active_ref, first_ref, gh_ref, gc_ref, g2_ref, rims_ref, lines_ref,
    rims_in_ref, in_ref, c_ref, g_ref, stencils_ref, shift_ref,
    pack_ref, conv_ref, back_ref,
    second_ref, h_ref, taps_ref, acc1_ref, acc2_ref, accl_ref, sums_ref, buf_ref,
):
    w0 = tap_rows(stencils_ref, 0)
    w1 = tap_rows(stencils_ref, 1)
    acc1_ref[...] = jnp.zeros_like(acc1_ref)
    acc2_ref[...] = jnp.zeros_like(acc2_ref)
    accl_ref[...] = jnp.zeros_like(accl_ref)
    sums_ref[...] = jnp.zeros_like(sums_ref)
    buf_ref[0:64] = rims_in_ref[...]
    buf_ref[64:128] = in_ref[:, 0:S, :]
    fill_tap_sets(taps_ref, stencils_ref, 1)

    def folded(x):
        return jnp.sum(x.reshape(-1, 8, 256), axis=0)

    def taps_of(acc_ref, g, left, centre, right):
        for b, x in enumerate((left, centre, right)):
            acc_ref[b] += folded(g[S:] * x[: CELLS - S])
            acc_ref[3 + b] += folded(g * x)
            acc_ref[6 + b] += folded(g[: CELLS - S] * x[S:])

    def one(t, carry):
        gc = tile_of(gc_ref, t)
        moved = dot(shift_ref[...], gc)
        gcf = gc.astype(F32)
        put_tile(back_ref, t, back_inner(moved[:CELLS], gcf, moved[CELLS:], w0))
        x = tile_of(states_ref, t)
        moved = dot(shift_ref[...], x)
        taps_of(acc1_ref, gcf, moved[:CELLS], x.astype(F32), moved[CELLS:])
        x = tile_of(active_ref, t)
        moved = dot(shift_ref[...], x)
        xf = x.astype(F32)
        second = conv_inner(moved[:CELLS], xf, moved[CELLS:], w1)
        put_tile(conv_ref, t, second)
        put_tile(second_ref, t, second.astype(BF16))
        taps_of(acc2_ref, tile_of(g2_ref, t).astype(F32), moved[:CELLS], xf, moved[CELLS:])
        sums_ref[0] += folded(tile_of(gh_ref, t).astype(F32))
        sums_ref[1] += folded(tile_of(cot_ref, t).astype(F32))
        return carry

    lax.fori_loop(0, T, one, 0)

    def halves(x):
        return x[0:8] + x[8:16]

    def first_halo(t, carry):
        for d in range(8):
            x = buf_ref[tab_ref[0, t * 8 + d]].astype(F32)
            g = lines_ref[(t * 8 + d) * 2].astype(F32)
            if d < 4:
                before, after = neighbours(x)
                for k, y in zip(SIDE_TAPS[d], (before, x, after)):
                    acc1_ref[k] += halves(g * y)
            else:
                acc1_ref[CORNER_TAP[d]] += halves(g * x)
        return carry

    lax.fori_loop(0, T, first_halo, 0)

    def second_halo(i, carry):
        x = rims_ref[(tab_ref[2, i] >> 1) * 2].astype(F32)
        g = g_ref[i].astype(F32)
        before, after = neighbours(x)
        kind = tab_ref[3, i]
        u = taps_ref[kind]
        h_ref[i] = (u[0:1] * before + u[1:2] * x + u[2:3] * after).astype(BF16)
        for m, y in enumerate((before, x, after)):
            accl_ref[kind, m] += halves(g * y)
        return carry

    lax.fori_loop(0, 128, second_halo, 0, unroll=8)
    for d in range(8):
        for f in range(2):
            if d < 4:
                taps = SIDE_TAPS[d][::-1] if f else SIDE_TAPS[d]
                for m, k in enumerate(taps):
                    acc2_ref[k] += accl_ref[2 * d + f, m]
            else:
                acc2_ref[CORNER_TAP[d]] += accl_ref[2 * d + f, 1]

    mixer_first = t_dot(first_ref[...], gh_ref[...])
    mixer_second = t_dot(second_ref[...], cot_ref[...]) + t_dot(
        h_ref[...].reshape(2048, 256), c_ref[...].reshape(2048, 256)
    )
    half = pack_ref.shape[0] // 2
    for r in range(half):
        pack_ref[r, 0:16] = mixer_first[16 * r : 16 * r + 16].astype(BF16)
        pack_ref[half + r, 0:16] = mixer_second[16 * r : 16 * r + 16].astype(BF16)
    rows = [jnp.sum(acc1_ref[k], axis=0, keepdims=True) for k in range(9)]
    rows += [jnp.sum(acc2_ref[k], axis=0, keepdims=True) for k in range(9)]
    rows += [jnp.sum(sums_ref[k], axis=0, keepdims=True) for k in range(2)]
    rows += [jnp.zeros_like(rows[0])] * 4
    for r in range(3):
        pack_ref[r, 16:24] = jnp.concatenate(rows[8 * r : 8 * r + 8], axis=0).astype(BF16)
    for r in range(3, pack_ref.shape[0]):
        pack_ref[r, 16:24] = jnp.zeros((8, 256), BF16)


def last_kernel(
    tab_ref, in_ref, rims_in_ref, own_in_ref, conv_ref, back_ref, states_ref, cot_ref, mixers_ref,
    stencils_ref, shifts_ref, spread_ref,
    outcome_ref, grad_ref,
    buf_ref, split_ref, split2_ref, rim_ref, taps_ref, lines_ref,
):
    w1 = tap_rows(stencils_ref, 1)
    buf_ref[0:64] = rims_in_ref[...]
    buf_ref[64:128] = in_ref[:, 0:S, :]
    forward_lines(split_ref, buf_ref, tab_ref, w1)
    fill_tap_sets(taps_ref, stencils_ref, 0)
    live_lines(lines_ref, own_in_ref, in_ref, tab_ref)
    rim_gradients(split2_ref, rim_ref, lines_ref, tab_ref, taps_ref)

    def one(t, carry):
        second = (tile_of(conv_ref, t) + dot(spread_ref[...], split_ref[t])).astype(BF16)
        out = tile_of(states_ref, t).astype(F32) + dot(second, mixers_ref[1]) + shifts_ref[1:2, :]
        put_tile(outcome_ref, t, out.astype(BF16))
        grad = tile_of(back_ref, t) + dot(spread_ref[...], split2_ref[t])
        put_tile(grad_ref, t, (tile_of(cot_ref, t).astype(F32) + grad).astype(BF16))
        return carry

    lax.fori_loop(0, T, one, 0)


def sum_kernel(in_ref, out_ref):
    total = in_ref[0].astype(F32)
    for r in range(1, in_ref.shape[0]):
        total = total + in_ref[r].astype(F32)
    out_ref[...] = total


def spread_kernel(a_ref, b_ref, out_ref):
    value = (a_ref[...] + b_ref[...]).astype(BF16)
    for r in range(out_ref.shape[0]):
        out_ref[r] = value


def unpack_kernel(scale, in_ref, mixer_ref, stencil_ref, shift_ref):
    half = in_ref.shape[0] // 2
    for r in range(half):
        for k in range(2):
            mixer_ref[k, 16 * r : 16 * r + 16, :] = in_ref[k * half + r, 0:16].astype(F32) * scale
    rows = [in_ref[r, 16:24].astype(F32) * scale for r in range(3)]
    rows = [row for block in rows for row in jnp.split(block, 8, axis=0)]
    for k in range(2):
        for j in range(9):
            stencil_ref[k, j : j + 1, :] = rows[9 * k + j]
        shift_ref[k : k + 1, :] = rows[18 + k]


def shape_of(*dims, dtype=BF16):
    return jax.ShapeDtypeStruct(dims, dtype)


def call(body, outs, scratch=(), smem_first=False, count=0):
    vmem = pl.BlockSpec(memory_space=pltpu.VMEM)
    specs = [vmem] * count
    if smem_first:
        specs[0] = pl.BlockSpec(memory_space=pltpu.SMEM)
    many = isinstance(outs, (list, tuple))
    return pl.pallas_call(
        body,
        out_shape=outs,
        in_specs=specs,
        out_specs=[vmem] * len(outs) if many else vmem,
        scratch_shapes=list(scratch),
        compiler_params=pltpu.CompilerParams(vmem_limit_bytes=VMEM_LIMIT),
    )


def exchange(array):
    return lax.all_to_all(array, TILE, split_axis=0, concat_axis=0, tiled=True)


def whole_block(states, cotangent, beside_slot, beside_code, mixers, stencils, shifts):
    groups = lax.axis_size(TILE)
    batch = lax.axis_size("batch")
    shape = states.shape
    x = states.reshape(T * CELLS, 256)
    cot = cotangent.reshape(T * CELLS, 256)
    comb = (beside_slot * 8 + beside_code).astype(I32).reshape(groups, 64)
    comb = jnp.pad(comb, ((0, 0), (0, 64)))
    sel = jnp.asarray(selection(), BF16)
    spread = jnp.asarray(spreading(), BF16)
    shift = jnp.asarray(shifting(), BF16)
    lines16 = shape_of(128, S, 256)
    rims16 = shape_of(64, S, 256)
    field = shape_of(T * CELLS, 256)
    wide = shape_of(T * CELLS, 256, dtype=F32)
    tab, out1, rims1, own1 = call(
        first_kernel,
        [shape_of(8, 128, dtype=I32), shape_of(64, 2 * S, 256), rims16, rims16],
        [pltpu.VMEM((128, S, 256), BF16), pltpu.SMEM((8, 128), I32), pltpu.SemaphoreType.DMA],
        count=4,
    )(comb, x, cot, sel)
    in1 = exchange(out1.reshape(groups, 4 * S, 256)).reshape(64, 2 * S, 256)
    conv1, back2, g2 = call(inner_kernel, [wide, wide, field], count=5)(
        x, cot, mixers, stencils, shift
    )
    line_scratch = [
        pltpu.VMEM((128, S, 256), BF16),
        pltpu.VMEM((T, 128, 256), BF16),
        pltpu.VMEM((T, 128, 256), BF16),
        pltpu.VMEM((32, S, 256), F32),
        pltpu.VMEM((16, 3, 256), F32),
    ]
    active, first, gh, gc, rims2, lines2, out2, own2, c_lines, g_lines = call(
        middle_kernel,
        [field, field, field, field, rims16, lines16, shape_of(64, 2 * S, 256), rims16, lines16, lines16],
        line_scratch,
        smem_first=True,
        count=11,
    )(tab, in1, rims1, own1, conv1, back2, mixers, stencils, shifts, sel, spread)
    in2 = exchange(out2.reshape(groups, 4 * S, 256)).reshape(64, 2 * S, 256)
    pack, conv2, back1 = call(
        weight_kernel,
        [shape_of(groups, 24, 256), wide, wide],
        [
            pltpu.VMEM((T * CELLS, 256), BF16),
            pltpu.VMEM((128, S, 256), BF16),
            pltpu.VMEM((16, 3, 256), F32),
            pltpu.VMEM((9, 8, 256), F32),
            pltpu.VMEM((9, 8, 256), F32),
            pltpu.VMEM((16, 3, 8, 256), F32),
            pltpu.VMEM((2, 8, 256), F32),
            pltpu.VMEM((128, S, 256), BF16),
        ],
        smem_first=True,
        count=16,
    )(
        tab, x, cot, active, first, gh, gc, g2, rims2, lines2, rims1, in1, c_lines, g_lines,
        stencils, shift,
    )
    parts = exchange(pack)
    outcome, state_grad = call(
        last_kernel,
        [field, field],
        line_scratch + [pltpu.VMEM((128, S, 256), BF16)],
        smem_first=True,
        count=12,
    )(tab, in2, rims2, own2, conv2, back1, x, cot, mixers, stencils, shifts, spread)
    part = call(sum_kernel, shape_of(24, 256, dtype=F32), count=1)(parts)
    step = 1
    while 2 * step < batch:
        part = part + lax.ppermute(part, "batch", [(i, i ^ step) for i in range(batch)])
        step *= 2
    other = lax.ppermute(part, "batch", [(i, i ^ step) for i in range(batch)])
    spread_out = call(spread_kernel, shape_of(groups, 24, 256), count=2)(part, other)
    whole = exchange(spread_out)
    scale = 1.0 / math.sqrt(T * CELLS * groups * batch)

    def unpack(*refs):
        unpack_kernel(scale, *refs)

    mixer_grads, stencil_grads, shift_grads = call(
        unpack,
        [shape_of(2, 256, 256, dtype=F32), shape_of(2, 9, 256, dtype=F32), shape_of(2, 256, dtype=F32)],
        count=1,
    )(whole)
    return (
        outcome.reshape(shape),
        state_grad.reshape(shape),
        mixer_grads,
        stencil_grads,
        shift_grads,
    )


def solution(mesh):
    torus = Mesh(
        mesh.devices.reshape(4, 4, 2, mesh.shape["batch"]), ("tile_0", "tile_1", "tile_2", "batch")
    )
    in_specs = (
        P("batch", TILE, None, None, None),
        P("batch", TILE, None, None, None),
        P(),
        P(),
        P(),
        P(),
        P(),
    )
    out_specs = (
        P("batch", TILE, None, None, None),
        P("batch", TILE, None, None, None),
        P(),
        P(),
        P(),
    )
    return jax.shard_map(
        whole_block, mesh=torus, in_specs=in_specs, out_specs=out_specs, check_vma=False
    )
```

```python
import math

import jax
import jax.numpy as jnp
import numpy as np
from jax import lax
from jax.experimental import pallas as pl
from jax.experimental.pallas import tpu as pltpu
from jax.sharding import Mesh
from jax.sharding import PartitionSpec as P


TILE = ("tile_0", "tile_1", "tile_2")
SQRT_HALF = 0.7071067811865476
INV_ROOT_TAU = 0.3989422804014327

F32 = jnp.float32
BF16 = jnp.bfloat16
I32 = jnp.int32

S = 16
T = 8
CELLS = S * S
SIDE_TAPS = {0: (0, 1, 2), 1: (2, 5, 8), 2: (6, 7, 8), 3: (0, 3, 6)}
CORNER_TAP = {4: 2, 5: 8, 6: 6, 7: 0}


def line_cell(d, i):
    if d == 0:
        return i
    if d == 1:
        return S * i + S - 1
    if d == 2:
        return S * (S - 1) + i
    if d == 3:
        return S * i
    if i != 0:
        return None
    return {4: S - 1, 5: CELLS - 1, 6: S * (S - 1), 7: 0}[d]


def selection():
    sel = np.zeros((256, CELLS), np.float32)
    for d in range(8):
        for f in range(2):
            for i in range(S):
                cell = line_cell(d, S - 1 - i if f else i)
                if cell is not None:
                    sel[(2 * d + f) * S + i, cell] = 1.0
    return sel


def spreading():
    out = np.zeros((CELLS, 128), np.float32)
    for d in range(4):
        for i in range(S):
            out[line_cell(d, i), d * S + i] = 1.0
            out[line_cell(d, i), 64 + d * S + i] = 1.0
    return out


def shifting():
    out = np.zeros((512, CELLS), np.float32)
    for i in range(S):
        for j in range(S):
            if j > 0:
                out[S * i + j, S * i + j - 1] = 1.0
            if j < S - 1:
                out[256 + S * i + j, S * i + j + 1] = 1.0
    return out


def dot(a, b):
    return jnp.dot(a, b, preferred_element_type=F32)


def dot_t(a, b):
    return lax.dot_general(a, b, (((1,), (1,)), ((), ())), preferred_element_type=F32)


def t_dot(a, b):
    return lax.dot_general(a, b, (((0,), (0,)), ((), ())), preferred_element_type=F32)


def iota(shape, axis):
    return lax.broadcasted_iota(I32, shape, axis)


def neighbours(x):
    place = iota(x.shape, 0)
    before = jnp.where(place == 0, 0.0, pltpu.roll(x, 1, 0))
    after = jnp.where(place == S - 1, 0.0, pltpu.roll(x, S - 1, 0))
    return before, after


def down(x):
    return jnp.concatenate([jnp.zeros((S, x.shape[1]), x.dtype), x[: CELLS - S]], axis=0)


def up(x):
    return jnp.concatenate([x[S:], jnp.zeros((S, x.shape[1]), x.dtype)], axis=0)


def conv_inner(left, centre, right, w):
    rows = [w[3 * a] * left + w[3 * a + 1] * centre + w[3 * a + 2] * right for a in range(3)]
    return rows[1] + down(rows[0]) + up(rows[2])


def back_inner(left, centre, right, w):
    rows = [w[3 * a] * right + w[3 * a + 1] * centre + w[3 * a + 2] * left for a in range(3)]
    return rows[1] + up(rows[0]) + down(rows[2])


def tap_rows(ref, layer):
    return [ref[k, layer : layer + 1, :] for k in range(9)]


def fill_tap_sets(taps_ref, stencil_ref, layer):
    w = tap_rows(stencil_ref, layer)
    zero = jnp.zeros_like(w[0])
    for d in range(8):
        if d < 4:
            three = [w[k] for k in SIDE_TAPS[d]]
        else:
            three = [zero, w[CORNER_TAP[d]], zero]
        for f in range(2):
            for m, row in enumerate(three[::-1] if f else three):
                taps_ref[2 * d + f, m : m + 1, :] = row


def tile_of(ref, t):
    return ref[pl.ds(pl.multiple_of(t * CELLS, CELLS), CELLS), :]


def put_tile(ref, t, value):
    ref[pl.ds(pl.multiple_of(t * CELLS, CELLS), CELLS), :] = value


def split_store(ref, t, first, value):
    high = value.astype(BF16)
    ref[t, pl.ds(first, value.shape[0]), :] = high
    ref[t, pl.ds(64 + first, value.shape[0]), :] = (value - high.astype(F32)).astype(BF16)


def forward_lines(split_ref, buf_ref, tab_ref, w):
    def one(t, carry):
        corner = {}
        for d in range(4, 8):
            row = buf_ref[tab_ref[0, t * 8 + d]][:8, :].astype(F32)[:1, :]
            corner[d] = w[CORNER_TAP[d]] * row
        for d in range(4):
            x = buf_ref[tab_ref[0, t * 8 + d]].astype(F32)
            before, after = neighbours(x)
            a, b, c = SIDE_TAPS[d]
            line = w[a] * before + w[b] * x + w[c] * after
            at = iota(line.shape, 0)
            if d == 0:
                line = line + jnp.where(at == 0, corner[7], 0.0)
                line = line + jnp.where(at == S - 1, corner[4], 0.0)
            if d == 2:
                line = line + jnp.where(at == 0, corner[6], 0.0)
                line = line + jnp.where(at == S - 1, corner[5], 0.0)
            split_store(split_ref, t, d * S, line)
        return carry

    lax.fori_loop(0, T, one, 0, unroll=2)


def rim_gradients(rim_ref, lines_ref, tab_ref, taps_ref, first, count):
    def one(i, carry):
        x = lines_ref[i].astype(F32)
        before, after = neighbours(x)
        u = taps_ref[tab_ref[3, first + i]]
        rim = tab_ref[2, first + i] >> 1
        rim_ref[rim] += u[0:1] * after + u[1:2] * x + u[2:3] * before
        return carry

    lax.fori_loop(0, count, one, 0, unroll=8)


def split_rims(split_ref, rim_ref):
    def split(t, carry):
        for e in range(4):
            split_store(split_ref, t, e * S, rim_ref[t * 4 + e])
        return carry

    lax.fori_loop(0, T, split, 0, unroll=2)


def live_lines(dst_ref, dst_first, src_ref, offset, tab_ref, tab_first):
    def one(i, carry):
        line = src_ref[i, offset : offset + S]
        live = tab_ref[4, tab_first + i] > 0
        dst_ref[dst_first + i] = jnp.where(live, line, jnp.zeros((S, 256), BF16))
        return carry

    lax.fori_loop(0, 64, one, 0, unroll=8)


def line_grads(g_ref, c_ref, mixers_ref):
    for b in range(4):
        part = c_ref[b * 16 : b * 16 + 16].reshape(256, 256)
        g_ref[b * 16 : b * 16 + 16] = dot_t(part, mixers_ref[1]).astype(BF16).reshape(16, S, 256)


def gather_out(leave, ports, out_ref, own_ref, rims_ref, lines_ref, tab_ref):
    def some(q, carry):
        for r in range(16):
            s = q * 16 + r
            out_ref[s, 0:S] = rims_ref[tab_ref[2, 64 + s]]
            out_ref[s, S : 2 * S] = lines_ref[tab_ref[1, s]]
            own_ref[s] = lines_ref[tab_ref[5, s]]
        leave(ports[0], q * 16, 16)
        leave(ports[1], q * 16, 16)
        return carry

    lax.fori_loop(0, 4, some, 0)


def banks(rims_ref, lines_ref, rim_field, line_field, sel_ref):
    def one(t, carry):
        rims = dot(sel_ref[0:128, :], tile_of(rim_field, t)).astype(BF16)
        rims_ref[pl.ds(t * 8, 8)] = rims.reshape(8, S, 256)
        lines = dot(sel_ref[...], tile_of(line_field, t)).astype(BF16)
        lines_ref[pl.ds(t * 16, 16)] = lines.reshape(16, S, 256)
        return carry

    lax.fori_loop(0, T, one, 0)


def own_position():
    a, b, c = (lax.axis_index(name) for name in TILE)
    return (a * lax.axis_size(TILE[1]) + b) * lax.axis_size(TILE[2]) + c


def first_kernel(
    arrive, leave, comb_ref, states_ref, cot_ref, sel_ref, tab_ref, out_ref, rims_ref, own_ref, lines_ref, smem, sem
):
    me = own_position()
    comb = comb_ref[...]
    lane = iota(comb.shape, 1)
    home = iota(comb.shape, 0)
    slot = comb >> 3
    wanted = (lane < 64) & ((slot >> 3) == me) & (home != me)
    wanted_f = wanted.astype(F32)
    before = (iota((128, 128), 0) < iota((128, 128), 1)).astype(F32).astype(BF16)
    place = dot(wanted_f.astype(BF16), before)
    code = comb & 7
    rim_code = (slot & 7) * 8 + code
    tap_set = (lane & 7) * 2 + (code & 1)
    packed = (rim_code * 16 + tap_set + 1024).astype(F32)
    asked = jnp.zeros((1, 128), F32)
    for k in range(2):
        value = jnp.sum(
            jnp.where(wanted & (place == k), packed, 0.0), axis=1, keepdims=True
        )
        at = (lane >= 64) & (((lane - 64) >> 1) == home) & ((lane & 1) == k)
        asked = asked + jnp.sum(jnp.where(at, value, 0.0), axis=0, keepdims=True)
    asked = asked.astype(I32)

    own = comb_ref[pl.ds(me, 1), :]
    sub2 = iota((128, 128), 0)
    lane2 = iota((128, 128), 1)
    own_wide = jnp.broadcast_to(own, (128, 128))
    own_col = jnp.sum(
        jnp.where(sub2 == lane2, own_wide, 0).astype(F32), axis=1, keepdims=True
    ).astype(I32)
    owner_col = own_col >> 6
    owner_row = own >> 6
    same = (owner_col == owner_row) & (sub2 < 64) & (lane2 < 64)
    place_col = jnp.sum((same & (lane2 < sub2)).astype(F32), axis=1, keepdims=True).astype(I32)
    place_row = jnp.sum((same & (sub2 < lane2)).astype(F32), axis=0, keepdims=True).astype(I32)
    lane1 = iota((1, 128), 1)
    sub1 = iota((128, 1), 0)
    remote_row = owner_row != me
    slot_col = jnp.where((owner_col != me) & (sub1 < 64), owner_col * 2 + place_col, -1)
    line_col = (sub1 * 2 + (own_col & 1)).astype(F32)
    sent = jnp.sum(jnp.where(slot_col == lane2, line_col, 0.0), axis=0, keepdims=True).astype(I32)
    own_rim = (own & 511)
    own_rim = ((own_rim >> 3) & 7) * 8 + (own_rim & 7)
    in_own = lane1 < 64
    panel = jnp.where(remote_row, 64 + owner_row * 2 + place_row, own_rim)
    tab_ref[...] = jnp.zeros_like(tab_ref)
    tab_ref[0:1, :] = jnp.where(in_own, panel, 0)
    tab_ref[1:2, :] = jnp.where(in_own, sent, 0)
    tab_ref[2:3, :] = jnp.where(in_own, own_rim, (asked & 1023) >> 4)
    tab_ref[3:4, :] = jnp.where(in_own, (lane1 & 7) * 2 + (own & 1), asked & 15)
    tab_ref[4:5, :] = jnp.where(in_own, (~remote_row).astype(I32), asked >> 10)
    tab_ref[5:6, :] = jnp.where(in_own, lane1 * 2 + (own & 1), 0)
    copy = pltpu.make_async_copy(tab_ref, smem, sem)
    copy.start()
    arrive(1)
    arrive(2)
    banks(rims_ref, lines_ref, states_ref, cot_ref, sel_ref)
    leave(2, 0, 64)
    copy.wait()
    gather_out(leave, (1, 3), out_ref, own_ref, rims_ref, lines_ref, smem)


def inner_kernel(
    arrive, leave, tab_ref, states_ref, cot_ref, own_in_ref, mixers_ref, stencils_ref, shift_ref,
    conv_ref, back_ref, g_ref, c_ref, gl_ref, rim_ref, taps_ref,
):
    w0 = tap_rows(stencils_ref, 0)
    w1 = tap_rows(stencils_ref, 1)
    arrive(1)
    arrive(2)

    def one(t, carry):
        x = tile_of(states_ref, t)
        moved = dot(shift_ref[...], x)
        put_tile(conv_ref, t, conv_inner(moved[:CELLS], x.astype(F32), moved[CELLS:], w0))
        leave(0, t * CELLS, CELLS)
        g = dot_t(tile_of(cot_ref, t), mixers_ref[1]).astype(BF16)
        put_tile(g_ref, t, g)
        leave(2, t * CELLS, CELLS)
        moved = dot(shift_ref[...], g)
        put_tile(back_ref, t, back_inner(moved[:CELLS], g.astype(F32), moved[CELLS:], w1))
        leave(1, t * CELLS, CELLS)
        return carry

    lax.fori_loop(0, T, one, 0)
    arrive(3)
    fill_tap_sets(taps_ref, stencils_ref, 1)
    live_lines(c_ref, 0, own_in_ref, 0, tab_ref, 0)
    leave(3, 0, 64)
    line_grads(gl_ref, c_ref, mixers_ref)
    leave(4, 0, 64)
    rim_ref[...] = jnp.zeros_like(rim_ref)
    rim_gradients(rim_ref, gl_ref, tab_ref, taps_ref, 0, 64)
    leave(5, 0, 32)


def middle_kernel(
    arrive, leave,
    tab_ref, in_ref, rims_in_ref, rim_ref, conv_ref, back_ref, mixers_ref, stencils_ref,
    shifts_ref, sel_ref, spread_ref,
    active_ref, first_ref, gh_ref, gc_ref, rims_ref, lines_ref, out_ref, own_ref, c_ref, g_ref,
    buf_ref, split_ref, split2_ref, taps_ref,
):
    w0 = tap_rows(stencils_ref, 0)
    fill_tap_sets(taps_ref, stencils_ref, 1)
    buf_ref[64:128] = in_ref[:, 0:S, :]
    live_lines(c_ref, 0, in_ref, S, tab_ref, 64)
    leave(8, 0, 64)
    line_grads(g_ref, c_ref, mixers_ref)
    leave(9, 0, 64)
    arrive(2)
    buf_ref[0:64] = rims_in_ref[...]
    forward_lines(split_ref, buf_ref, tab_ref, w0)
    arrive(3)
    rim_gradients(rim_ref, g_ref, tab_ref, taps_ref, 64, 64)
    split_rims(split2_ref, rim_ref)
    arrive(4)
    arrive(5)

    def one(t, carry):
        first = (tile_of(conv_ref, t) + dot(spread_ref[...], split_ref[t])).astype(BF16)
        put_tile(first_ref, t, first)
        leave(1, t * CELLS, CELLS)
        hidden = dot(first, mixers_ref[0]) + shifts_ref[0:1, :]
        cdf = 0.5 * (1.0 + lax.erf(hidden * SQRT_HALF))
        active = (hidden * cdf).astype(BF16)
        put_tile(active_ref, t, active)
        leave(0, t * CELLS, CELLS)
        slope = cdf + hidden * jnp.exp(-0.5 * hidden * hidden) * INV_ROOT_TAU
        grad = tile_of(back_ref, t) + dot(spread_ref[...], split2_ref[t])
        gh = (grad * slope).astype(BF16)
        put_tile(gh_ref, t, gh)
        leave(2, t * CELLS, CELLS)
        gc = dot_t(gh, mixers_ref[0]).astype(BF16)
        put_tile(gc_ref, t, gc)
        leave(3, t * CELLS, CELLS)
        return carry

    lax.fori_loop(0, T, one, 0, unroll=2)
    banks(rims_ref, lines_ref, active_ref, gc_ref, sel_ref)
    leave(4, 0, 64)
    leave(5, 0, 128)
    gather_out(leave, (6, 7), out_ref, own_ref, rims_ref, lines_ref, tab_ref)


def weight_kernel(
    arrive, leave,
    tab_ref, states_ref, cot_ref, active_ref, first_ref, gh_ref, gc_ref, g2_ref, rims_ref, lines_ref,
    rims_in_ref, in_ref, c_own_ref, g_own_ref, c_in_ref, g_in_ref, stencils_ref, shift_ref,
    pack_ref, conv_ref,
    second_ref, h_ref, taps_ref, acc1_ref, acc2_ref, accl_ref, sums_ref,
):
    w1 = tap_rows(stencils_ref, 1)
    acc1_ref[...] = jnp.zeros_like(acc1_ref)
    acc2_ref[...] = jnp.zeros_like(acc2_ref)
    accl_ref[...] = jnp.zeros_like(accl_ref)
    sums_ref[...] = jnp.zeros_like(sums_ref)
    fill_tap_sets(taps_ref, stencils_ref, 1)

    def folded(x):
        return jnp.sum(x.reshape(-1, 8, 256), axis=0)

    def taps_of(acc_ref, g, left, centre, right):
        for b, x in enumerate((left, centre, right)):
            acc_ref[b] += folded(g[S:] * x[: CELLS - S])
            acc_ref[3 + b] += folded(g * x)
            acc_ref[6 + b] += folded(g[: CELLS - S] * x[S:])

    def halves(x):
        return x[0:8] + x[8:16]

    def second_halo(source_ref):
        def one(i, carry):
            x = rims_ref[(tab_ref[2, i] >> 1) * 2].astype(F32)
            g = source_ref[i & 63].astype(F32)
            before, after = neighbours(x)
            kind = tab_ref[3, i]
            u = taps_ref[kind]
            h_ref[i] = (u[0:1] * before + u[1:2] * x + u[2:3] * after).astype(BF16)
            for m, y in enumerate((before, x, after)):
                accl_ref[kind, m] += halves(g * y)
            return carry

        return one

    arrive(8)
    arrive(13)
    lax.fori_loop(0, 64, second_halo(g_own_ref), 0, unroll=8)
    arrive(15)
    lax.fori_loop(64, 128, second_halo(g_in_ref), 0, unroll=8)

    for k in (9, 10, 11):
        arrive(k)

    def first_halo(t, carry):
        for d in range(8):
            place = tab_ref[0, t * 8 + d]
            own = rims_in_ref[jnp.minimum(place, 63)]
            sent = in_ref[jnp.maximum(place - 64, 0), 0:S]
            x = jnp.where(place < 64, own, sent).astype(F32)
            g = lines_ref[(t * 8 + d) * 2].astype(F32)
            if d < 4:
                before, after = neighbours(x)
                for k, y in zip(SIDE_TAPS[d], (before, x, after)):
                    acc1_ref[k] += halves(g * y)
            else:
                acc1_ref[CORNER_TAP[d]] += halves(g * x)
        return carry

    lax.fori_loop(0, T, first_halo, 0, unroll=2)

    for k in (6, 1, 3, 7, 5, 2):
        arrive(k)

    def one(t, carry):
        gcf = tile_of(gc_ref, t).astype(F32)
        x = tile_of(states_ref, t)
        moved = dot(shift_ref[...], x)
        taps_of(acc1_ref, gcf, moved[:CELLS], x.astype(F32), moved[CELLS:])
        x = tile_of(active_ref, t)
        moved = dot(shift_ref[...], x)
        xf = x.astype(F32)
        second = conv_inner(moved[:CELLS], xf, moved[CELLS:], w1)
        put_tile(conv_ref, t, second)
        leave(1, t * CELLS, CELLS)
        put_tile(second_ref, t, second.astype(BF16))
        taps_of(acc2_ref, tile_of(g2_ref, t).astype(F32), moved[:CELLS], xf, moved[CELLS:])
        sums_ref[0] += folded(tile_of(gh_ref, t).astype(F32))
        sums_ref[1] += folded(tile_of(cot_ref, t).astype(F32))
        return carry

    lax.fori_loop(0, T, one, 0)
    for k in (4, 12, 14):
        arrive(k)
    for d in range(8):
        for f in range(2):
            if d < 4:
                taps = SIDE_TAPS[d][::-1] if f else SIDE_TAPS[d]
                for m, k in enumerate(taps):
                    acc2_ref[k] += accl_ref[2 * d + f, m]
            else:
                acc2_ref[CORNER_TAP[d]] += accl_ref[2 * d + f, 1]

    rows = [jnp.sum(acc1_ref[k], axis=0, keepdims=True) for k in range(9)]
    rows += [jnp.sum(acc2_ref[k], axis=0, keepdims=True) for k in range(9)]
    rows += [jnp.sum(sums_ref[k], axis=0, keepdims=True) for k in range(2)]
    rows += [jnp.zeros_like(rows[0])] * 4
    for r in range(3):
        pack_ref[r, 16:24] = jnp.concatenate(rows[8 * r : 8 * r + 8], axis=0).astype(BF16)
    for r in range(3, pack_ref.shape[0]):
        pack_ref[r, 16:24] = jnp.zeros((8, 256), BF16)
    half = pack_ref.shape[0] // 2
    mixer_first = t_dot(first_ref[...], gh_ref[...])
    for r in range(half):
        pack_ref[r, 0:16] = mixer_first[16 * r : 16 * r + 16].astype(BF16)
    leave(0, 0, half)
    mixer_second = (
        t_dot(second_ref[...], cot_ref[...])
        + t_dot(h_ref[0:64].reshape(1024, 256), c_own_ref[...].reshape(1024, 256))
        + t_dot(h_ref[64:128].reshape(1024, 256), c_in_ref[...].reshape(1024, 256))
    )
    for r in range(half):
        pack_ref[half + r, 0:16] = mixer_second[16 * r : 16 * r + 16].astype(BF16)
    leave(0, half, half)


def back_kernel(arrive, leave, gc_ref, stencils_ref, shift_ref, back_ref):
    w0 = tap_rows(stencils_ref, 0)
    arrive(0)

    def one(t, carry):
        gc = tile_of(gc_ref, t)
        moved = dot(shift_ref[...], gc)
        put_tile(back_ref, t, back_inner(moved[:CELLS], gc.astype(F32), moved[CELLS:], w0))
        leave(0, t * CELLS, CELLS)
        return carry

    lax.fori_loop(0, T, one, 0, unroll=2)


def outcome_kernel(
    arrive, leave,
    tab_ref, in_ref, rims_in_ref, conv_ref, states_ref, mixers_ref, stencils_ref, shifts_ref, spread_ref,
    outcome_ref,
    buf_ref, split_ref,
):
    w1 = tap_rows(stencils_ref, 1)
    arrive(2)
    buf_ref[0:64] = rims_in_ref[...]
    arrive(1)
    buf_ref[64:128] = in_ref[:, 0:S, :]
    forward_lines(split_ref, buf_ref, tab_ref, w1)
    arrive(3)
    arrive(4)

    def one(t, carry):
        second = (tile_of(conv_ref, t) + dot(spread_ref[...], split_ref[t])).astype(BF16)
        out = tile_of(states_ref, t).astype(F32) + dot(second, mixers_ref[1]) + shifts_ref[1:2, :]
        put_tile(outcome_ref, t, out.astype(BF16))
        leave(0, t * CELLS, CELLS)
        return carry

    lax.fori_loop(0, T, one, 0, unroll=2)


def grad_kernel(
    arrive, leave,
    tab_ref, in_ref, own_in_ref, back_ref, cot_ref, stencils_ref, spread_ref,
    grad_ref,
    lines_ref, split_ref, rim_ref, taps_ref,
):
    fill_tap_sets(taps_ref, stencils_ref, 0)
    rim_ref[...] = jnp.zeros_like(rim_ref)
    arrive(2)
    live_lines(lines_ref, 0, own_in_ref, 0, tab_ref, 0)
    arrive(1)
    live_lines(lines_ref, 64, in_ref, S, tab_ref, 64)
    rim_gradients(rim_ref, lines_ref, tab_ref, taps_ref, 0, 128)
    split_rims(split_ref, rim_ref)
    arrive(3)
    arrive(4)

    def one(t, carry):
        grad = tile_of(back_ref, t) + dot(spread_ref[...], split_ref[t])
        put_tile(grad_ref, t, (tile_of(cot_ref, t).astype(F32) + grad).astype(BF16))
        leave(0, t * CELLS, CELLS)
        return carry

    lax.fori_loop(0, T, one, 0, unroll=2)


def sum_kernel(arrive, leave, in_ref, out_ref):
    total = in_ref[0].astype(F32)
    for r in range(1, in_ref.shape[0]):
        total = total + in_ref[r].astype(F32)
    for r in range(out_ref.shape[0]):
        out_ref[r] = total.astype(BF16)


def spread_kernel(arrive, leave, in_ref, out_ref):
    total = in_ref[0].astype(F32)
    for r in range(1, in_ref.shape[0]):
        total = total + in_ref[r].astype(F32)
    value = total.astype(BF16)
    for r in range(out_ref.shape[0]):
        out_ref[r] = value


def unpack_kernel(scale, arrive, leave, in_ref, mixer_ref, stencil_ref, shift_ref):
    half = in_ref.shape[0] // 2
    for k in range(2):
        for r in range(half):
            mixer_ref[k, 16 * r : 16 * r + 16, :] = in_ref[k * half + r, 0:16].astype(F32) * scale
        leave(0, k, 1)
    rows = [in_ref[r, 16:24].astype(F32) * scale for r in range(3)]
    rows = [row for block in rows for row in jnp.split(block, 8, axis=0)]
    for k in range(2):
        for j in range(9):
            stencil_ref[j, k : k + 1, :] = rows[9 * k + j]
        shift_ref[k : k + 1, :] = rows[18 + k]


def shape_of(*dims, dtype=BF16):
    return jax.ShapeDtypeStruct(dims, dtype)


def call(body, ins, in_modes, outs, out_modes, scratch=(), limit=60.0, order=None):
    spaces = {"s": pltpu.SMEM, "v": pltpu.VMEM, "h": pltpu.HBM}
    ports_in = order or [k for k, mode in enumerate(in_modes) if mode == "h"]
    ports_out = [k for k, mode in enumerate(out_modes) if mode == "h"]
    n_in, n_out, n_own = len(ins), len(outs), len(scratch)

    def kernel(*refs):
        in_refs = list(refs[:n_in])
        out_refs = list(refs[n_in : n_in + n_out])
        rest = list(refs[n_in + n_out :])
        own, rest = rest[:n_own], rest[n_own:]
        sem_in, sem_out = rest[-2:]
        inward, outward = {}, {}
        for q, k in enumerate(ports_in):
            inward[k] = pltpu.make_async_copy(in_refs[k], rest[q], sem_in.at[q])
            inward[k].start()
            in_refs[k] = rest[q]
        for q, k in enumerate(ports_out):
            buffer = rest[len(ports_in) + q]
            outward[k] = (buffer, out_refs[k], sem_out.at[q])
            out_refs[k] = buffer

        def arrive(k):
            if k in inward:
                inward[k].wait()

        def leave(k, first, count):
            if k in outward:
                source, target, sem = outward[k]
                part = pl.ds(first, count)
                pltpu.make_async_copy(source.at[part], target.at[part], sem).start()

        body(arrive, leave, *in_refs, *out_refs, *own)
        for source, target, sem in outward.values():
            pltpu.make_async_copy(source, target, sem).wait()

    buffers = [pltpu.VMEM(ins[k].shape, ins[k].dtype) for k in ports_in]
    buffers += [pltpu.VMEM(outs[k].shape, outs[k].dtype) for k in ports_out]
    sems = [pltpu.SemaphoreType.DMA((max(1, len(p)),)) for p in (ports_in, ports_out)]
    return pl.pallas_call(
        kernel,
        out_shape=[
            pltpu.HBM(o.shape, o.dtype) if m == "h" else o for o, m in zip(outs, out_modes)
        ],
        in_specs=[pl.BlockSpec(memory_space=spaces[m]) for m in in_modes],
        out_specs=[pl.BlockSpec(memory_space=spaces[m]) for m in out_modes],
        scratch_shapes=list(scratch) + buffers + sems,
        compiler_params=pltpu.CompilerParams(vmem_limit_bytes=int(limit * 1024 * 1024)),
    )(*ins)


def exchange(array):
    return lax.all_to_all(array, TILE, split_axis=0, concat_axis=0, tiled=True)


def whole_block(states, cotangent, beside_slot, beside_code, mixers, stencils, shifts):
    groups = lax.axis_size(TILE)
    batch = lax.axis_size("batch")
    shape = states.shape
    x = states.reshape(T * CELLS, 256)
    cot = cotangent.reshape(T * CELLS, 256)
    comb = (beside_slot * 8 + beside_code).astype(I32).reshape(groups, 64)
    comb = jnp.pad(comb, ((0, 0), (0, 64)))
    sel = jnp.asarray(selection(), BF16)
    spread = jnp.asarray(spreading(), BF16)
    shift = jnp.asarray(shifting(), BF16)
    taps = stencils.swapaxes(0, 1)
    lines16 = shape_of(128, S, 256)
    rims16 = shape_of(64, S, 256)
    sent16 = shape_of(64, 2 * S, 256)
    field = shape_of(T * CELLS, 256)
    wide = shape_of(T * CELLS, 256, dtype=F32)
    lines_scratch = pltpu.VMEM((128, S, 256), BF16)
    split_scratch = pltpu.VMEM((T, 128, 256), BF16)
    rim_scratch = pltpu.VMEM((32, S, 256), F32)
    taps_scratch = pltpu.VMEM((16, 3, 256), F32)
    tab, out1, rims1, own1 = call(
        first_kernel,
        (comb, x, cot, sel),
        "vhhv",
        [shape_of(8, 128, dtype=I32), sent16, rims16, rims16],
        "vhhh",
        [lines_scratch, pltpu.SMEM((8, 128), I32), pltpu.SemaphoreType.DMA],
    )
    in1 = exchange(out1.reshape(groups, 4 * S, 256)).reshape(64, 2 * S, 256)
    conv1, back2, g2, c_own, g_own, rim_own = call(
        inner_kernel,
        (tab, x, cot, own1, mixers, taps, shift),
        "shhhvvv",
        [wide, wide, field, rims16, rims16, shape_of(32, S, 256, dtype=F32)],
        "hhhhhh",
        [taps_scratch],
    )
    active, first, gh, gc, rims2, lines2, out2, own2, c_in, g_in = call(
        middle_kernel,
        (tab, in1, rims1, rim_own, conv1, back2, mixers, taps, shifts, sel, spread),
        "svhhhhvvvvv",
        [field, field, field, field, rims16, lines16, sent16, rims16, rims16, rims16],
        "hhhhhhhhhh",
        [lines_scratch, split_scratch, split_scratch, taps_scratch],
        limit=59.5,
    )
    in2 = exchange(out2.reshape(groups, 4 * S, 256)).reshape(64, 2 * S, 256)
    pack, conv2 = call(
        weight_kernel,
        (tab, x, cot, active, first, gh, gc, g2, rims2, lines2, rims1, in1, c_own, g_own, c_in, g_in,
         taps, shift),
        "shhhhhhhhhhhhhhhvv",
        [shape_of(groups, 24, 256), wide],
        "hh",
        [
            pltpu.VMEM((T * CELLS, 256), BF16),
            lines_scratch,
            taps_scratch,
            pltpu.VMEM((9, 8, 256), F32),
            pltpu.VMEM((9, 8, 256), F32),
            pltpu.VMEM((16, 3, 8, 256), F32),
            pltpu.VMEM((2, 8, 256), F32),
        ],
        order=(8, 13, 15, 9, 10, 11, 6, 1, 3, 7, 5, 2, 4, 12, 14),
    )
    (back1,) = call(back_kernel, (gc, taps, shift), "hvv", [wide], "h")
    parts = exchange(pack)
    (outcome,) = call(
        outcome_kernel,
        (tab, in2, rims2, conv2, x, mixers, taps, shifts, spread),
        "shhhhvvvv",
        [field],
        "h",
        [lines_scratch, split_scratch],
    )
    (part,) = call(sum_kernel, (parts,), "v", [shape_of(batch, 24, 256)], "v", limit=4)
    part = lax.all_to_all(part, "batch", split_axis=0, concat_axis=0, tiled=True)
    (spread_out,) = call(spread_kernel, (part,), "v", [shape_of(groups, 24, 256)], "v", limit=4)
    whole = exchange(spread_out)
    (state_grad,) = call(
        grad_kernel,
        (tab, in2, own2, back1, cot, taps, spread),
        "shhhhvv",
        [field],
        "h",
        [lines_scratch, split_scratch, rim_scratch, taps_scratch],
    )
    scale = 1.0 / math.sqrt(T * CELLS * groups * batch)

    def unpack(*refs):
        unpack_kernel(scale, *refs)

    mixer_grads, stencil_grads, shift_grads = call(
        unpack,
        (whole,),
        "v",
        [shape_of(2, 256, 256, dtype=F32), shape_of(9, 2, 256, dtype=F32), shape_of(2, 256, dtype=F32)],
        "hvv",
        limit=4,
    )
    stencil_grads = stencil_grads.swapaxes(0, 1)
    return (
        outcome.reshape(shape),
        state_grad.reshape(shape),
        mixer_grads,
        stencil_grads,
        shift_grads,
    )


def solution(mesh):
    torus = Mesh(
        mesh.devices.reshape(4, 4, 2, mesh.shape["batch"]), ("tile_0", "tile_1", "tile_2", "batch")
    )
    in_specs = (
        P("batch", TILE, None, None, None),
        P("batch", TILE, None, None, None),
        P(),
        P(),
        P(),
        P(),
        P(),
    )
    out_specs = (
        P("batch", TILE, None, None, None),
        P("batch", TILE, None, None, None),
        P(),
        P(),
        P(),
    )
    return jax.shard_map(
        whole_block, mesh=torus, in_specs=in_specs, out_specs=out_specs, check_vma=False
    )
```

```python
import math

import jax
import jax.numpy as jnp
import numpy as np
from jax import lax
from jax.experimental import pallas as pl
from jax.experimental.pallas import tpu as pltpu
from jax.sharding import Mesh
from jax.sharding import PartitionSpec as P


TILE = ("tile_0", "tile_1", "tile_2")
SQRT_HALF = 0.7071067811865476
INV_ROOT_TAU = 0.3989422804014327

F32 = jnp.float32
BF16 = jnp.bfloat16
I32 = jnp.int32

S = 16
T = 8
CELLS = S * S
SIDE_TAPS = {0: (0, 1, 2), 1: (2, 5, 8), 2: (6, 7, 8), 3: (0, 3, 6)}
CORNER_TAP = {4: 2, 5: 8, 6: 6, 7: 0}


def line_cell(d, i):
    if d == 0:
        return i
    if d == 1:
        return S * i + S - 1
    if d == 2:
        return S * (S - 1) + i
    if d == 3:
        return S * i
    if i != 0:
        return None
    return {4: S - 1, 5: CELLS - 1, 6: S * (S - 1), 7: 0}[d]


def selection():
    sel = np.zeros((256, CELLS), np.float32)
    for d in range(8):
        for f in range(2):
            for i in range(S):
                cell = line_cell(d, S - 1 - i if f else i)
                if cell is not None:
                    sel[(2 * d + f) * S + i, cell] = 1.0
    return sel


def spreading():
    out = np.zeros((CELLS, 128), np.float32)
    for d in range(4):
        for i in range(S):
            out[line_cell(d, i), d * S + i] = 1.0
            out[line_cell(d, i), 64 + d * S + i] = 1.0
    return out


def shifting():
    out = np.zeros((512, CELLS), np.float32)
    for i in range(S):
        for j in range(S):
            if j > 0:
                out[S * i + j, S * i + j - 1] = 1.0
            if j < S - 1:
                out[256 + S * i + j, S * i + j + 1] = 1.0
    return out


def dot(a, b):
    return jnp.dot(a, b, preferred_element_type=F32)


def dot_t(a, b):
    return lax.dot_general(a, b, (((1,), (1,)), ((), ())), preferred_element_type=F32)


def t_dot(a, b):
    return lax.dot_general(a, b, (((0,), (0,)), ((), ())), preferred_element_type=F32)


def iota(shape, axis):
    return lax.broadcasted_iota(I32, shape, axis)


def neighbours(x):
    place = iota(x.shape, 0)
    before = jnp.where(place == 0, 0.0, pltpu.roll(x, 1, 0))
    after = jnp.where(place == S - 1, 0.0, pltpu.roll(x, S - 1, 0))
    return before, after


def down(x):
    return jnp.concatenate([jnp.zeros((S, x.shape[1]), x.dtype), x[: CELLS - S]], axis=0)


def up(x):
    return jnp.concatenate([x[S:], jnp.zeros((S, x.shape[1]), x.dtype)], axis=0)


def conv_inner(left, centre, right, w):
    rows = [w[3 * a] * left + w[3 * a + 1] * centre + w[3 * a + 2] * right for a in range(3)]
    return rows[1] + down(rows[0]) + up(rows[2])


def back_inner(left, centre, right, w):
    rows = [w[3 * a] * right + w[3 * a + 1] * centre + w[3 * a + 2] * left for a in range(3)]
    return rows[1] + up(rows[0]) + down(rows[2])


def tap_rows(ref, layer):
    return [ref[k, layer : layer + 1, :] for k in range(9)]


def fill_tap_sets(taps_ref, stencil_ref, layer):
    w = tap_rows(stencil_ref, layer)
    zero = jnp.zeros_like(w[0])
    for d in range(8):
        if d < 4:
            three = [w[k] for k in SIDE_TAPS[d]]
        else:
            three = [zero, w[CORNER_TAP[d]], zero]
        for f in range(2):
            for m, row in enumerate(three[::-1] if f else three):
                taps_ref[2 * d + f, m : m + 1, :] = row


def tile_of(ref, t):
    return ref[pl.ds(pl.multiple_of(t * CELLS, CELLS), CELLS), :]


def put_tile(ref, t, value):
    ref[pl.ds(pl.multiple_of(t * CELLS, CELLS), CELLS), :] = value


def split_store(ref, t, first, value):
    high = value.astype(BF16)
    ref[t, pl.ds(first, value.shape[0]), :] = high
    ref[t, pl.ds(64 + first, value.shape[0]), :] = (value - high.astype(F32)).astype(BF16)


def forward_lines(split_ref, buf_ref, tab_ref, w, panels_ref=None):
    def one(t, carry):
        corner = {}
        for d in range(4, 8):
            panel = buf_ref[tab_ref[0, t * 8 + d]]
            if panels_ref is not None:
                panels_ref[t * 8 + d] = panel
            row = panel[:8, :].astype(F32)[:1, :]
            corner[d] = w[CORNER_TAP[d]] * row
        for d in range(4):
            panel = buf_ref[tab_ref[0, t * 8 + d]]
            if panels_ref is not None:
                panels_ref[t * 8 + d] = panel
            x = panel.astype(F32)
            before, after = neighbours(x)
            a, b, c = SIDE_TAPS[d]
            line = w[a] * before + w[b] * x + w[c] * after
            at = iota(line.shape, 0)
            if d == 0:
                line = line + jnp.where(at == 0, corner[7], 0.0)
                line = line + jnp.where(at == S - 1, corner[4], 0.0)
            if d == 2:
                line = line + jnp.where(at == 0, corner[6], 0.0)
                line = line + jnp.where(at == S - 1, corner[5], 0.0)
            split_store(split_ref, t, d * S, line)
        return carry

    lax.fori_loop(0, T, one, 0, unroll=2)


def rim_rows_at(base, rim):
    return pl.ds(pl.multiple_of(base + rim * S, S), S)


def rim_gradients(rim_ref, base, lines_ref, tab_ref, taps_ref, first, count):
    def one(i, carry):
        x = lines_ref[i].astype(F32)
        before, after = neighbours(x)
        u = taps_ref[tab_ref[3, first + i]]
        rim = tab_ref[2, first + i] >> 1
        rim_ref[rim_rows_at(base, rim)] += u[0:1] * after + u[1:2] * x + u[2:3] * before
        return carry

    lax.fori_loop(0, count, one, 0, unroll=8)


def split_rims(split_ref, rim_ref, base):
    def split(t, carry):
        for e in range(4):
            split_store(split_ref, t, e * S, rim_ref[rim_rows_at(base, t * 4 + e)])
        return carry

    lax.fori_loop(0, T, split, 0, unroll=2)


def live_lines(dst_ref, dst_first, src_ref, offset, tab_ref, tab_first):
    def one(i, carry):
        line = src_ref[i, offset : offset + S]
        live = tab_ref[4, tab_first + i] > 0
        dst_ref[dst_first + i] = jnp.where(live, line, jnp.zeros((S, 256), BF16))
        return carry

    lax.fori_loop(0, 64, one, 0, unroll=8)


def line_grads(g_ref, c_ref, mixers_ref):
    for b in range(4):
        part = c_ref[b * 16 : b * 16 + 16].reshape(256, 256)
        g_ref[b * 16 : b * 16 + 16] = dot_t(part, mixers_ref[1]).astype(BF16).reshape(16, S, 256)


def gather_out(leave, ports, out_ref, own_ref, rims_ref, lines_ref, tab_ref):
    def some(q, carry):
        for r in range(16):
            s = q * 16 + r
            out_ref[s, 0:S] = rims_ref[tab_ref[2, 64 + s]]
            out_ref[s, S : 2 * S] = lines_ref[tab_ref[1, s]]
            own_ref[s] = lines_ref[tab_ref[5, s]]
        leave(ports[0], q * 16, 16)
        leave(ports[1], q * 16, 16)
        return carry

    lax.fori_loop(0, 4, some, 0)


def banks(rims_ref, lines_ref, t, rim_tile, line_tile, sel_ref):
    rims = dot(sel_ref[0:128, :], rim_tile).astype(BF16)
    rims_ref[pl.ds(t * 8, 8)] = rims.reshape(8, S, 256)
    lines = dot(sel_ref[...], line_tile).astype(BF16)
    lines_ref[pl.ds(t * 16, 16)] = lines.reshape(16, S, 256)


def own_position():
    a, b, c = (lax.axis_index(name) for name in TILE)
    return (a * lax.axis_size(TILE[1]) + b) * lax.axis_size(TILE[2]) + c


def first_kernel(
    arrive, leave, slot_ref, code_ref, states_ref, cot_ref, sel_ref, tab_ref, out_ref, rims_ref, own_ref,
    lines_ref, comb_ref, smem, sem,
):
    me = own_position()
    entries = slot_ref.shape[1]
    groups = entries // T
    sub = iota((128, entries), 0)
    tile = iota((128, entries), 1)
    belongs = (tile & (T - 1)) == (sub >> 3)
    member = (iota((groups, entries), 0) == (iota((groups, entries), 1) >> 3)).astype(F32).astype(BF16)

    def by_block(ref):
        copies = jnp.concatenate([ref[...].astype(F32)] * 16, axis=0)
        return dot_t(member, jnp.where(belongs, copies, 0.0).astype(BF16)).astype(I32)

    comb = by_block(slot_ref) * 8 + by_block(code_ref)
    comb_ref[...] = comb
    lane = iota(comb.shape, 1)
    home = iota(comb.shape, 0)
    slot = comb >> 3
    wanted = (lane < 64) & ((slot >> 3) == me) & (home != me)
    wanted_f = wanted.astype(F32)
    before = (iota((128, 128), 0) < iota((128, 128), 1)).astype(F32).astype(BF16)
    place = dot(wanted_f.astype(BF16), before)
    code = comb & 7
    rim_code = (slot & 7) * 8 + code
    tap_set = (lane & 7) * 2 + (code & 1)
    packed = (rim_code * 16 + tap_set + 1024).astype(F32)
    asked = jnp.zeros((1, 128), F32)
    for k in range(2):
        value = jnp.sum(
            jnp.where(wanted & (place == k), packed, 0.0), axis=1, keepdims=True
        )
        at = (lane >= 64) & (((lane - 64) >> 1) == home) & ((lane & 1) == k)
        asked = asked + jnp.sum(jnp.where(at, value, 0.0), axis=0, keepdims=True)
    asked = asked.astype(I32)

    own = comb_ref[pl.ds(me, 1), :]
    sub2 = iota((128, 128), 0)
    lane2 = iota((128, 128), 1)
    own_wide = jnp.broadcast_to(own, (128, 128))
    own_col = jnp.sum(
        jnp.where(sub2 == lane2, own_wide, 0).astype(F32), axis=1, keepdims=True
    ).astype(I32)
    owner_col = own_col >> 6
    owner_row = own >> 6
    same = (owner_col == owner_row) & (sub2 < 64) & (lane2 < 64)
    place_col = jnp.sum((same & (lane2 < sub2)).astype(F32), axis=1, keepdims=True).astype(I32)
    place_row = jnp.sum((same & (sub2 < lane2)).astype(F32), axis=0, keepdims=True).astype(I32)
    lane1 = iota((1, 128), 1)
    sub1 = iota((128, 1), 0)
    remote_row = owner_row != me
    slot_col = jnp.where((owner_col != me) & (sub1 < 64), owner_col * 2 + place_col, -1)
    line_col = (sub1 * 2 + (own_col & 1)).astype(F32)
    sent = jnp.sum(jnp.where(slot_col == lane2, line_col, 0.0), axis=0, keepdims=True).astype(I32)
    own_rim = (own & 511)
    own_rim = ((own_rim >> 3) & 7) * 8 + (own_rim & 7)
    in_own = lane1 < 64
    panel = jnp.where(remote_row, 64 + owner_row * 2 + place_row, own_rim)
    tab_ref[...] = jnp.zeros_like(tab_ref)
    tab_ref[0:1, :] = jnp.where(in_own, panel, 0)
    tab_ref[1:2, :] = jnp.where(in_own, sent, 0)
    tab_ref[2:3, :] = jnp.where(in_own, own_rim, (asked & 1023) >> 4)
    tab_ref[3:4, :] = jnp.where(in_own, (lane1 & 7) * 2 + (own & 1), asked & 15)
    tab_ref[4:5, :] = jnp.where(in_own, (~remote_row).astype(I32), asked >> 10)
    tab_ref[5:6, :] = jnp.where(in_own, lane1 * 2 + (own & 1), 0)
    copy = pltpu.make_async_copy(tab_ref, smem, sem)
    copy.start()
    arrive(2)
    arrive(3)

    def lines_of(t, carry):
        banks(rims_ref, lines_ref, t, tile_of(states_ref, t), tile_of(cot_ref, t), sel_ref)
        return carry

    lax.fori_loop(0, T, lines_of, 0, unroll=4)
    leave(2, 0, 64)
    copy.wait()
    gather_out(leave, (1, 3), out_ref, own_ref, rims_ref, lines_ref, smem)


def inner_kernel(
    arrive, leave, tab_ref, states_ref, cot_ref, own_in_ref, mixers_ref, stencils_ref, shift_ref,
    conv_ref, back_ref, g_ref, c_ref, gl_ref, taps_ref,
):
    w0 = tap_rows(stencils_ref, 0)
    w1 = tap_rows(stencils_ref, 1)
    arrive(1)
    arrive(2)

    def one(t, carry):
        x = tile_of(states_ref, t)
        moved = dot(shift_ref[...], x)
        put_tile(conv_ref, t, conv_inner(moved[:CELLS], x.astype(F32), moved[CELLS:], w0))
        leave(0, t * CELLS, CELLS)
        g = dot_t(tile_of(cot_ref, t), mixers_ref[1]).astype(BF16)
        put_tile(g_ref, t, g)
        leave(2, t * CELLS, CELLS)
        moved = dot(shift_ref[...], g)
        put_tile(back_ref, t, back_inner(moved[:CELLS], g.astype(F32), moved[CELLS:], w1))
        leave(1, t * CELLS, CELLS)
        return carry

    lax.fori_loop(0, T, one, 0)
    arrive(3)
    fill_tap_sets(taps_ref, stencils_ref, 1)
    live_lines(c_ref, 0, own_in_ref, 0, tab_ref, 0)
    leave(3, 0, 64)
    line_grads(gl_ref, c_ref, mixers_ref)
    leave(4, 0, 64)
    back_ref[T * CELLS :] = jnp.zeros((2 * CELLS, 256), F32)
    rim_gradients(back_ref, T * CELLS, gl_ref, tab_ref, taps_ref, 0, 64)
    leave(1, T * CELLS, 2 * CELLS)


def middle_kernel(
    arrive, leave,
    tab_ref, in_ref, rims_in_ref, back_ref, conv_ref, mixers_ref, stencils_ref,
    shifts_ref, sel_ref, spread_ref,
    active_ref, first_ref, gh_ref, gc_ref, rims_ref, lines_ref, out_ref, own_ref, c_ref, g_ref, panels_ref,
    buf_ref, split_ref, split2_ref, taps_ref,
):
    w0 = tap_rows(stencils_ref, 0)
    fill_tap_sets(taps_ref, stencils_ref, 1)
    buf_ref[64:128] = in_ref[:, 0:S, :]
    live_lines(c_ref, 0, in_ref, S, tab_ref, 64)
    leave(8, 0, 64)
    line_grads(g_ref, c_ref, mixers_ref)
    leave(9, 0, 64)
    arrive(2)
    buf_ref[0:64] = rims_in_ref[...]
    forward_lines(split_ref, buf_ref, tab_ref, w0, panels_ref)
    leave(10, 0, 64)
    arrive(3)
    rim_gradients(back_ref, T * CELLS, g_ref, tab_ref, taps_ref, 64, 64)
    split_rims(split2_ref, back_ref, T * CELLS)
    arrive(4)

    def one(t, carry):
        first = (tile_of(conv_ref, t) + dot(spread_ref[...], split_ref[t])).astype(BF16)
        put_tile(first_ref, t, first)
        leave(1, t * CELLS, CELLS)
        hidden = dot(first, mixers_ref[0]) + shifts_ref[0:1, :]
        cdf = 0.5 * (1.0 + lax.erf(hidden * SQRT_HALF))
        active = (hidden * cdf).astype(BF16)
        put_tile(active_ref, t, active)
        leave(0, t * CELLS, CELLS)
        slope = cdf + hidden * jnp.exp(-0.5 * hidden * hidden) * INV_ROOT_TAU
        grad = tile_of(back_ref, t) + dot(spread_ref[...], split2_ref[t])
        gh = (grad * slope).astype(BF16)
        put_tile(gh_ref, t, gh)
        leave(2, t * CELLS, CELLS)
        gc = dot_t(gh, mixers_ref[0]).astype(BF16)
        put_tile(gc_ref, t, gc)
        leave(3, t * CELLS, CELLS)
        banks(rims_ref, lines_ref, t, active, gc, sel_ref)
        return carry

    lax.fori_loop(0, T, one, 0, unroll=2)
    leave(4, 0, 64)
    leave(5, 0, 128)
    gather_out(leave, (6, 7), out_ref, own_ref, rims_ref, lines_ref, tab_ref)


def weight_kernel(
    arrive, leave,
    tab_ref, states_ref, cot_ref, active_ref, first_ref, gh_ref, gc_ref, g2_ref, rims_ref, lines_ref,
    panels_ref, c_own_ref, g_own_ref, c_in_ref, g_in_ref, stencils_ref, shift_ref,
    pack_ref, conv_ref,
    second_ref, h_ref, taps_ref, acc1_ref, acc2_ref, accl_ref, sums_ref,
):
    w1 = tap_rows(stencils_ref, 1)
    acc1_ref[...] = jnp.zeros_like(acc1_ref)
    acc2_ref[...] = jnp.zeros_like(acc2_ref)
    accl_ref[...] = jnp.zeros_like(accl_ref)
    sums_ref[...] = jnp.zeros_like(sums_ref)
    fill_tap_sets(taps_ref, stencils_ref, 1)

    def folded(x):
        return jnp.sum(x.reshape(-1, 8, 256), axis=0)

    def taps_of(acc_ref, g, left, centre, right):
        for b, x in enumerate((left, centre, right)):
            acc_ref[b] += folded(g[S:] * x[: CELLS - S])
            acc_ref[3 + b] += folded(g * x)
            acc_ref[6 + b] += folded(g[: CELLS - S] * x[S:])

    def halves(x):
        return x[0:8] + x[8:16]

    def second_halo(source_ref):
        def one(i, carry):
            x = rims_ref[(tab_ref[2, i] >> 1) * 2].astype(F32)
            g = source_ref[i & 63].astype(F32)
            before, after = neighbours(x)
            kind = tab_ref[3, i]
            u = taps_ref[kind]
            h_ref[i] = (u[0:1] * before + u[1:2] * x + u[2:3] * after).astype(BF16)
            for m, y in enumerate((before, x, after)):
                accl_ref[kind, m] += halves(g * y)
            return carry

        return one

    arrive(8)
    arrive(12)
    lax.fori_loop(0, 64, second_halo(g_own_ref), 0, unroll=8)
    arrive(14)
    lax.fori_loop(64, 128, second_halo(g_in_ref), 0, unroll=8)

    for k in (9, 10):
        arrive(k)

    def first_halo(t, carry):
        for d in range(8):
            x = panels_ref[t * 8 + d].astype(F32)
            g = lines_ref[(t * 8 + d) * 2].astype(F32)
            if d < 4:
                before, after = neighbours(x)
                for k, y in zip(SIDE_TAPS[d], (before, x, after)):
                    acc1_ref[k] += halves(g * y)
            else:
                acc1_ref[CORNER_TAP[d]] += halves(g * x)
        return carry

    lax.fori_loop(0, T, first_halo, 0, unroll=2)

    for k in (6, 1, 3, 7, 5, 2):
        arrive(k)

    def one(t, carry):
        gcf = tile_of(gc_ref, t).astype(F32)
        x = tile_of(states_ref, t)
        moved = dot(shift_ref[...], x)
        taps_of(acc1_ref, gcf, moved[:CELLS], x.astype(F32), moved[CELLS:])
        x = tile_of(active_ref, t)
        moved = dot(shift_ref[...], x)
        xf = x.astype(F32)
        second = conv_inner(moved[:CELLS], xf, moved[CELLS:], w1)
        put_tile(conv_ref, t, second)
        leave(1, t * CELLS, CELLS)
        put_tile(second_ref, t, second.astype(BF16))
        taps_of(acc2_ref, tile_of(g2_ref, t).astype(F32), moved[:CELLS], xf, moved[CELLS:])
        sums_ref[0] += folded(tile_of(gh_ref, t).astype(F32))
        sums_ref[1] += folded(tile_of(cot_ref, t).astype(F32))
        return carry

    lax.fori_loop(0, T, one, 0)
    for k in (4, 11, 13):
        arrive(k)
    for d in range(8):
        for f in range(2):
            if d < 4:
                taps = SIDE_TAPS[d][::-1] if f else SIDE_TAPS[d]
                for m, k in enumerate(taps):
                    acc2_ref[k] += accl_ref[2 * d + f, m]
            else:
                acc2_ref[CORNER_TAP[d]] += accl_ref[2 * d + f, 1]

    rows = [jnp.sum(acc1_ref[k], axis=0, keepdims=True) for k in range(9)]
    rows += [jnp.sum(acc2_ref[k], axis=0, keepdims=True) for k in range(9)]
    rows += [jnp.sum(sums_ref[k], axis=0, keepdims=True) for k in range(2)]
    rows = [row[:, 128 * h : 128 * h + 128] for row in rows for h in range(2)]
    for r in range(5):
        pack_ref[r, 32:40] = jnp.concatenate(rows[8 * r : 8 * r + 8], axis=0).astype(BF16)
    for r in range(5, pack_ref.shape[0]):
        pack_ref[r, 32:40] = jnp.zeros((8, 128), BF16)
    half = pack_ref.shape[0] // 2

    def put_rows(r, rows16):
        for q in range(4):
            at = (q // 2) * 8, (q % 2) * 128
            pack_ref[r, 8 * q : 8 * q + 8] = rows16[at[0] : at[0] + 8, at[1] : at[1] + 128].astype(BF16)

    mixer_first = t_dot(first_ref[...], gh_ref[...])
    for r in range(half):
        put_rows(r, mixer_first[16 * r : 16 * r + 16])
    leave(0, 0, half)
    mixer_second = (
        t_dot(second_ref[...], cot_ref[...])
        + t_dot(h_ref[0:64].reshape(1024, 256), c_own_ref[...].reshape(1024, 256))
        + t_dot(h_ref[64:128].reshape(1024, 256), c_in_ref[...].reshape(1024, 256))
    )
    for r in range(half):
        put_rows(half + r, mixer_second[16 * r : 16 * r + 16])
    leave(0, half, half)


def back_kernel(arrive, leave, gc_ref, stencils_ref, shift_ref, back_ref):
    w0 = tap_rows(stencils_ref, 0)
    arrive(0)

    def one(t, carry):
        gc = tile_of(gc_ref, t)
        moved = dot(shift_ref[...], gc)
        put_tile(back_ref, t, back_inner(moved[:CELLS], gc.astype(F32), moved[CELLS:], w0))
        leave(0, t * CELLS, CELLS)
        return carry

    lax.fori_loop(0, T, one, 0)


def outcome_kernel(
    arrive, leave,
    tab_ref, in_ref, rims_in_ref, conv_ref, states_ref, mixers_ref, stencils_ref, shifts_ref, spread_ref,
    outcome_ref,
    buf_ref, split_ref,
):
    w1 = tap_rows(stencils_ref, 1)
    arrive(2)
    buf_ref[0:64] = rims_in_ref[...]
    arrive(1)
    buf_ref[64:128] = in_ref[:, 0:S, :]
    forward_lines(split_ref, buf_ref, tab_ref, w1)
    arrive(3)
    arrive(4)

    def one(t, carry):
        second = (tile_of(conv_ref, t) + dot(spread_ref[...], split_ref[t])).astype(BF16)
        out = tile_of(states_ref, t).astype(F32) + dot(second, mixers_ref[1]) + shifts_ref[1:2, :]
        put_tile(outcome_ref, t, out.astype(BF16))
        leave(0, t * CELLS, CELLS)
        return carry

    lax.fori_loop(0, T, one, 0, unroll=2)


def grad_kernel(
    arrive, leave,
    tab_ref, in_ref, own_in_ref, back_ref, cot_ref, stencils_ref, spread_ref,
    grad_ref,
    lines_ref, split_ref, rim_ref, taps_ref,
):
    fill_tap_sets(taps_ref, stencils_ref, 0)
    rim_ref[...] = jnp.zeros_like(rim_ref)
    arrive(2)
    live_lines(lines_ref, 0, own_in_ref, 0, tab_ref, 0)
    arrive(1)
    live_lines(lines_ref, 64, in_ref, S, tab_ref, 64)
    rim_gradients(rim_ref, 0, lines_ref, tab_ref, taps_ref, 0, 128)
    split_rims(split_ref, rim_ref, 0)
    arrive(3)
    arrive(4)

    def one(t, carry):
        grad = tile_of(back_ref, t) + dot(spread_ref[...], split_ref[t])
        put_tile(grad_ref, t, (tile_of(cot_ref, t).astype(F32) + grad).astype(BF16))
        leave(0, t * CELLS, CELLS)
        return carry

    lax.fori_loop(0, T, one, 0, unroll=2)


def sum_kernel(arrive, leave, in_ref, out_ref):
    total = in_ref[0].astype(F32)
    for r in range(1, in_ref.shape[0]):
        total = total + in_ref[r].astype(F32)
    for r in range(out_ref.shape[0]):
        out_ref[r] = total.astype(BF16)


def spread_kernel(arrive, leave, in_ref, out_ref):
    total = in_ref[0].astype(F32)
    for r in range(1, in_ref.shape[0]):
        total = total + in_ref[r].astype(F32)
    value = total.astype(BF16)
    for r in range(out_ref.shape[0]):
        out_ref[r] = value


def unpack_kernel(scale, arrive, leave, in_ref, mixer_ref, stencil_ref, shift_ref):
    half = in_ref.shape[0] // 2
    for k in range(2):
        for r in range(half):
            for q in range(4):
                block = in_ref[k * half + r, 8 * q : 8 * q + 8].astype(F32) * scale
                row, col = 16 * r + (q // 2) * 8, (q % 2) * 128
                mixer_ref[k, row : row + 8, col : col + 128] = block
        leave(0, k, 1)
    rows = [in_ref[r, 32:40].astype(F32) * scale for r in range(5)]
    rows = [row for block in rows for row in jnp.split(block, 8, axis=0)]
    for k in range(2):
        for h in range(2):
            part = slice(128 * h, 128 * h + 128)
            for j in range(9):
                stencil_ref[j, k : k + 1, part] = rows[2 * (9 * k + j) + h]
            shift_ref[k : k + 1, part] = rows[2 * (18 + k) + h]


def shape_of(*dims, dtype=BF16):
    return jax.ShapeDtypeStruct(dims, dtype)


def call(body, ins, in_modes, outs, out_modes, scratch=(), limit=60.0, order=None):
    spaces = {"s": pltpu.SMEM, "v": pltpu.VMEM, "h": pltpu.HBM}
    ports_in = order or [k for k, mode in enumerate(in_modes) if mode == "h"]
    ports_out = [k for k, mode in enumerate(out_modes) if mode == "h"]
    n_in, n_out, n_own = len(ins), len(outs), len(scratch)

    def kernel(*refs):
        in_refs = list(refs[:n_in])
        out_refs = list(refs[n_in : n_in + n_out])
        rest = list(refs[n_in + n_out :])
        own, rest = rest[:n_own], rest[n_own:]
        sem_in, sem_out = rest[-2:]
        inward, outward = {}, {}
        for q, k in enumerate(ports_in):
            inward[k] = pltpu.make_async_copy(in_refs[k], rest[q], sem_in.at[q])
            inward[k].start()
            in_refs[k] = rest[q]
        for q, k in enumerate(ports_out):
            buffer = rest[len(ports_in) + q]
            outward[k] = (buffer, out_refs[k], sem_out.at[q])
            out_refs[k] = buffer

        def arrive(k):
            if k in inward:
                inward[k].wait()

        def leave(k, first, count):
            if k in outward:
                source, target, sem = outward[k]
                part = pl.ds(first, count)
                pltpu.make_async_copy(source.at[part], target.at[part], sem).start()

        body(arrive, leave, *in_refs, *out_refs, *own)
        for source, target, sem in outward.values():
            pltpu.make_async_copy(source, target, sem).wait()

    buffers = [pltpu.VMEM(ins[k].shape, ins[k].dtype) for k in ports_in]
    buffers += [pltpu.VMEM(outs[k].shape, outs[k].dtype) for k in ports_out]
    sems = [pltpu.SemaphoreType.DMA((max(1, len(p)),)) for p in (ports_in, ports_out)]
    return pl.pallas_call(
        kernel,
        out_shape=[
            pltpu.HBM(o.shape, o.dtype) if m == "h" else o for o, m in zip(outs, out_modes)
        ],
        in_specs=[pl.BlockSpec(memory_space=spaces[m]) for m in in_modes],
        out_specs=[pl.BlockSpec(memory_space=spaces[m]) for m in out_modes],
        scratch_shapes=list(scratch) + buffers + sems,
        compiler_params=pltpu.CompilerParams(vmem_limit_bytes=int(limit * 1024 * 1024)),
    )(*ins)


def exchange(array):
    return lax.all_to_all(array, TILE, split_axis=0, concat_axis=0, tiled=True)


def whole_block(states, cotangent, beside_slot, beside_code, mixers, stencils, shifts):
    groups = lax.axis_size(TILE)
    batch = lax.axis_size("batch")
    shape = states.shape
    x = states.reshape(T * CELLS, 256)
    cot = cotangent.reshape(T * CELLS, 256)
    sel = jnp.asarray(selection(), BF16)
    spread = jnp.asarray(spreading(), BF16)
    shift = jnp.asarray(shifting(), BF16)
    taps = stencils.swapaxes(0, 1)
    lines16 = shape_of(128, S, 256)
    rims16 = shape_of(64, S, 256)
    sent16 = shape_of(64, 2 * S, 256)
    field = shape_of(T * CELLS, 256)
    wide = shape_of(T * CELLS, 256, dtype=F32)
    lines_scratch = pltpu.VMEM((128, S, 256), BF16)
    split_scratch = pltpu.VMEM((T, 128, 256), BF16)
    rim_scratch = pltpu.VMEM((2 * CELLS, 256), F32)
    taps_scratch = pltpu.VMEM((16, 3, 256), F32)
    tab, out1, rims1, own1 = call(
        first_kernel,
        (beside_slot.astype(I32).T, beside_code.astype(I32).T, x, cot, sel),
        "vvhhv",
        [shape_of(8, 128, dtype=I32), sent16, rims16, rims16],
        "vhhh",
        [
            lines_scratch,
            pltpu.VMEM((groups, 128), I32),
            pltpu.SMEM((8, 128), I32),
            pltpu.SemaphoreType.DMA,
        ],
    )
    in1 = exchange(out1.reshape(groups, 4 * S, 256)).reshape(64, 2 * S, 256)
    conv1, back2, g2, c_own, g_own = call(
        inner_kernel,
        (tab, x, cot, own1, mixers, taps, shift),
        "shhhvvv",
        [wide, shape_of((T + 2) * CELLS, 256, dtype=F32), field, rims16, rims16],
        "hhhhh",
        [taps_scratch],
    )
    active, first, gh, gc, rims2, lines2, out2, own2, c_in, g_in, panels = call(
        middle_kernel,
        (tab, in1, rims1, back2, conv1, mixers, taps, shifts, sel, spread),
        "svhhhvvvvv",
        [field, field, field, field, rims16, lines16, sent16, rims16, rims16, rims16, rims16],
        "hhhhhhhhhhh",
        [lines_scratch, split_scratch, split_scratch, taps_scratch],
        limit=51.0,
    )
    in2 = exchange(out2.reshape(groups, 4 * S, 256)).reshape(64, 2 * S, 256)
    pack, conv2 = call(
        weight_kernel,
        (tab, x, cot, active, first, gh, gc, g2, rims2, lines2, panels, c_own, g_own, c_in, g_in,
         taps, shift),
        "shhhhhhhhhhhhhhvv",
        [shape_of(groups, 40, 128), wide],
        "hh",
        [
            pltpu.VMEM((T * CELLS, 256), BF16),
            lines_scratch,
            taps_scratch,
            pltpu.VMEM((9, 8, 256), F32),
            pltpu.VMEM((9, 8, 256), F32),
            pltpu.VMEM((16, 3, 8, 256), F32),
            pltpu.VMEM((2, 8, 256), F32),
        ],
        order=(8, 12, 14, 9, 10, 6, 1, 3, 7, 5, 2, 4, 11, 13),
    )
    (back1,) = call(back_kernel, (gc, taps, shift), "hvv", [wide], "h")
    parts = exchange(pack)
    (outcome,) = call(
        outcome_kernel,
        (tab, in2, rims2, conv2, x, mixers, taps, shifts, spread),
        "shhhhvvvv",
        [field],
        "h",
        [lines_scratch, split_scratch],
    )
    (part,) = call(sum_kernel, (parts,), "v", [shape_of(batch, 40, 128)], "v", limit=4)
    part = lax.all_to_all(part, "batch", split_axis=0, concat_axis=0, tiled=True)
    (spread_out,) = call(spread_kernel, (part,), "v", [shape_of(groups, 40, 128)], "v", limit=4)
    whole = exchange(spread_out)
    (state_grad,) = call(
        grad_kernel,
        (tab, in2, own2, back1, cot, taps, spread),
        "shhhhvv",
        [field],
        "h",
        [lines_scratch, split_scratch, rim_scratch, taps_scratch],
    )
    scale = 1.0 / math.sqrt(T * CELLS * groups * batch)

    def unpack(*refs):
        unpack_kernel(scale, *refs)

    mixer_grads, stencil_grads, shift_grads = call(
        unpack,
        (whole,),
        "v",
        [shape_of(2, 256, 256, dtype=F32), shape_of(9, 2, 256, dtype=F32), shape_of(2, 256, dtype=F32)],
        "hvv",
        limit=4,
    )
    stencil_grads = stencil_grads.swapaxes(0, 1)
    return (
        outcome.reshape(shape),
        state_grad.reshape(shape),
        mixer_grads,
        stencil_grads,
        shift_grads,
    )


def solution(mesh):
    torus = Mesh(
        mesh.devices.reshape(4, 4, 2, mesh.shape["batch"]), ("tile_0", "tile_1", "tile_2", "batch")
    )
    in_specs = (
        P("batch", TILE, None, None, None),
        P("batch", TILE, None, None, None),
        P(),
        P(),
        P(),
        P(),
        P(),
    )
    out_specs = (
        P("batch", TILE, None, None, None),
        P("batch", TILE, None, None, None),
        P(),
        P(),
        P(),
    )
    return jax.shard_map(
        whole_block, mesh=torus, in_specs=in_specs, out_specs=out_specs, check_vma=False
    )
```

```python
import math

import jax
import jax.numpy as jnp
import numpy as np
from jax import lax
from jax.experimental import pallas as pl
from jax.experimental.pallas import tpu as pltpu
from jax.sharding import Mesh
from jax.sharding import PartitionSpec as P


TILE = ("tile_0", "tile_1", "tile_2")
SQRT_HALF = 0.7071067811865476
INV_ROOT_TAU = 0.3989422804014327

F32 = jnp.float32
BF16 = jnp.bfloat16
I32 = jnp.int32

S = 16
T = 8
CELLS = S * S
SIDE_TAPS = {0: (0, 1, 2), 1: (2, 5, 8), 2: (6, 7, 8), 3: (0, 3, 6)}
CORNER_TAP = {4: 2, 5: 8, 6: 6, 7: 0}


def line_cell(d, i):
    if d == 0:
        return i
    if d == 1:
        return S * i + S - 1
    if d == 2:
        return S * (S - 1) + i
    if d == 3:
        return S * i
    if i != 0:
        return None
    return {4: S - 1, 5: CELLS - 1, 6: S * (S - 1), 7: 0}[d]


def selection():
    sel = np.zeros((256, CELLS), np.float32)
    for d in range(8):
        for f in range(2):
            for i in range(S):
                cell = line_cell(d, S - 1 - i if f else i)
                if cell is not None:
                    sel[(2 * d + f) * S + i, cell] = 1.0
    return sel


def spreading():
    out = np.zeros((CELLS, 128), np.float32)
    for d in range(4):
        for i in range(S):
            out[line_cell(d, i), d * S + i] = 1.0
            out[line_cell(d, i), 64 + d * S + i] = 1.0
    return out


def shifting():
    out = np.zeros((512, CELLS), np.float32)
    for i in range(S):
        for j in range(S):
            if j > 0:
                out[S * i + j, S * i + j - 1] = 1.0
            if j < S - 1:
                out[256 + S * i + j, S * i + j + 1] = 1.0
    return out


def line_matrices():
    sel = selection()
    lines = np.concatenate([sel[32 * d : 32 * d + S] for d in range(4)])
    bank = np.zeros((256, 64), np.float32)
    for row in range(256):
        cells = np.flatnonzero(sel[row])
        if cells.size:
            bank[row, np.flatnonzero(lines[:, cells[0]])[0]] = 1.0
    place = np.zeros((CELLS, 64), np.float32)
    for cell in range(CELLS):
        at = np.flatnonzero(lines[:, cell])
        if at.size:
            home = [q for q in at if (q // S) % 2 == 0] or list(at)
            place[cell, home[0]] = 1.0
    return bank, lines @ spreading(), place


def dot(a, b):
    return jnp.dot(a, b, preferred_element_type=F32)


def dot_t(a, b):
    return lax.dot_general(a, b, (((1,), (1,)), ((), ())), preferred_element_type=F32)


def t_dot(a, b):
    return lax.dot_general(a, b, (((0,), (0,)), ((), ())), preferred_element_type=F32)


def iota(shape, axis):
    return lax.broadcasted_iota(I32, shape, axis)


def neighbours(x):
    place = iota(x.shape, 0)
    before = jnp.where(place == 0, 0.0, pltpu.roll(x, 1, 0))
    after = jnp.where(place == S - 1, 0.0, pltpu.roll(x, S - 1, 0))
    return before, after


def down(x):
    return jnp.concatenate([jnp.zeros((S, x.shape[1]), x.dtype), x[: CELLS - S]], axis=0)


def up(x):
    return jnp.concatenate([x[S:], jnp.zeros((S, x.shape[1]), x.dtype)], axis=0)


def conv_inner(left, centre, right, w):
    rows = [w[3 * a] * left + w[3 * a + 1] * centre + w[3 * a + 2] * right for a in range(3)]
    return rows[1] + down(rows[0]) + up(rows[2])


def back_inner(left, centre, right, w):
    rows = [w[3 * a] * right + w[3 * a + 1] * centre + w[3 * a + 2] * left for a in range(3)]
    return rows[1] + up(rows[0]) + down(rows[2])


def tap_rows(ref, layer):
    return [ref[k, layer : layer + 1, :] for k in range(9)]


def fill_tap_sets(taps_ref, stencil_ref, layer):
    w = tap_rows(stencil_ref, layer)
    zero = jnp.zeros_like(w[0])
    for d in range(8):
        if d < 4:
            three = [w[k] for k in SIDE_TAPS[d]]
        else:
            three = [zero, w[CORNER_TAP[d]], zero]
        for f in range(2):
            for m, row in enumerate(three[::-1] if f else three):
                taps_ref[2 * d + f, m : m + 1, :] = row


def tile_of(ref, t):
    return ref[pl.ds(pl.multiple_of(t * CELLS, CELLS), CELLS), :]


def put_tile(ref, t, value):
    ref[pl.ds(pl.multiple_of(t * CELLS, CELLS), CELLS), :] = value


def split_store(ref, t, first, value):
    high = value.astype(BF16)
    ref[t, pl.ds(first, value.shape[0]), :] = high
    ref[t, pl.ds(64 + first, value.shape[0]), :] = (value - high.astype(F32)).astype(BF16)


def forward_lines(split_ref, buf_ref, tab_ref, w, panels_ref=None):
    def one(t, carry):
        corner = {}
        for d in range(4, 8):
            panel = buf_ref[tab_ref[0, t * 8 + d]]
            if panels_ref is not None:
                panels_ref[t * 8 + d] = panel
            row = panel[:8, :].astype(F32)[:1, :]
            corner[d] = w[CORNER_TAP[d]] * row
        for d in range(4):
            panel = buf_ref[tab_ref[0, t * 8 + d]]
            if panels_ref is not None:
                panels_ref[t * 8 + d] = panel
            x = panel.astype(F32)
            before, after = neighbours(x)
            a, b, c = SIDE_TAPS[d]
            line = w[a] * before + w[b] * x + w[c] * after
            at = iota(line.shape, 0)
            if d == 0:
                line = line + jnp.where(at == 0, corner[7], 0.0)
                line = line + jnp.where(at == S - 1, corner[4], 0.0)
            if d == 2:
                line = line + jnp.where(at == 0, corner[6], 0.0)
                line = line + jnp.where(at == S - 1, corner[5], 0.0)
            split_store(split_ref, t, d * S, line)
        return carry

    lax.fori_loop(0, T, one, 0, unroll=2)


def rim_rows_at(base, rim):
    return pl.ds(pl.multiple_of(base + rim * S, S), S)


def rim_gradients(rim_ref, base, lines_ref, tab_ref, taps_ref, first, count):
    def one(i, carry):
        x = lines_ref[i].astype(F32)
        before, after = neighbours(x)
        u = taps_ref[tab_ref[3, first + i]]
        rim = tab_ref[2, first + i] >> 1
        rim_ref[rim_rows_at(base, rim)] += u[0:1] * after + u[1:2] * x + u[2:3] * before
        return carry

    lax.fori_loop(0, count, one, 0, unroll=8)


def split_rims(split_ref, rim_ref, base):
    def split(t, carry):
        for e in range(4):
            split_store(split_ref, t, e * S, rim_ref[rim_rows_at(base, t * 4 + e)])
        return carry

    lax.fori_loop(0, T, split, 0, unroll=2)


def live_lines(dst_ref, dst_first, src_ref, offset, tab_ref, tab_first):
    def one(i, carry):
        line = src_ref[i, offset : offset + S]
        live = tab_ref[4, tab_first + i] > 0
        dst_ref[dst_first + i] = jnp.where(live, line, jnp.zeros((S, 256), BF16))
        return carry

    lax.fori_loop(0, 64, one, 0, unroll=8)


def line_grads(g_ref, c_ref, mixers_ref):
    for b in range(4):
        part = c_ref[b * 16 : b * 16 + 16].reshape(256, 256)
        g_ref[b * 16 : b * 16 + 16] = dot_t(part, mixers_ref[1]).astype(BF16).reshape(16, S, 256)


def gather_out(leave, ports, out_ref, own_ref, rims_ref, lines_ref, tab_ref):
    def some(q, carry):
        for r in range(16):
            s = q * 16 + r
            out_ref[s, 0:S] = rims_ref[tab_ref[2, 64 + s]]
            out_ref[s, S : 2 * S] = lines_ref[tab_ref[1, s]]
            own_ref[s] = lines_ref[tab_ref[5, s]]
        leave(ports[0], q * 16, 16)
        leave(ports[1], q * 16, 16)
        return carry

    lax.fori_loop(0, 4, some, 0)


def banks(rims_ref, lines_ref, t, rim_tile, line_tile, sel_ref):
    rims = dot(sel_ref[0:128, :], rim_tile).astype(BF16)
    rims_ref[pl.ds(t * 8, 8)] = rims.reshape(8, S, 256)
    lines = dot(sel_ref[...], line_tile).astype(BF16)
    lines_ref[pl.ds(t * 16, 16)] = lines.reshape(16, S, 256)


def own_position():
    a, b, c = (lax.axis_index(name) for name in TILE)
    return (a * lax.axis_size(TILE[1]) + b) * lax.axis_size(TILE[2]) + c


def first_kernel(
    arrive, leave, slot_ref, code_ref, states_ref, cot_ref, sel_ref, tab_ref, out_ref, rims_ref, own_ref,
    lines_ref, comb_ref, smem, sem,
):
    me = own_position()
    entries = slot_ref.shape[1]
    groups = entries // T
    sub = iota((128, entries), 0)
    tile = iota((128, entries), 1)
    belongs = (tile & (T - 1)) == (sub >> 3)
    member = (iota((groups, entries), 0) == (iota((groups, entries), 1) >> 3)).astype(F32).astype(BF16)

    def by_block(ref):
        copies = jnp.concatenate([ref[...].astype(F32)] * 16, axis=0)
        return dot_t(member, jnp.where(belongs, copies, 0.0).astype(BF16)).astype(I32)

    comb = by_block(slot_ref) * 8 + by_block(code_ref)
    comb_ref[...] = comb
    lane = iota(comb.shape, 1)
    home = iota(comb.shape, 0)
    slot = comb >> 3
    wanted = (lane < 64) & ((slot >> 3) == me) & (home != me)
    wanted_f = wanted.astype(F32)
    before = (iota((128, 128), 0) < iota((128, 128), 1)).astype(F32).astype(BF16)
    place = dot(wanted_f.astype(BF16), before)
    code = comb & 7
    rim_code = (slot & 7) * 8 + code
    tap_set = (lane & 7) * 2 + (code & 1)
    packed = (rim_code * 16 + tap_set + 1024).astype(F32)
    asked = jnp.zeros((1, 128), F32)
    for k in range(2):
        value = jnp.sum(
            jnp.where(wanted & (place == k), packed, 0.0), axis=1, keepdims=True
        )
        at = (lane >= 64) & (((lane - 64) >> 1) == home) & ((lane & 1) == k)
        asked = asked + jnp.sum(jnp.where(at, value, 0.0), axis=0, keepdims=True)
    asked = asked.astype(I32)

    own = comb_ref[pl.ds(me, 1), :]
    sub2 = iota((128, 128), 0)
    lane2 = iota((128, 128), 1)
    own_wide = jnp.broadcast_to(own, (128, 128))
    own_col = jnp.sum(
        jnp.where(sub2 == lane2, own_wide, 0).astype(F32), axis=1, keepdims=True
    ).astype(I32)
    owner_col = own_col >> 6
    owner_row = own >> 6
    same = (owner_col == owner_row) & (sub2 < 64) & (lane2 < 64)
    place_col = jnp.sum((same & (lane2 < sub2)).astype(F32), axis=1, keepdims=True).astype(I32)
    place_row = jnp.sum((same & (sub2 < lane2)).astype(F32), axis=0, keepdims=True).astype(I32)
    lane1 = iota((1, 128), 1)
    sub1 = iota((128, 1), 0)
    remote_row = owner_row != me
    slot_col = jnp.where((owner_col != me) & (sub1 < 64), owner_col * 2 + place_col, -1)
    line_col = (sub1 * 2 + (own_col & 1)).astype(F32)
    sent = jnp.sum(jnp.where(slot_col == lane2, line_col, 0.0), axis=0, keepdims=True).astype(I32)
    own_rim = (own & 511)
    own_rim = ((own_rim >> 3) & 7) * 8 + (own_rim & 7)
    in_own = lane1 < 64
    panel = jnp.where(remote_row, 64 + owner_row * 2 + place_row, own_rim)
    tab_ref[...] = jnp.zeros_like(tab_ref)
    tab_ref[0:1, :] = jnp.where(in_own, panel, 0)
    tab_ref[1:2, :] = jnp.where(in_own, sent, 0)
    tab_ref[2:3, :] = jnp.where(in_own, own_rim, (asked & 1023) >> 4)
    tab_ref[3:4, :] = jnp.where(in_own, (lane1 & 7) * 2 + (own & 1), asked & 15)
    tab_ref[4:5, :] = jnp.where(in_own, (~remote_row).astype(I32), asked >> 10)
    tab_ref[5:6, :] = jnp.where(in_own, lane1 * 2 + (own & 1), 0)
    copy = pltpu.make_async_copy(tab_ref, smem, sem)
    copy.start()
    arrive(2)
    arrive(3)

    def lines_of(t, carry):
        banks(rims_ref, lines_ref, t, tile_of(states_ref, t), tile_of(cot_ref, t), sel_ref)
        return carry

    lax.fori_loop(0, T, lines_of, 0, unroll=4)
    leave(2, 0, 64)
    copy.wait()
    gather_out(leave, (1, 3), out_ref, own_ref, rims_ref, lines_ref, smem)


def edge_cells():
    row = iota((CELLS, 1), 0)
    i, j = row >> 4, row & (S - 1)
    return (i == 0) | (i == S - 1) | (j == 0) | (j == S - 1)


def keep_lines(lines_ref, t, tile_ref):
    at = [pl.ds(0, S), pl.ds(S - 1, S, stride=S), pl.ds(S * (S - 1), S), pl.ds(0, S, stride=S)]
    for d in range(4):
        for h in range(2):
            lines_ref[pl.ds(pl.multiple_of(t * 64 + d * S, S), S), 128 * h : 128 * h + 128] = tile_ref[
                h, at[d], :
            ]


def put_halves(tile_ref, value):
    tile_ref[0] = value[:, 0:128]
    tile_ref[1] = value[:, 128:256]


def activation(hidden):
    cdf = 0.5 * (1.0 + lax.erf(hidden * SQRT_HALF))
    slope = cdf + hidden * jnp.exp(-0.5 * hidden * hidden) * INV_ROOT_TAU
    return (hidden * cdf).astype(BF16), slope


def inner_kernel(
    arrive, leave, tab_ref, states_ref, cot_ref, own_in_ref, mixers_ref, stencils_ref, shifts_ref, shift_ref,
    back_ref, g_ref, c_ref, gl_ref, active_ref, first_ref, gh_ref, gc_ref,
    taps_ref, tile1_ref, tile2_ref,
):
    w0 = tap_rows(stencils_ref, 0)
    w1 = tap_rows(stencils_ref, 1)
    arrive(1)
    arrive(2)
    edge = edge_cells()

    def one(t, carry):
        x = tile_of(states_ref, t)
        moved = dot(shift_ref[...], x)
        conv = conv_inner(moved[:CELLS], x.astype(F32), moved[CELLS:], w0)
        put_halves(tile1_ref, conv)
        keep_lines(back_ref, t + 2 * T, tile1_ref)
        first = conv.astype(BF16)
        put_tile(first_ref, t, first)
        leave(5, t * CELLS, CELLS)
        active, slope = activation(dot(first, mixers_ref[0]) + shifts_ref[0:1, :])
        put_tile(active_ref, t, jnp.where(edge, 0.0, active.astype(F32)).astype(BF16))
        leave(4, t * CELLS, CELLS)
        g = dot_t(tile_of(cot_ref, t), mixers_ref[1]).astype(BF16)
        put_tile(g_ref, t, g)
        leave(1, t * CELLS, CELLS)
        moved = dot(shift_ref[...], g)
        back = back_inner(moved[:CELLS], g.astype(F32), moved[CELLS:], w1)
        put_halves(tile2_ref, back)
        keep_lines(back_ref, t, tile2_ref)
        gh = jnp.where(edge, 0.0, back * slope).astype(BF16)
        put_tile(gh_ref, t, gh)
        leave(6, t * CELLS, CELLS)
        put_tile(gc_ref, t, dot_t(gh, mixers_ref[0]).astype(BF16))
        leave(7, t * CELLS, CELLS)
        return carry

    lax.fori_loop(0, T, one, 0)
    arrive(3)
    fill_tap_sets(taps_ref, stencils_ref, 1)
    live_lines(c_ref, 0, own_in_ref, 0, tab_ref, 0)
    leave(2, 0, 64)
    line_grads(gl_ref, c_ref, mixers_ref)
    leave(3, 0, 64)
    back_ref[2 * CELLS : 4 * CELLS] = jnp.zeros((2 * CELLS, 256), F32)
    rim_gradients(back_ref, 2 * CELLS, gl_ref, tab_ref, taps_ref, 0, 64)
    leave(0, 0, 6 * CELLS)


def middle_kernel(
    arrive, leave,
    tab_ref, in_ref, rims_in_ref, back_ref, mixers_ref, stencils_ref,
    shifts_ref, bank_ref, cross_ref,
    active_ref, first_ref, gh_ref, gc_ref, rims_ref, lines_ref, out_ref, own_ref, c_ref, g_ref, panels_ref,
    buf_ref, split_ref, split2_ref, taps_ref,
):
    w0 = tap_rows(stencils_ref, 0)
    fill_tap_sets(taps_ref, stencils_ref, 1)
    buf_ref[64:128] = in_ref[:, 0:S, :]
    live_lines(c_ref, 0, in_ref, S, tab_ref, 64)
    leave(8, 0, 64)
    line_grads(g_ref, c_ref, mixers_ref)
    leave(9, 0, 64)
    arrive(2)
    buf_ref[0:64] = rims_in_ref[...]
    forward_lines(split_ref, buf_ref, tab_ref, w0, panels_ref)
    leave(10, 0, 64)
    arrive(3)
    rim_gradients(back_ref, 2 * CELLS, g_ref, tab_ref, taps_ref, 64, 64)
    split_rims(split2_ref, back_ref, 2 * CELLS)
    at = iota((CELLS, 1), 0)
    twice = (((at >> 4) & 1) == 1) & (((at & (S - 1)) == 0) | ((at & (S - 1)) == S - 1))

    def updates(ref, u):
        return jnp.concatenate([dot(cross_ref[...], ref[4 * u + q]) for q in range(4)], axis=0)

    for u in range(2):
        part = slice(u * CELLS, (u + 1) * CELLS)
        conv = back_ref[(u + 4) * CELLS : (u + 5) * CELLS]
        first = (conv + updates(split_ref, u)).astype(BF16)
        first_ref[part] = first
        active, slope = activation(dot(first, mixers_ref[0]) + shifts_ref[0:1, :])
        active_ref[part] = active
        grad = (back_ref[part] + updates(split2_ref, u)) * slope
        gh_ref[part] = jnp.where(twice, 0.0, grad).astype(BF16)
        gc = dot_t(grad.astype(BF16), mixers_ref[0]).astype(BF16)
        gc_ref[part] = gc
        for q in range(4):
            t = 4 * u + q
            rows = slice(64 * q, 64 * q + 64)
            rims = dot(bank_ref[0:128, :], active[rows]).astype(BF16)
            rims_ref[8 * t : 8 * t + 8] = rims.reshape(8, S, 256)
            lines = dot(bank_ref[...], gc[rows]).astype(BF16)
            lines_ref[16 * t : 16 * t + 16] = lines.reshape(16, S, 256)
    for k in range(4):
        leave(k, 0, 2 * CELLS)
    leave(4, 0, 64)
    leave(5, 0, 128)
    gather_out(leave, (6, 7), out_ref, own_ref, rims_ref, lines_ref, tab_ref)


def weight_kernel(
    arrive, leave,
    tab_ref, states_ref, cot_ref, active_ref, first_ref, gh_ref, gc_ref, g2_ref, rims_ref, lines_ref,
    panels_ref, c_own_ref, g_own_ref, c_in_ref, g_in_ref,
    active_edge_ref, first_edge_ref, gh_edge_ref, gc_edge_ref, stencils_ref, shift_ref, place_ref,
    pack_ref, conv_ref, gc_out_ref,
    second_ref, h_ref, taps_ref, acc1_ref, acc2_ref, accl_ref, sums_ref,
):
    w1 = tap_rows(stencils_ref, 1)
    acc1_ref[...] = jnp.zeros_like(acc1_ref)
    acc2_ref[...] = jnp.zeros_like(acc2_ref)
    accl_ref[...] = jnp.zeros_like(accl_ref)
    sums_ref[...] = jnp.zeros_like(sums_ref)
    fill_tap_sets(taps_ref, stencils_ref, 1)

    def folded(x):
        return jnp.sum(x.reshape(-1, 8, 256), axis=0)

    def taps_of(acc_ref, g, left, centre, right):
        for b, x in enumerate((left, centre, right)):
            acc_ref[b] += folded(g[S:] * x[: CELLS - S])
            acc_ref[3 + b] += folded(g * x)
            acc_ref[6 + b] += folded(g[: CELLS - S] * x[S:])

    def halves(x):
        return x[0:8] + x[8:16]

    def second_halo(source_ref):
        def one(i, carry):
            x = rims_ref[(tab_ref[2, i] >> 1) * 2].astype(F32)
            g = source_ref[i & 63].astype(F32)
            before, after = neighbours(x)
            kind = tab_ref[3, i]
            u = taps_ref[kind]
            h_ref[i] = (u[0:1] * before + u[1:2] * x + u[2:3] * after).astype(BF16)
            for m, y in enumerate((before, x, after)):
                accl_ref[kind, m] += halves(g * y)
            return carry

        return one

    arrive(8)
    arrive(12)
    lax.fori_loop(0, 64, second_halo(g_own_ref), 0, unroll=8)
    arrive(14)
    lax.fori_loop(64, 128, second_halo(g_in_ref), 0, unroll=8)

    for k in (9, 10):
        arrive(k)

    def first_halo(t, carry):
        for d in range(8):
            x = panels_ref[t * 8 + d].astype(F32)
            g = lines_ref[(t * 8 + d) * 2].astype(F32)
            if d < 4:
                before, after = neighbours(x)
                for k, y in zip(SIDE_TAPS[d], (before, x, after)):
                    acc1_ref[k] += halves(g * y)
            else:
                acc1_ref[CORNER_TAP[d]] += halves(g * x)
        return carry

    lax.fori_loop(0, T, first_halo, 0, unroll=2)

    for k in (6, 18, 1, 3, 15, 7, 5, 17, 2):
        arrive(k)

    def whole(inner_ref, edge_ref, t):
        edges = edge_ref[pl.ds(pl.multiple_of(t * 64, 64), 64), :]
        return tile_of(inner_ref, t).astype(F32) + dot(place_ref[...], edges)

    sums_ref[0] += folded(gh_edge_ref[...].astype(F32))

    def one(t, carry):
        gcf = whole(gc_ref, gc_edge_ref, t)
        put_tile(gc_out_ref, t, gcf.astype(BF16))
        leave(2, t * CELLS, CELLS)
        x = tile_of(states_ref, t)
        moved = dot(shift_ref[...], x)
        taps_of(acc1_ref, gcf, moved[:CELLS], x.astype(F32), moved[CELLS:])
        xf = whole(active_ref, active_edge_ref, t)
        moved = dot(shift_ref[...], xf.astype(BF16))
        second = conv_inner(moved[:CELLS], xf, moved[CELLS:], w1)
        put_tile(conv_ref, t, second)
        leave(1, t * CELLS, CELLS)
        put_tile(second_ref, t, second.astype(BF16))
        taps_of(acc2_ref, tile_of(g2_ref, t).astype(F32), moved[:CELLS], xf, moved[CELLS:])
        sums_ref[0] += folded(tile_of(gh_ref, t).astype(F32))
        sums_ref[1] += folded(tile_of(cot_ref, t).astype(F32))
        return carry

    lax.fori_loop(0, T, one, 0)
    for k in (4, 16, 11, 13):
        arrive(k)
    for d in range(8):
        for f in range(2):
            if d < 4:
                taps = SIDE_TAPS[d][::-1] if f else SIDE_TAPS[d]
                for m, k in enumerate(taps):
                    acc2_ref[k] += accl_ref[2 * d + f, m]
            else:
                acc2_ref[CORNER_TAP[d]] += accl_ref[2 * d + f, 1]

    rows = [jnp.sum(acc1_ref[k], axis=0, keepdims=True) for k in range(9)]
    rows += [jnp.sum(acc2_ref[k], axis=0, keepdims=True) for k in range(9)]
    rows += [jnp.sum(sums_ref[k], axis=0, keepdims=True) for k in range(2)]
    rows = [row[:, 128 * h : 128 * h + 128] for row in rows for h in range(2)]
    for r in range(5):
        pack_ref[r, 32:40] = jnp.concatenate(rows[8 * r : 8 * r + 8], axis=0).astype(BF16)
    for r in range(5, pack_ref.shape[0]):
        pack_ref[r, 32:40] = jnp.zeros((8, 128), BF16)
    half = pack_ref.shape[0] // 2

    def put_rows(r, rows16):
        for q in range(4):
            at = (q // 2) * 8, (q % 2) * 128
            pack_ref[r, 8 * q : 8 * q + 8] = rows16[at[0] : at[0] + 8, at[1] : at[1] + 128].astype(BF16)

    mixer_first = t_dot(first_ref[...], gh_ref[...]) + t_dot(first_edge_ref[...], gh_edge_ref[...])
    for r in range(half):
        put_rows(r, mixer_first[16 * r : 16 * r + 16])
    leave(0, 0, half)
    mixer_second = (
        t_dot(second_ref[...], cot_ref[...])
        + t_dot(h_ref[0:64].reshape(1024, 256), c_own_ref[...].reshape(1024, 256))
        + t_dot(h_ref[64:128].reshape(1024, 256), c_in_ref[...].reshape(1024, 256))
    )
    for r in range(half):
        put_rows(half + r, mixer_second[16 * r : 16 * r + 16])
    leave(0, half, half)


def outcome_kernel(
    arrive, leave,
    tab_ref, in_ref, rims_in_ref, own_in_ref, conv_ref, states_ref, mixers_ref, stencils_ref, shifts_ref,
    spread_ref,
    outcome_ref, halo_ref,
    buf_ref, split_ref, rim_ref, taps_ref, lines_ref,
):
    w1 = tap_rows(stencils_ref, 1)
    arrive(2)
    buf_ref[0:64] = rims_in_ref[...]
    arrive(1)
    buf_ref[64:128] = in_ref[:, 0:S, :]
    forward_lines(split_ref, buf_ref, tab_ref, w1)
    arrive(4)
    arrive(5)

    def one(t, carry):
        second = (tile_of(conv_ref, t) + dot(spread_ref[...], split_ref[t])).astype(BF16)
        out = tile_of(states_ref, t).astype(F32) + dot(second, mixers_ref[1]) + shifts_ref[1:2, :]
        put_tile(outcome_ref, t, out.astype(BF16))
        leave(0, t * CELLS, CELLS)
        return carry

    lax.fori_loop(0, T, one, 0, unroll=2)
    fill_tap_sets(taps_ref, stencils_ref, 0)
    rim_ref[...] = jnp.zeros_like(rim_ref)
    arrive(3)
    live_lines(lines_ref, 0, own_in_ref, 0, tab_ref, 0)
    live_lines(lines_ref, 64, in_ref, S, tab_ref, 64)
    rim_gradients(rim_ref, 0, lines_ref, tab_ref, taps_ref, 0, 128)
    split_rims(halo_ref, rim_ref, 0)
    leave(1, 0, T)


def grad_kernel(
    arrive, leave,
    gc_ref, halo_ref, cot_ref, stencils_ref, shift_ref, spread_ref,
    grad_ref,
):
    w0 = tap_rows(stencils_ref, 0)
    for k in range(3):
        arrive(k)

    def one(t, carry):
        gc = tile_of(gc_ref, t)
        moved = dot(shift_ref[...], gc)
        grad = back_inner(moved[:CELLS], gc.astype(F32), moved[CELLS:], w0)
        grad = grad + dot(spread_ref[...], halo_ref[t]) + tile_of(cot_ref, t).astype(F32)
        put_tile(grad_ref, t, grad.astype(BF16))
        leave(0, t * CELLS, CELLS)
        return carry

    lax.fori_loop(0, T, one, 0)


def sum_kernel(arrive, leave, in_ref, out_ref):
    total = in_ref[0].astype(F32)
    for r in range(1, in_ref.shape[0]):
        total = total + in_ref[r].astype(F32)
    for r in range(out_ref.shape[0]):
        out_ref[r] = total.astype(BF16)


def spread_kernel(arrive, leave, in_ref, out_ref):
    total = in_ref[0].astype(F32)
    for r in range(1, in_ref.shape[0]):
        total = total + in_ref[r].astype(F32)
    value = total.astype(BF16)
    for r in range(out_ref.shape[0]):
        out_ref[r] = value


def unpack_kernel(scale, arrive, leave, in_ref, mixer_ref, stencil_ref, shift_ref):
    half = in_ref.shape[0] // 2
    for k in range(2):
        for r in range(half):
            for q in range(4):
                block = in_ref[k * half + r, 8 * q : 8 * q + 8].astype(F32) * scale
                row, col = 16 * r + (q // 2) * 8, (q % 2) * 128
                mixer_ref[k, row : row + 8, col : col + 128] = block
        leave(0, k, 1)
    rows = [in_ref[r, 32:40].astype(F32) * scale for r in range(5)]
    rows = [row for block in rows for row in jnp.split(block, 8, axis=0)]
    for k in range(2):
        for h in range(2):
            part = slice(128 * h, 128 * h + 128)
            for j in range(9):
                stencil_ref[j, k : k + 1, part] = rows[2 * (9 * k + j) + h]
            shift_ref[k : k + 1, part] = rows[2 * (18 + k) + h]


def shape_of(*dims, dtype=BF16):
    return jax.ShapeDtypeStruct(dims, dtype)


def call(body, ins, in_modes, outs, out_modes, scratch=(), limit=60.0, order=None):
    spaces = {"s": pltpu.SMEM, "v": pltpu.VMEM, "h": pltpu.HBM}
    ports_in = order or [k for k, mode in enumerate(in_modes) if mode == "h"]
    ports_out = [k for k, mode in enumerate(out_modes) if mode == "h"]
    n_in, n_out, n_own = len(ins), len(outs), len(scratch)

    def kernel(*refs):
        in_refs = list(refs[:n_in])
        out_refs = list(refs[n_in : n_in + n_out])
        rest = list(refs[n_in + n_out :])
        own, rest = rest[:n_own], rest[n_own:]
        sem_in, sem_out = rest[-2:]
        inward, outward = {}, {}
        for q, k in enumerate(ports_in):
            inward[k] = pltpu.make_async_copy(in_refs[k], rest[q], sem_in.at[q])
            inward[k].start()
            in_refs[k] = rest[q]
        for q, k in enumerate(ports_out):
            buffer = rest[len(ports_in) + q]
            outward[k] = (buffer, out_refs[k], sem_out.at[q])
            out_refs[k] = buffer

        def arrive(k):
            if k in inward:
                inward[k].wait()

        def leave(k, first, count):
            if k in outward:
                source, target, sem = outward[k]
                part = pl.ds(first, count)
                pltpu.make_async_copy(source.at[part], target.at[part], sem).start()

        body(arrive, leave, *in_refs, *out_refs, *own)
        for source, target, sem in outward.values():
            pltpu.make_async_copy(source, target, sem).wait()

    buffers = [pltpu.VMEM(ins[k].shape, ins[k].dtype) for k in ports_in]
    buffers += [pltpu.VMEM(outs[k].shape, outs[k].dtype) for k in ports_out]
    sems = [pltpu.SemaphoreType.DMA((max(1, len(p)),)) for p in (ports_in, ports_out)]
    return pl.pallas_call(
        kernel,
        out_shape=[
            pltpu.HBM(o.shape, o.dtype) if m == "h" else o for o, m in zip(outs, out_modes)
        ],
        in_specs=[pl.BlockSpec(memory_space=spaces[m]) for m in in_modes],
        out_specs=[pl.BlockSpec(memory_space=spaces[m]) for m in out_modes],
        scratch_shapes=list(scratch) + buffers + sems,
        compiler_params=pltpu.CompilerParams(vmem_limit_bytes=int(limit * 1024 * 1024)),
    )(*ins)


def exchange(array):
    return lax.all_to_all(array, TILE, split_axis=0, concat_axis=0, tiled=True)


def whole_block(states, cotangent, beside_slot, beside_code, mixers, stencils, shifts):
    groups = lax.axis_size(TILE)
    batch = lax.axis_size("batch")
    shape = states.shape
    x = states.reshape(T * CELLS, 256)
    cot = cotangent.reshape(T * CELLS, 256)
    sel = jnp.asarray(selection(), BF16)
    spread = jnp.asarray(spreading(), BF16)
    shift = jnp.asarray(shifting(), BF16)
    taps = stencils.swapaxes(0, 1)
    lines16 = shape_of(128, S, 256)
    rims16 = shape_of(64, S, 256)
    sent16 = shape_of(64, 2 * S, 256)
    field = shape_of(T * CELLS, 256)
    wide = shape_of(T * CELLS, 256, dtype=F32)
    lines_scratch = pltpu.VMEM((128, S, 256), BF16)
    split_scratch = pltpu.VMEM((T, 128, 256), BF16)
    rim_scratch = pltpu.VMEM((2 * CELLS, 256), F32)
    taps_scratch = pltpu.VMEM((16, 3, 256), F32)
    tab, out1, rims1, own1 = call(
        first_kernel,
        (beside_slot.astype(I32).T, beside_code.astype(I32).T, x, cot, sel),
        "vvhhv",
        [shape_of(8, 128, dtype=I32), sent16, rims16, rims16],
        "vhhh",
        [
            lines_scratch,
            pltpu.VMEM((groups, 128), I32),
            pltpu.SMEM((8, 128), I32),
            pltpu.SemaphoreType.DMA,
        ],
    )
    in1 = exchange(out1.reshape(groups, 4 * S, 256)).reshape(64, 2 * S, 256)
    bank, cross, place = (jnp.asarray(m, BF16) for m in line_matrices())
    edge = shape_of(2 * CELLS, 256)
    tile_scratch = pltpu.VMEM((2, CELLS, 128), F32)
    back2, g2, c_own, g_own, active, first, gh, gc = call(
        inner_kernel,
        (tab, x, cot, own1, mixers, taps, shifts, shift),
        "shhhvvvv",
        [
            shape_of(6 * CELLS, 256, dtype=F32),
            field,
            rims16,
            rims16,
            field,
            field,
            field,
            field,
        ],
        "hhhhhhhh",
        [taps_scratch, tile_scratch, tile_scratch],
    )
    active_e, first_e, gh_e, gc_e, rims2, lines2, out2, own2, c_in, g_in, panels = call(
        middle_kernel,
        (tab, in1, rims1, back2, mixers, taps, shifts, bank, cross),
        "svhhvvvvv",
        [edge, edge, edge, edge, rims16, lines16, sent16, rims16, rims16, rims16, rims16],
        "hhhhhhhhhhh",
        [lines_scratch, split_scratch, split_scratch, taps_scratch],
        limit=51.0,
    )
    in2 = exchange(out2.reshape(groups, 4 * S, 256)).reshape(64, 2 * S, 256)
    pack, conv2, gc_all = call(
        weight_kernel,
        (tab, x, cot, active, first, gh, gc, g2, rims2, lines2, panels, c_own, g_own, c_in, g_in,
         active_e, first_e, gh_e, gc_e, taps, shift, place),
        "shhhhhhhhhhhhhhhhhhvvv",
        [shape_of(groups, 40, 128), wide, field],
        "hhh",
        [
            pltpu.VMEM((T * CELLS, 256), BF16),
            lines_scratch,
            taps_scratch,
            pltpu.VMEM((9, 8, 256), F32),
            pltpu.VMEM((9, 8, 256), F32),
            pltpu.VMEM((16, 3, 8, 256), F32),
            pltpu.VMEM((2, 8, 256), F32),
        ],
        order=(8, 12, 14, 9, 10, 6, 18, 1, 3, 15, 7, 5, 17, 2, 4, 16, 11, 13),
    )
    parts = exchange(pack)
    outcome, halo = call(
        outcome_kernel,
        (tab, in2, rims2, own2, conv2, x, mixers, taps, shifts, spread),
        "shhhhhvvvv",
        [field, shape_of(T, 128, 256)],
        "hh",
        [lines_scratch, split_scratch, rim_scratch, taps_scratch, lines_scratch],
        order=(2, 1, 4, 5, 3),
    )
    (part,) = call(sum_kernel, (parts,), "v", [shape_of(batch, 40, 128)], "v", limit=4)
    part = lax.all_to_all(part, "batch", split_axis=0, concat_axis=0, tiled=True)
    (spread_out,) = call(spread_kernel, (part,), "v", [shape_of(groups, 40, 128)], "v", limit=4)
    whole = exchange(spread_out)
    (state_grad,) = call(
        grad_kernel, (gc_all, halo, cot, taps, shift, spread), "hhhvvv", [field], "h"
    )
    scale = 1.0 / math.sqrt(T * CELLS * groups * batch)

    def unpack(*refs):
        unpack_kernel(scale, *refs)

    mixer_grads, stencil_grads, shift_grads = call(
        unpack,
        (whole,),
        "v",
        [shape_of(2, 256, 256, dtype=F32), shape_of(9, 2, 256, dtype=F32), shape_of(2, 256, dtype=F32)],
        "hvv",
        limit=4,
    )
    stencil_grads = stencil_grads.swapaxes(0, 1)
    return (
        outcome.reshape(shape),
        state_grad.reshape(shape),
        mixer_grads,
        stencil_grads,
        shift_grads,
    )


def solution(mesh):
    torus = Mesh(
        mesh.devices.reshape(4, 4, 2, mesh.shape["batch"]), ("tile_0", "tile_1", "tile_2", "batch")
    )
    in_specs = (
        P("batch", TILE, None, None, None),
        P("batch", TILE, None, None, None),
        P(),
        P(),
        P(),
        P(),
        P(),
    )
    out_specs = (
        P("batch", TILE, None, None, None),
        P("batch", TILE, None, None, None),
        P(),
        P(),
        P(),
    )
    return jax.shard_map(
        whole_block, mesh=torus, in_specs=in_specs, out_specs=out_specs, check_vma=False
    )
```

```python
import math

import jax
import jax.numpy as jnp
import numpy as np
from jax import lax
from jax.experimental import pallas as pl
from jax.experimental.pallas import tpu as pltpu
from jax.sharding import Mesh
from jax.sharding import PartitionSpec as P


TILE = ("tile_0", "tile_1", "tile_2")
SQRT_HALF = 0.7071067811865476
INV_ROOT_TAU = 0.3989422804014327

F32 = jnp.float32
BF16 = jnp.bfloat16
I32 = jnp.int32

S = 16
T = 8
CELLS = S * S
SIDE_TAPS = {0: (0, 1, 2), 1: (2, 5, 8), 2: (6, 7, 8), 3: (0, 3, 6)}
CORNER_TAP = {4: 2, 5: 8, 6: 6, 7: 0}


def line_cell(d, i):
    if d == 0:
        return i
    if d == 1:
        return S * i + S - 1
    if d == 2:
        return S * (S - 1) + i
    if d == 3:
        return S * i
    if i != 0:
        return None
    return {4: S - 1, 5: CELLS - 1, 6: S * (S - 1), 7: 0}[d]


def selection():
    sel = np.zeros((256, CELLS), np.float32)
    for d in range(8):
        for f in range(2):
            for i in range(S):
                cell = line_cell(d, S - 1 - i if f else i)
                if cell is not None:
                    sel[(2 * d + f) * S + i, cell] = 1.0
    return sel


def spreading():
    out = np.zeros((CELLS, 128), np.float32)
    for d in range(4):
        for i in range(S):
            out[line_cell(d, i), d * S + i] = 1.0
            out[line_cell(d, i), 64 + d * S + i] = 1.0
    return out


def shifting():
    out = np.zeros((512, CELLS), np.float32)
    for i in range(S):
        for j in range(S):
            if j > 0:
                out[S * i + j, S * i + j - 1] = 1.0
            if j < S - 1:
                out[256 + S * i + j, S * i + j + 1] = 1.0
    return out


def line_matrices():
    sel = selection()
    lines = np.concatenate([sel[32 * d : 32 * d + S] for d in range(4)])
    turn = np.kron(np.eye(4), np.eye(S)[::-1]).astype(np.float32)
    place = np.zeros((CELLS, 64), np.float32)
    for cell in range(CELLS):
        at = np.flatnonzero(lines[:, cell])
        if at.size:
            home = [q for q in at if (q // S) % 2 == 0] or list(at)
            place[cell, home[0]] = 1.0
    return turn, lines @ spreading(), place


def dot(a, b):
    return jnp.dot(a, b, preferred_element_type=F32)


def dot_t(a, b):
    return lax.dot_general(a, b, (((1,), (1,)), ((), ())), preferred_element_type=F32)


def t_dot(a, b):
    return lax.dot_general(a, b, (((0,), (0,)), ((), ())), preferred_element_type=F32)


def iota(shape, axis):
    return lax.broadcasted_iota(I32, shape, axis)


def neighbours(x):
    place = iota(x.shape, 0)
    before = jnp.where(place == 0, 0.0, pltpu.roll(x, 1, 0))
    after = jnp.where(place == S - 1, 0.0, pltpu.roll(x, S - 1, 0))
    return before, after


def down(x):
    return jnp.concatenate([jnp.zeros((S, x.shape[1]), x.dtype), x[: CELLS - S]], axis=0)


def up(x):
    return jnp.concatenate([x[S:], jnp.zeros((S, x.shape[1]), x.dtype)], axis=0)


def conv_inner(left, centre, right, w):
    rows = [w[3 * a] * left + w[3 * a + 1] * centre + w[3 * a + 2] * right for a in range(3)]
    return rows[1] + down(rows[0]) + up(rows[2])


def back_inner(left, centre, right, w):
    rows = [w[3 * a] * right + w[3 * a + 1] * centre + w[3 * a + 2] * left for a in range(3)]
    return rows[1] + up(rows[0]) + down(rows[2])


def tap_rows(ref, layer):
    return [ref[k, layer : layer + 1, :] for k in range(9)]


def fill_tap_sets(taps_ref, stencil_ref, layer):
    w = tap_rows(stencil_ref, layer)
    zero = jnp.zeros_like(w[0])
    for d in range(8):
        if d < 4:
            three = [w[k] for k in SIDE_TAPS[d]]
        else:
            three = [zero, w[CORNER_TAP[d]], zero]
        for f in range(2):
            for m, row in enumerate(three[::-1] if f else three):
                taps_ref[2 * d + f, m : m + 1, :] = row


def tile_of(ref, t):
    return ref[pl.ds(pl.multiple_of(t * CELLS, CELLS), CELLS), :]


def put_tile(ref, t, value):
    ref[pl.ds(pl.multiple_of(t * CELLS, CELLS), CELLS), :] = value


def split_store(ref, t, first, value):
    high = value.astype(BF16)
    ref[t, pl.ds(first, value.shape[0]), :] = high
    ref[t, pl.ds(64 + first, value.shape[0]), :] = (value - high.astype(F32)).astype(BF16)


def forward_lines(split_ref, buf_ref, tab_ref, w, panels_ref=None):
    def one(t, carry):
        corner = {}
        for d in range(4, 8):
            panel = buf_ref[tab_ref[0, t * 8 + d]]
            if panels_ref is not None:
                panels_ref[t * 8 + d] = panel
            row = panel[:8, :].astype(F32)[:1, :]
            corner[d] = w[CORNER_TAP[d]] * row
        for d in range(4):
            panel = buf_ref[tab_ref[0, t * 8 + d]]
            if panels_ref is not None:
                panels_ref[t * 8 + d] = panel
            x = panel.astype(F32)
            before, after = neighbours(x)
            a, b, c = SIDE_TAPS[d]
            line = w[a] * before + w[b] * x + w[c] * after
            at = iota(line.shape, 0)
            if d == 0:
                line = line + jnp.where(at == 0, corner[7], 0.0)
                line = line + jnp.where(at == S - 1, corner[4], 0.0)
            if d == 2:
                line = line + jnp.where(at == 0, corner[6], 0.0)
                line = line + jnp.where(at == S - 1, corner[5], 0.0)
            split_store(split_ref, t, d * S, line)
        return carry

    lax.fori_loop(0, T, one, 0, unroll=2)


def rim_rows_at(base, rim):
    return pl.ds(pl.multiple_of(base + rim * S, S), S)


def rim_gradients(rim_ref, base, lines_ref, tab_ref, taps_ref, first, count):
    def one(i, carry):
        x = lines_ref[i].astype(F32)
        before, after = neighbours(x)
        u = taps_ref[tab_ref[3, first + i]]
        rim = tab_ref[2, first + i] >> 1
        rim_ref[rim_rows_at(base, rim)] += u[0:1] * after + u[1:2] * x + u[2:3] * before
        return carry

    lax.fori_loop(0, count, one, 0, unroll=8)


def split_rims(split_ref, rim_ref, base):
    def split(t, carry):
        for e in range(4):
            split_store(split_ref, t, e * S, rim_ref[rim_rows_at(base, t * 4 + e)])
        return carry

    lax.fori_loop(0, T, split, 0, unroll=2)


def live_lines(dst_ref, dst_first, line_of, tab_ref, tab_first):
    def one(i, carry):
        live = tab_ref[4, tab_first + i] > 0
        dst_ref[dst_first + i] = jnp.where(live, line_of(i), jnp.zeros((S, 256), BF16))
        return carry

    lax.fori_loop(0, 64, one, 0, unroll=8)


def line_grads(g_ref, c_ref, mixers_ref):
    for b in range(4):
        part = c_ref[b * 16 : b * 16 + 16].reshape(256, 256)
        g_ref[b * 16 : b * 16 + 16] = dot_t(part, mixers_ref[1]).astype(BF16).reshape(16, S, 256)


def gather_out(leave, port, out_ref, rims_ref, lines_ref, tab_ref):
    def some(q, carry):
        for r in range(8):
            s = q * 8 + r
            out_ref[s, 0:S] = rims_ref[tab_ref[2, 64 + s]]
            out_ref[s, S : 2 * S] = lines_ref[tab_ref[1, s]]
        leave(port, q * 8, 8)
        return carry

    lax.fori_loop(0, 8, some, 0)


CORNER_SOURCE = {4: (0, 1), 5: (2, 1), 6: (2, 0), 7: (0, 0)}


def put_corners(lines_ref, t, sides):
    at = iota((S, 1), 0)
    for d, (side, flip) in CORNER_SOURCE.items():
        for f in range(2):
            value = jnp.where(at == (S - 1 if f else 0), sides[side][flip ^ f], 0.0)
            lines_ref[16 * t + 2 * d + f] = value.astype(BF16)


def banks(rims_ref, lines_ref, t, rim_tile, line_tile, sel_ref):
    rims = dot(sel_ref[...], rim_tile).astype(BF16)
    rims_ref[pl.ds(t * 8, 8)] = rims.reshape(8, S, 256)
    lines = dot(sel_ref[...], line_tile)
    lines_ref[pl.ds(t * 16, 8)] = lines.astype(BF16).reshape(8, S, 256)
    groups = [lines[S * k : S * k + S] for k in range(8)]
    put_corners(lines_ref, t, [groups[2 * d : 2 * d + 2] for d in range(4)])


def edge_banks(rims_ref, lines_ref, t, active, gc, turn_ref):
    turned = dot(turn_ref[...], active).astype(BF16)
    back = dot(turn_ref[...], gc)
    sides = []
    for d in range(4):
        part = slice(S * d, S * d + S)
        rims_ref[8 * t + 2 * d] = active[part]
        rims_ref[8 * t + 2 * d + 1] = turned[part]
        lines_ref[16 * t + 2 * d] = gc[part]
        lines_ref[16 * t + 2 * d + 1] = back[part].astype(BF16)
        sides.append((gc[part].astype(F32), back[part]))
    put_corners(lines_ref, t, sides)


def own_position():
    a, b, c = (lax.axis_index(name) for name in TILE)
    return (a * lax.axis_size(TILE[1]) + b) * lax.axis_size(TILE[2]) + c


def first_kernel(
    arrive, leave, slot_ref, code_ref, states_ref, cot_ref, sel_ref, tab_ref, out_ref, rims_ref, lines_ref,
    comb_ref, smem, sem,
):
    me = own_position()
    entries = slot_ref.shape[1]
    groups = entries // T
    sub = iota((128, entries), 0)
    tile = iota((128, entries), 1)
    belongs = (tile & (T - 1)) == (sub >> 3)
    member = (iota((groups, entries), 0) == (iota((groups, entries), 1) >> 3)).astype(F32).astype(BF16)

    def by_block(ref):
        copies = jnp.concatenate([ref[...].astype(F32)] * 16, axis=0)
        return dot_t(member, jnp.where(belongs, copies, 0.0).astype(BF16)).astype(I32)

    comb = by_block(slot_ref) * 8 + by_block(code_ref)
    comb_ref[...] = comb
    lane = iota(comb.shape, 1)
    home = iota(comb.shape, 0)
    slot = comb >> 3
    wanted = (lane < 64) & ((slot >> 3) == me) & (home != me)
    wanted_f = wanted.astype(F32)
    before = (iota((128, 128), 0) < iota((128, 128), 1)).astype(F32).astype(BF16)
    place = dot(wanted_f.astype(BF16), before)
    code = comb & 7
    rim_code = (slot & 7) * 8 + code
    tap_set = (lane & 7) * 2 + (code & 1)
    packed = (rim_code * 16 + tap_set + 1024).astype(F32)
    asked = jnp.zeros((1, 128), F32)
    for k in range(2):
        value = jnp.sum(
            jnp.where(wanted & (place == k), packed, 0.0), axis=1, keepdims=True
        )
        at = (lane >= 64) & (((lane - 64) >> 1) == home) & ((lane & 1) == k)
        asked = asked + jnp.sum(jnp.where(at, value, 0.0), axis=0, keepdims=True)
    asked = asked.astype(I32)

    own = comb_ref[pl.ds(me, 1), :]
    sub2 = iota((128, 128), 0)
    lane2 = iota((128, 128), 1)
    own_wide = jnp.broadcast_to(own, (128, 128))
    own_col = jnp.sum(
        jnp.where(sub2 == lane2, own_wide, 0).astype(F32), axis=1, keepdims=True
    ).astype(I32)
    owner_col = own_col >> 6
    owner_row = own >> 6
    same = (owner_col == owner_row) & (sub2 < 64) & (lane2 < 64)
    place_col = jnp.sum((same & (lane2 < sub2)).astype(F32), axis=1, keepdims=True).astype(I32)
    place_row = jnp.sum((same & (sub2 < lane2)).astype(F32), axis=0, keepdims=True).astype(I32)
    lane1 = iota((1, 128), 1)
    sub1 = iota((128, 1), 0)
    remote_row = owner_row != me
    slot_col = jnp.where((owner_col != me) & (sub1 < 64), owner_col * 2 + place_col, -1)
    line_col = (sub1 * 2 + (own_col & 1)).astype(F32)
    sent = jnp.sum(jnp.where(slot_col == lane2, line_col, 0.0), axis=0, keepdims=True).astype(I32)
    own_rim = (own & 511)
    own_rim = ((own_rim >> 3) & 7) * 8 + (own_rim & 7)
    in_own = lane1 < 64
    panel = jnp.where(remote_row, 64 + owner_row * 2 + place_row, own_rim)
    tab_ref[...] = jnp.zeros_like(tab_ref)
    tab_ref[0:1, :] = jnp.where(in_own, panel, 0)
    tab_ref[1:2, :] = jnp.where(in_own, sent, 0)
    tab_ref[2:3, :] = jnp.where(in_own, own_rim, (asked & 1023) >> 4)
    tab_ref[3:4, :] = jnp.where(in_own, (lane1 & 7) * 2 + (own & 1), asked & 15)
    tab_ref[4:5, :] = jnp.where(in_own, (~remote_row).astype(I32), asked >> 10)
    tab_ref[5:6, :] = jnp.where(in_own, lane1 * 2 + (own & 1), 0)
    copy = pltpu.make_async_copy(tab_ref, smem, sem)
    copy.start()
    arrive(2)
    arrive(3)

    def lines_of(t, carry):
        banks(rims_ref, lines_ref, t, tile_of(states_ref, t), tile_of(cot_ref, t), sel_ref)
        return carry

    lax.fori_loop(0, T, lines_of, 0, unroll=4)
    leave(2, 0, 64)
    leave(3, 0, 128)
    copy.wait()
    gather_out(leave, 1, out_ref, rims_ref, lines_ref, smem)


def edge_cells():
    row = iota((CELLS, 1), 0)
    i, j = row >> 4, row & (S - 1)
    return (i == 0) | (i == S - 1) | (j == 0) | (j == S - 1)


def keep_lines(lines_ref, t, tile_ref):
    at = [pl.ds(0, S), pl.ds(S - 1, S, stride=S), pl.ds(S * (S - 1), S), pl.ds(0, S, stride=S)]
    for d in range(4):
        for h in range(2):
            lines_ref[pl.ds(pl.multiple_of(t * 64 + d * S, S), S), 128 * h : 128 * h + 128] = tile_ref[
                h, at[d], :
            ]


def put_halves(tile_ref, value):
    tile_ref[0] = value[:, 0:128]
    tile_ref[1] = value[:, 128:256]


def activation(hidden):
    cdf = 0.5 * (1.0 + lax.erf(hidden * SQRT_HALF))
    slope = cdf + hidden * jnp.exp(-0.5 * hidden * hidden) * INV_ROOT_TAU
    return (hidden * cdf).astype(BF16), slope


def inner_kernel(
    arrive, leave, tab_ref, states_ref, cot_ref, bank_ref, mixers_ref, stencils_ref, shifts_ref, shift_ref,
    back_ref, g_ref, c_ref, gl_ref, active_ref, first_ref, gh_ref, gc_ref,
    taps_ref, tile1_ref, tile2_ref,
):
    w0 = tap_rows(stencils_ref, 0)
    w1 = tap_rows(stencils_ref, 1)
    arrive(1)
    arrive(2)
    edge = edge_cells()

    def one(t, carry):
        x = tile_of(states_ref, t)
        moved = dot(shift_ref[...], x)
        conv = conv_inner(moved[:CELLS], x.astype(F32), moved[CELLS:], w0)
        put_halves(tile1_ref, conv)
        keep_lines(back_ref, t + 2 * T, tile1_ref)
        first = conv.astype(BF16)
        put_tile(first_ref, t, first)
        leave(5, t * CELLS, CELLS)
        active, slope = activation(dot(first, mixers_ref[0]) + shifts_ref[0:1, :])
        put_tile(active_ref, t, jnp.where(edge, 0.0, active.astype(F32)).astype(BF16))
        leave(4, t * CELLS, CELLS)
        g = dot_t(tile_of(cot_ref, t), mixers_ref[1]).astype(BF16)
        put_tile(g_ref, t, g)
        leave(1, t * CELLS, CELLS)
        moved = dot(shift_ref[...], g)
        back = back_inner(moved[:CELLS], g.astype(F32), moved[CELLS:], w1)
        put_halves(tile2_ref, back)
        keep_lines(back_ref, t, tile2_ref)
        gh = jnp.where(edge, 0.0, back * slope).astype(BF16)
        put_tile(gh_ref, t, gh)
        leave(6, t * CELLS, CELLS)
        put_tile(gc_ref, t, dot_t(gh, mixers_ref[0]).astype(BF16))
        leave(7, t * CELLS, CELLS)
        return carry

    lax.fori_loop(0, T, one, 0)
    arrive(3)
    fill_tap_sets(taps_ref, stencils_ref, 1)
    live_lines(c_ref, 0, lambda i: bank_ref[tab_ref[5, i]], tab_ref, 0)
    leave(2, 0, 64)
    line_grads(gl_ref, c_ref, mixers_ref)
    leave(3, 0, 64)
    back_ref[2 * CELLS : 4 * CELLS] = jnp.zeros((2 * CELLS, 256), F32)
    rim_gradients(back_ref, 2 * CELLS, gl_ref, tab_ref, taps_ref, 0, 64)
    leave(0, 0, 6 * CELLS)


def middle_kernel(
    arrive, leave,
    tab_ref, in_ref, rims_in_ref, back_ref, mixers_ref, stencils_ref,
    shifts_ref, turn_ref, cross_ref,
    active_ref, first_ref, gh_ref, gc_ref, rims_ref, lines_ref, out_ref, c_ref, g_ref, panels_ref,
    buf_ref, split_ref, split2_ref, taps_ref,
):
    w0 = tap_rows(stencils_ref, 0)
    fill_tap_sets(taps_ref, stencils_ref, 1)
    buf_ref[64:128] = in_ref[:, 0:S, :]
    live_lines(c_ref, 0, lambda i: in_ref[i, S : 2 * S], tab_ref, 64)
    leave(7, 0, 64)
    line_grads(g_ref, c_ref, mixers_ref)
    leave(8, 0, 64)
    arrive(2)
    buf_ref[0:64] = rims_in_ref[...]
    forward_lines(split_ref, buf_ref, tab_ref, w0, panels_ref)
    leave(9, 0, 64)
    arrive(3)
    rim_gradients(back_ref, 2 * CELLS, g_ref, tab_ref, taps_ref, 64, 64)
    split_rims(split2_ref, back_ref, 2 * CELLS)
    at = iota((CELLS, 1), 0)
    twice = (((at >> 4) & 1) == 1) & (((at & (S - 1)) == 0) | ((at & (S - 1)) == S - 1))

    def updates(ref, u):
        return jnp.concatenate([dot(cross_ref[...], ref[4 * u + q]) for q in range(4)], axis=0)

    for u in range(2):
        part = slice(u * CELLS, (u + 1) * CELLS)
        conv = back_ref[(u + 4) * CELLS : (u + 5) * CELLS]
        first = (conv + updates(split_ref, u)).astype(BF16)
        first_ref[part] = first
        active, slope = activation(dot(first, mixers_ref[0]) + shifts_ref[0:1, :])
        active_ref[part] = active
        grad = (back_ref[part] + updates(split2_ref, u)) * slope
        gh_ref[part] = jnp.where(twice, 0.0, grad).astype(BF16)
        gc = dot_t(grad.astype(BF16), mixers_ref[0]).astype(BF16)
        gc_ref[part] = gc
        for q in range(4):
            t = 4 * u + q
            rows = slice(64 * q, 64 * q + 64)
            edge_banks(rims_ref, lines_ref, t, active[rows], gc[rows], turn_ref)
    for k in range(4):
        leave(k, 0, 2 * CELLS)
    leave(4, 0, 64)
    leave(5, 0, 128)
    gather_out(leave, 6, out_ref, rims_ref, lines_ref, tab_ref)


def weight_kernel(
    arrive, leave,
    tab_ref, states_ref, cot_ref, active_ref, first_ref, gh_ref, gc_ref, g2_ref, rims_ref, lines_ref,
    panels_ref, c_own_ref, g_own_ref, c_in_ref, g_in_ref,
    active_edge_ref, first_edge_ref, gh_edge_ref, gc_edge_ref, stencils_ref, shift_ref, place_ref,
    pack_ref, conv_ref, gc_out_ref,
    second_ref, h_ref, taps_ref, acc1_ref, acc2_ref, accl_ref, sums_ref,
):
    w1 = tap_rows(stencils_ref, 1)
    acc1_ref[...] = jnp.zeros_like(acc1_ref)
    acc2_ref[...] = jnp.zeros_like(acc2_ref)
    accl_ref[...] = jnp.zeros_like(accl_ref)
    sums_ref[...] = jnp.zeros_like(sums_ref)
    fill_tap_sets(taps_ref, stencils_ref, 1)

    def folded(x):
        return jnp.sum(x.reshape(-1, 8, 256), axis=0)

    def taps_of(acc_ref, g, left, centre, right):
        for b, x in enumerate((left, centre, right)):
            acc_ref[b] += folded(g[S:] * x[: CELLS - S])
            acc_ref[3 + b] += folded(g * x)
            acc_ref[6 + b] += folded(g[: CELLS - S] * x[S:])

    def halves(x):
        return x[0:8] + x[8:16]

    def second_halo(source_ref):
        def one(i, carry):
            x = rims_ref[(tab_ref[2, i] >> 1) * 2].astype(F32)
            g = source_ref[i & 63].astype(F32)
            before, after = neighbours(x)
            kind = tab_ref[3, i]
            u = taps_ref[kind]
            h_ref[i] = (u[0:1] * before + u[1:2] * x + u[2:3] * after).astype(BF16)
            for m, y in enumerate((before, x, after)):
                accl_ref[kind, m] += halves(g * y)
            return carry

        return one

    arrive(8)
    arrive(12)
    lax.fori_loop(0, 64, second_halo(g_own_ref), 0, unroll=8)
    arrive(14)
    lax.fori_loop(64, 128, second_halo(g_in_ref), 0, unroll=8)

    for k in (9, 10):
        arrive(k)

    def first_halo(t, carry):
        for d in range(8):
            x = panels_ref[t * 8 + d].astype(F32)
            g = lines_ref[(t * 8 + d) * 2].astype(F32)
            if d < 4:
                before, after = neighbours(x)
                for k, y in zip(SIDE_TAPS[d], (before, x, after)):
                    acc1_ref[k] += halves(g * y)
            else:
                acc1_ref[CORNER_TAP[d]] += halves(g * x)
        return carry

    lax.fori_loop(0, T, first_halo, 0, unroll=2)

    for k in (6, 18, 1, 3, 15, 7, 5, 17, 2):
        arrive(k)

    def whole(inner_ref, edge_ref, t):
        edges = edge_ref[pl.ds(pl.multiple_of(t * 64, 64), 64), :]
        return tile_of(inner_ref, t).astype(F32) + dot(place_ref[...], edges)

    sums_ref[0] += folded(gh_edge_ref[...].astype(F32))

    def one(t, carry):
        gcf = whole(gc_ref, gc_edge_ref, t)
        put_tile(gc_out_ref, t, gcf.astype(BF16))
        leave(2, t * CELLS, CELLS)
        x = tile_of(states_ref, t)
        moved = dot(shift_ref[...], x)
        taps_of(acc1_ref, gcf, moved[:CELLS], x.astype(F32), moved[CELLS:])
        xf = whole(active_ref, active_edge_ref, t)
        moved = dot(shift_ref[...], xf.astype(BF16))
        second = conv_inner(moved[:CELLS], xf, moved[CELLS:], w1)
        put_tile(conv_ref, t, second)
        leave(1, t * CELLS, CELLS)
        put_tile(second_ref, t, second.astype(BF16))
        taps_of(acc2_ref, tile_of(g2_ref, t).astype(F32), moved[:CELLS], xf, moved[CELLS:])
        sums_ref[0] += folded(tile_of(gh_ref, t).astype(F32))
        sums_ref[1] += folded(tile_of(cot_ref, t).astype(F32))
        return carry

    lax.fori_loop(0, T, one, 0)
    for k in (4, 16, 11, 13):
        arrive(k)
    for d in range(8):
        for f in range(2):
            if d < 4:
                taps = SIDE_TAPS[d][::-1] if f else SIDE_TAPS[d]
                for m, k in enumerate(taps):
                    acc2_ref[k] += accl_ref[2 * d + f, m]
            else:
                acc2_ref[CORNER_TAP[d]] += accl_ref[2 * d + f, 1]

    rows = [jnp.sum(acc1_ref[k], axis=0, keepdims=True) for k in range(9)]
    rows += [jnp.sum(acc2_ref[k], axis=0, keepdims=True) for k in range(9)]
    rows += [jnp.sum(sums_ref[k], axis=0, keepdims=True) for k in range(2)]
    rows = [row[:, 128 * h : 128 * h + 128] for row in rows for h in range(2)]
    for r in range(5):
        pack_ref[r, 32:40] = jnp.concatenate(rows[8 * r : 8 * r + 8], axis=0).astype(BF16)
    for r in range(5, pack_ref.shape[0]):
        pack_ref[r, 32:40] = jnp.zeros((8, 128), BF16)
    half = pack_ref.shape[0] // 2

    def put_rows(r, rows16):
        for q in range(4):
            at = (q // 2) * 8, (q % 2) * 128
            pack_ref[r, 8 * q : 8 * q + 8] = rows16[at[0] : at[0] + 8, at[1] : at[1] + 128].astype(BF16)

    mixer_first = t_dot(first_ref[...], gh_ref[...]) + t_dot(first_edge_ref[...], gh_edge_ref[...])
    for r in range(half):
        put_rows(r, mixer_first[16 * r : 16 * r + 16])
    leave(0, 0, half)
    mixer_second = (
        t_dot(second_ref[...], cot_ref[...])
        + t_dot(h_ref[0:64].reshape(1024, 256), c_own_ref[...].reshape(1024, 256))
        + t_dot(h_ref[64:128].reshape(1024, 256), c_in_ref[...].reshape(1024, 256))
    )
    for r in range(half):
        put_rows(half + r, mixer_second[16 * r : 16 * r + 16])
    leave(0, half, half)


def outcome_kernel(
    arrive, leave,
    tab_ref, in_ref, rims_in_ref, bank_ref, conv_ref, states_ref, mixers_ref, stencils_ref, shifts_ref,
    spread_ref,
    outcome_ref, halo_ref,
    buf_ref, split_ref, rim_ref, taps_ref, lines_ref,
):
    w1 = tap_rows(stencils_ref, 1)
    arrive(2)
    buf_ref[0:64] = rims_in_ref[...]
    arrive(1)
    buf_ref[64:128] = in_ref[:, 0:S, :]
    forward_lines(split_ref, buf_ref, tab_ref, w1)
    arrive(4)
    arrive(5)

    def one(t, carry):
        second = (tile_of(conv_ref, t) + dot(spread_ref[...], split_ref[t])).astype(BF16)
        out = tile_of(states_ref, t).astype(F32) + dot(second, mixers_ref[1]) + shifts_ref[1:2, :]
        put_tile(outcome_ref, t, out.astype(BF16))
        leave(0, t * CELLS, CELLS)
        return carry

    lax.fori_loop(0, T, one, 0, unroll=2)
    fill_tap_sets(taps_ref, stencils_ref, 0)
    rim_ref[...] = jnp.zeros_like(rim_ref)
    arrive(3)
    live_lines(lines_ref, 0, lambda i: bank_ref[tab_ref[5, i]], tab_ref, 0)
    live_lines(lines_ref, 64, lambda i: in_ref[i, S : 2 * S], tab_ref, 64)
    rim_gradients(rim_ref, 0, lines_ref, tab_ref, taps_ref, 0, 128)
    split_rims(halo_ref, rim_ref, 0)
    leave(1, 0, T)


def grad_kernel(
    arrive, leave,
    gc_ref, halo_ref, cot_ref, stencils_ref, shift_ref, spread_ref,
    grad_ref,
):
    w0 = tap_rows(stencils_ref, 0)
    for k in range(3):
        arrive(k)

    def one(t, carry):
        gc = tile_of(gc_ref, t)
        moved = dot(shift_ref[...], gc)
        grad = back_inner(moved[:CELLS], gc.astype(F32), moved[CELLS:], w0)
        grad = grad + dot(spread_ref[...], halo_ref[t]) + tile_of(cot_ref, t).astype(F32)
        put_tile(grad_ref, t, grad.astype(BF16))
        leave(0, t * CELLS, CELLS)
        return carry

    lax.fori_loop(0, T, one, 0)


def sum_kernel(arrive, leave, in_ref, out_ref):
    total = in_ref[0].astype(F32)
    for r in range(1, in_ref.shape[0]):
        total = total + in_ref[r].astype(F32)
    for r in range(out_ref.shape[0]):
        out_ref[r] = total.astype(BF16)


def spread_kernel(arrive, leave, in_ref, out_ref):
    total = in_ref[0].astype(F32)
    for r in range(1, in_ref.shape[0]):
        total = total + in_ref[r].astype(F32)
    value = total.astype(BF16)
    for r in range(out_ref.shape[0]):
        out_ref[r] = value


def unpack_kernel(scale, arrive, leave, in_ref, mixer_ref, stencil_ref, shift_ref):
    half = in_ref.shape[0] // 2
    for k in range(2):
        for r in range(half):
            for q in range(4):
                block = in_ref[k * half + r, 8 * q : 8 * q + 8].astype(F32) * scale
                row, col = 16 * r + (q // 2) * 8, (q % 2) * 128
                mixer_ref[k, row : row + 8, col : col + 128] = block
        leave(0, k, 1)
    rows = [in_ref[r, 32:40].astype(F32) * scale for r in range(5)]
    rows = [row for block in rows for row in jnp.split(block, 8, axis=0)]
    for k in range(2):
        for h in range(2):
            part = slice(128 * h, 128 * h + 128)
            for j in range(9):
                stencil_ref[j, k : k + 1, part] = rows[2 * (9 * k + j) + h]
            shift_ref[k : k + 1, part] = rows[2 * (18 + k) + h]


def shape_of(*dims, dtype=BF16):
    return jax.ShapeDtypeStruct(dims, dtype)


def call(body, ins, in_modes, outs, out_modes, scratch=(), limit=60.0, order=None):
    spaces = {"s": pltpu.SMEM, "v": pltpu.VMEM, "h": pltpu.HBM}
    ports_in = order or [k for k, mode in enumerate(in_modes) if mode == "h"]
    ports_out = [k for k, mode in enumerate(out_modes) if mode == "h"]
    n_in, n_out, n_own = len(ins), len(outs), len(scratch)

    def kernel(*refs):
        in_refs = list(refs[:n_in])
        out_refs = list(refs[n_in : n_in + n_out])
        rest = list(refs[n_in + n_out :])
        own, rest = rest[:n_own], rest[n_own:]
        sem_in, sem_out = rest[-2:]
        inward, outward = {}, {}
        for q, k in enumerate(ports_in):
            inward[k] = pltpu.make_async_copy(in_refs[k], rest[q], sem_in.at[q])
            inward[k].start()
            in_refs[k] = rest[q]
        for q, k in enumerate(ports_out):
            buffer = rest[len(ports_in) + q]
            outward[k] = (buffer, out_refs[k], sem_out.at[q])
            out_refs[k] = buffer

        def arrive(k):
            if k in inward:
                inward[k].wait()

        def leave(k, first, count):
            if k in outward:
                source, target, sem = outward[k]
                part = pl.ds(first, count)
                pltpu.make_async_copy(source.at[part], target.at[part], sem).start()

        body(arrive, leave, *in_refs, *out_refs, *own)
        for source, target, sem in outward.values():
            pltpu.make_async_copy(source, target, sem).wait()

    buffers = [pltpu.VMEM(ins[k].shape, ins[k].dtype) for k in ports_in]
    buffers += [pltpu.VMEM(outs[k].shape, outs[k].dtype) for k in ports_out]
    sems = [pltpu.SemaphoreType.DMA((max(1, len(p)),)) for p in (ports_in, ports_out)]
    return pl.pallas_call(
        kernel,
        out_shape=[
            pltpu.HBM(o.shape, o.dtype) if m == "h" else o for o, m in zip(outs, out_modes)
        ],
        in_specs=[pl.BlockSpec(memory_space=spaces[m]) for m in in_modes],
        out_specs=[pl.BlockSpec(memory_space=spaces[m]) for m in out_modes],
        scratch_shapes=list(scratch) + buffers + sems,
        compiler_params=pltpu.CompilerParams(vmem_limit_bytes=int(limit * 1024 * 1024)),
    )(*ins)


def exchange(array):
    return lax.all_to_all(array, TILE, split_axis=0, concat_axis=0, tiled=True)


def whole_block(states, cotangent, beside_slot, beside_code, mixers, stencils, shifts):
    groups = lax.axis_size(TILE)
    batch = lax.axis_size("batch")
    shape = states.shape
    x = states.reshape(T * CELLS, 256)
    cot = cotangent.reshape(T * CELLS, 256)
    sel = jnp.asarray(selection()[:128], BF16)
    spread = jnp.asarray(spreading(), BF16)
    shift = jnp.asarray(shifting(), BF16)
    taps = stencils.swapaxes(0, 1)
    lines16 = shape_of(128, S, 256)
    rims16 = shape_of(64, S, 256)
    sent16 = shape_of(64, 2 * S, 256)
    field = shape_of(T * CELLS, 256)
    wide = shape_of(T * CELLS, 256, dtype=F32)
    lines_scratch = pltpu.VMEM((128, S, 256), BF16)
    split_scratch = pltpu.VMEM((T, 128, 256), BF16)
    rim_scratch = pltpu.VMEM((2 * CELLS, 256), F32)
    taps_scratch = pltpu.VMEM((16, 3, 256), F32)
    tab, out1, rims1, lines1 = call(
        first_kernel,
        (beside_slot.astype(I32).T, beside_code.astype(I32).T, x, cot, sel),
        "vvhhv",
        [shape_of(8, 128, dtype=I32), sent16, rims16, lines16],
        "vhhh",
        [
            pltpu.VMEM((groups, 128), I32),
            pltpu.SMEM((8, 128), I32),
            pltpu.SemaphoreType.DMA,
        ],
    )
    in1 = exchange(out1.reshape(groups, 4 * S, 256)).reshape(64, 2 * S, 256)
    turn, cross, place = (jnp.asarray(m, BF16) for m in line_matrices())
    edge = shape_of(2 * CELLS, 256)
    tile_scratch = pltpu.VMEM((2, CELLS, 128), F32)
    back2, g2, c_own, g_own, active, first, gh, gc = call(
        inner_kernel,
        (tab, x, cot, lines1, mixers, taps, shifts, shift),
        "shhhvvvv",
        [
            shape_of(6 * CELLS, 256, dtype=F32),
            field,
            rims16,
            rims16,
            field,
            field,
            field,
            field,
        ],
        "hhhhhhhh",
        [taps_scratch, tile_scratch, tile_scratch],
    )
    active_e, first_e, gh_e, gc_e, rims2, lines2, out2, c_in, g_in, panels = call(
        middle_kernel,
        (tab, in1, rims1, back2, mixers, taps, shifts, turn, cross),
        "svhhvvvvv",
        [edge, edge, edge, edge, rims16, lines16, sent16, rims16, rims16, rims16],
        "hhhhhhhhhh",
        [lines_scratch, split_scratch, split_scratch, taps_scratch],
        limit=51.0,
    )
    in2 = exchange(out2.reshape(groups, 4 * S, 256)).reshape(64, 2 * S, 256)
    pack, conv2, gc_all = call(
        weight_kernel,
        (tab, x, cot, active, first, gh, gc, g2, rims2, lines2, panels, c_own, g_own, c_in, g_in,
         active_e, first_e, gh_e, gc_e, taps, shift, place),
        "shhhhhhhhhhhhhhhhhhvvv",
        [shape_of(groups, 40, 128), wide, field],
        "hhh",
        [
            pltpu.VMEM((T * CELLS, 256), BF16),
            lines_scratch,
            taps_scratch,
            pltpu.VMEM((9, 8, 256), F32),
            pltpu.VMEM((9, 8, 256), F32),
            pltpu.VMEM((16, 3, 8, 256), F32),
            pltpu.VMEM((2, 8, 256), F32),
        ],
        order=(8, 12, 14, 9, 10, 6, 18, 1, 3, 15, 7, 5, 17, 2, 4, 16, 11, 13),
    )
    parts = exchange(pack)
    outcome, halo = call(
        outcome_kernel,
        (tab, in2, rims2, lines2, conv2, x, mixers, taps, shifts, spread),
        "shhhhhvvvv",
        [field, shape_of(T, 128, 256)],
        "hh",
        [lines_scratch, split_scratch, rim_scratch, taps_scratch, lines_scratch],
        order=(2, 1, 4, 5, 3),
    )
    (part,) = call(sum_kernel, (parts,), "v", [shape_of(batch, 40, 128)], "v", limit=4)
    part = lax.all_to_all(part, "batch", split_axis=0, concat_axis=0, tiled=True)
    (spread_out,) = call(spread_kernel, (part,), "v", [shape_of(groups, 40, 128)], "v", limit=4)
    whole = exchange(spread_out)
    (state_grad,) = call(
        grad_kernel, (gc_all, halo, cot, taps, shift, spread), "hhhvvv", [field], "h"
    )
    scale = 1.0 / math.sqrt(T * CELLS * groups * batch)

    def unpack(*refs):
        unpack_kernel(scale, *refs)

    mixer_grads, stencil_grads, shift_grads = call(
        unpack,
        (whole,),
        "v",
        [shape_of(2, 256, 256, dtype=F32), shape_of(9, 2, 256, dtype=F32), shape_of(2, 256, dtype=F32)],
        "hvv",
        limit=4,
    )
    stencil_grads = stencil_grads.swapaxes(0, 1)
    return (
        outcome.reshape(shape),
        state_grad.reshape(shape),
        mixer_grads,
        stencil_grads,
        shift_grads,
    )


def solution(mesh):
    torus = Mesh(
        mesh.devices.reshape(4, 4, 2, mesh.shape["batch"]), ("tile_0", "tile_1", "tile_2", "batch")
    )
    in_specs = (
        P("batch", TILE, None, None, None),
        P("batch", TILE, None, None, None),
        P(),
        P(),
        P(),
        P(),
        P(),
    )
    out_specs = (
        P("batch", TILE, None, None, None),
        P("batch", TILE, None, None, None),
        P(),
        P(),
        P(),
    )
    return jax.shard_map(
        whole_block, mesh=torus, in_specs=in_specs, out_specs=out_specs, check_vma=False
    )
```

```python
import math

import jax
import jax.numpy as jnp
import numpy as np
from jax import lax
from jax.experimental import pallas as pl
from jax.experimental.pallas import tpu as pltpu
from jax.sharding import Mesh
from jax.sharding import PartitionSpec as P


TILE = ("tile_0", "tile_1", "tile_2")
SQRT_HALF = 0.7071067811865476
INV_ROOT_TAU = 0.3989422804014327

F32 = jnp.float32
BF16 = jnp.bfloat16
I32 = jnp.int32

S = 16
T = 8
CELLS = S * S
SIDE_TAPS = {0: (0, 1, 2), 1: (2, 5, 8), 2: (6, 7, 8), 3: (0, 3, 6)}
CORNER_TAP = {4: 2, 5: 8, 6: 6, 7: 0}


def line_cell(d, i):
    if d == 0:
        return i
    if d == 1:
        return S * i + S - 1
    if d == 2:
        return S * (S - 1) + i
    if d == 3:
        return S * i
    if i != 0:
        return None
    return {4: S - 1, 5: CELLS - 1, 6: S * (S - 1), 7: 0}[d]


def selection():
    sel = np.zeros((256, CELLS), np.float32)
    for d in range(8):
        for f in range(2):
            for i in range(S):
                cell = line_cell(d, S - 1 - i if f else i)
                if cell is not None:
                    sel[(2 * d + f) * S + i, cell] = 1.0
    return sel


def spreading():
    out = np.zeros((CELLS, 128), np.float32)
    for d in range(4):
        for i in range(S):
            out[line_cell(d, i), d * S + i] = 1.0
            out[line_cell(d, i), 64 + d * S + i] = 1.0
    return out


def shifting():
    out = np.zeros((512, CELLS), np.float32)
    for i in range(S):
        for j in range(S):
            if j > 0:
                out[S * i + j, S * i + j - 1] = 1.0
            if j < S - 1:
                out[256 + S * i + j, S * i + j + 1] = 1.0
    return out


def line_matrices():
    sel = selection()
    lines = np.concatenate([sel[32 * d : 32 * d + S] for d in range(4)])
    turn = np.kron(np.eye(4), np.eye(S)[::-1]).astype(np.float32)
    place = np.zeros((CELLS, 64), np.float32)
    for cell in range(CELLS):
        at = np.flatnonzero(lines[:, cell])
        if at.size:
            home = [q for q in at if (q // S) % 2 == 0] or list(at)
            place[cell, home[0]] = 1.0
    return turn, lines @ spreading(), place


def dot(a, b):
    return jnp.dot(a, b, preferred_element_type=F32)


def dot_t(a, b):
    return lax.dot_general(a, b, (((1,), (1,)), ((), ())), preferred_element_type=F32)


def t_dot(a, b):
    return lax.dot_general(a, b, (((0,), (0,)), ((), ())), preferred_element_type=F32)


def iota(shape, axis):
    return lax.broadcasted_iota(I32, shape, axis)


def neighbours(x):
    place = iota(x.shape, 0)
    before = jnp.where(place == 0, 0.0, pltpu.roll(x, 1, 0))
    after = jnp.where(place == S - 1, 0.0, pltpu.roll(x, S - 1, 0))
    return before, after


def down(x):
    return jnp.concatenate([jnp.zeros((S, x.shape[1]), x.dtype), x[: CELLS - S]], axis=0)


def up(x):
    return jnp.concatenate([x[S:], jnp.zeros((S, x.shape[1]), x.dtype)], axis=0)


def conv_inner(left, centre, right, w):
    rows = [w[3 * a] * left + w[3 * a + 1] * centre + w[3 * a + 2] * right for a in range(3)]
    return rows[1] + down(rows[0]) + up(rows[2])


def back_inner(left, centre, right, w):
    rows = [w[3 * a] * right + w[3 * a + 1] * centre + w[3 * a + 2] * left for a in range(3)]
    return rows[1] + up(rows[0]) + down(rows[2])


def tap_rows(ref, layer):
    return [ref[k, layer : layer + 1, :] for k in range(9)]


def fill_tap_sets(taps_ref, stencil_ref, layer):
    w = tap_rows(stencil_ref, layer)
    zero = jnp.zeros_like(w[0])
    for d in range(8):
        if d < 4:
            three = [w[k] for k in SIDE_TAPS[d]]
        else:
            three = [zero, w[CORNER_TAP[d]], zero]
        for f in range(2):
            for m, row in enumerate(three[::-1] if f else three):
                taps_ref[2 * d + f, m : m + 1, :] = row


def tile_of(ref, t):
    return ref[pl.ds(pl.multiple_of(t * CELLS, CELLS), CELLS), :]


def put_tile(ref, t, value):
    ref[pl.ds(pl.multiple_of(t * CELLS, CELLS), CELLS), :] = value


def split_store(ref, t, first, value):
    high = value.astype(BF16)
    ref[t, pl.ds(first, value.shape[0]), :] = high
    ref[t, pl.ds(64 + first, value.shape[0]), :] = (value - high.astype(F32)).astype(BF16)


def forward_lines(split_ref, rims_ref, in_ref, tab_ref, w, panels_ref=None):
    def panel_of(k):
        place = tab_ref[0, k]
        own = rims_ref[jnp.minimum(place, 63)]
        sent = in_ref[jnp.maximum(place - 64, 0), 0:S]
        return jnp.where(place < 64, own, sent)

    def one(t, carry):
        corner = {}
        for d in range(4, 8):
            panel = panel_of(t * 8 + d)
            if panels_ref is not None:
                panels_ref[t * 8 + d] = panel
            row = panel[:8, :].astype(F32)[:1, :]
            corner[d] = w[CORNER_TAP[d]] * row
        for d in range(4):
            panel = panel_of(t * 8 + d)
            if panels_ref is not None:
                panels_ref[t * 8 + d] = panel
            x = panel.astype(F32)
            before, after = neighbours(x)
            a, b, c = SIDE_TAPS[d]
            line = w[a] * before + w[b] * x + w[c] * after
            at = iota(line.shape, 0)
            if d == 0:
                line = line + jnp.where(at == 0, corner[7], 0.0)
                line = line + jnp.where(at == S - 1, corner[4], 0.0)
            if d == 2:
                line = line + jnp.where(at == 0, corner[6], 0.0)
                line = line + jnp.where(at == S - 1, corner[5], 0.0)
            split_store(split_ref, t, d * S, line)
        return carry

    lax.fori_loop(0, T, one, 0, unroll=2)


def rim_rows_at(base, rim):
    return pl.ds(pl.multiple_of(base + rim * S, S), S)


def rim_gradients(rim_ref, base, lines_ref, tab_ref, taps_ref, first, count):
    def one(i, carry):
        x = lines_ref[i].astype(F32)
        before, after = neighbours(x)
        u = taps_ref[tab_ref[3, first + i]]
        rim = tab_ref[2, first + i] >> 1
        rim_ref[rim_rows_at(base, rim)] += u[0:1] * after + u[1:2] * x + u[2:3] * before
        return carry

    lax.fori_loop(0, count, one, 0, unroll=8)


def split_rims(split_ref, rim_ref, base):
    def split(t, carry):
        for e in range(4):
            split_store(split_ref, t, e * S, rim_ref[rim_rows_at(base, t * 4 + e)])
        return carry

    lax.fori_loop(0, T, split, 0, unroll=2)


def live_lines(dst_ref, dst_first, line_of, tab_ref, tab_first):
    def one(i, carry):
        live = tab_ref[4, tab_first + i] > 0
        dst_ref[dst_first + i] = jnp.where(live, line_of(i), jnp.zeros((S, 256), BF16))
        return carry

    lax.fori_loop(0, 64, one, 0, unroll=8)


def line_grads(g_ref, c_ref, mixers_ref):
    for b in range(4):
        part = c_ref[b * 16 : b * 16 + 16].reshape(256, 256)
        g_ref[b * 16 : b * 16 + 16] = dot_t(part, mixers_ref[1]).astype(BF16).reshape(16, S, 256)


def gather_out(leave, port, out_ref, rims_ref, lines_ref, tab_ref):
    def some(q, carry):
        for r in range(8):
            s = q * 8 + r
            out_ref[s, 0:S] = rims_ref[tab_ref[2, 64 + s]]
            out_ref[s, S : 2 * S] = lines_ref[tab_ref[1, s]]
        leave(port, q * 8, 8)
        return carry

    lax.fori_loop(0, 8, some, 0)


CORNER_SOURCE = {4: (0, 1), 5: (2, 1), 6: (2, 0), 7: (0, 0)}


def put_corners(lines_ref, t, sides):
    at = iota((S, 1), 0)
    for d, (side, flip) in CORNER_SOURCE.items():
        for f in range(2):
            value = jnp.where(at == (S - 1 if f else 0), sides[side][flip ^ f], 0.0)
            lines_ref[16 * t + 2 * d + f] = value.astype(BF16)


def bank_rims(rims_ref, t, tile, sel_ref):
    rims = dot(sel_ref[...], tile).astype(BF16)
    rims_ref[pl.ds(t * 8, 8)] = rims.reshape(8, S, 256)


def bank_lines(lines_ref, t, tile, sel_ref):
    lines = dot(sel_ref[...], tile)
    lines_ref[pl.ds(t * 16, 8)] = lines.astype(BF16).reshape(8, S, 256)
    groups = [lines[S * k : S * k + S] for k in range(8)]
    put_corners(lines_ref, t, [groups[2 * d : 2 * d + 2] for d in range(4)])


def edge_banks(rims_ref, lines_ref, t, active, gc, turn_ref):
    turned = dot(turn_ref[...], active).astype(BF16)
    back = dot(turn_ref[...], gc)
    sides = []
    for d in range(4):
        part = slice(S * d, S * d + S)
        rims_ref[8 * t + 2 * d] = active[part]
        rims_ref[8 * t + 2 * d + 1] = turned[part]
        lines_ref[16 * t + 2 * d] = gc[part]
        lines_ref[16 * t + 2 * d + 1] = back[part].astype(BF16)
        sides.append((gc[part].astype(F32), back[part]))
    put_corners(lines_ref, t, sides)


def own_position():
    a, b, c = (lax.axis_index(name) for name in TILE)
    return (a * lax.axis_size(TILE[1]) + b) * lax.axis_size(TILE[2]) + c


def first_kernel(
    arrive, leave, slot_ref, code_ref, states_ref, cot_ref, sel_ref, tab_ref, out_ref, rims_ref,
    lines_ref, comb_ref, smem, sem,
):
    me = own_position()
    entries = slot_ref.shape[1]
    groups = entries // T
    sub = iota((128, entries), 0)
    tile = iota((128, entries), 1)
    belongs = (tile & (T - 1)) == (sub >> 3)
    member = (iota((groups, entries), 0) == (iota((groups, entries), 1) >> 3)).astype(F32).astype(BF16)

    def by_block(ref):
        copies = jnp.concatenate([ref[...].astype(F32)] * 16, axis=0)
        return dot_t(member, jnp.where(belongs, copies, 0.0).astype(BF16)).astype(I32)

    comb = by_block(slot_ref) * 8 + by_block(code_ref)
    comb_ref[...] = comb
    lane = iota(comb.shape, 1)
    home = iota(comb.shape, 0)
    slot = comb >> 3
    wanted = (lane < 64) & ((slot >> 3) == me) & (home != me)
    wanted_f = wanted.astype(F32)
    before = (iota((128, 128), 0) < iota((128, 128), 1)).astype(F32).astype(BF16)
    place = dot(wanted_f.astype(BF16), before)
    code = comb & 7
    rim_code = (slot & 7) * 8 + code
    tap_set = (lane & 7) * 2 + (code & 1)
    packed = (rim_code * 16 + tap_set + 1024).astype(F32)
    asked = jnp.zeros((1, 128), F32)
    for k in range(2):
        value = jnp.sum(
            jnp.where(wanted & (place == k), packed, 0.0), axis=1, keepdims=True
        )
        at = (lane >= 64) & (((lane - 64) >> 1) == home) & ((lane & 1) == k)
        asked = asked + jnp.sum(jnp.where(at, value, 0.0), axis=0, keepdims=True)
    asked = asked.astype(I32)

    own = comb_ref[pl.ds(me, 1), :]
    sub2 = iota((128, 128), 0)
    lane2 = iota((128, 128), 1)
    own_wide = jnp.broadcast_to(own, (128, 128))
    own_col = jnp.sum(
        jnp.where(sub2 == lane2, own_wide, 0).astype(F32), axis=1, keepdims=True
    ).astype(I32)
    owner_col = own_col >> 6
    owner_row = own >> 6
    same = (owner_col == owner_row) & (sub2 < 64) & (lane2 < 64)
    place_col = jnp.sum((same & (lane2 < sub2)).astype(F32), axis=1, keepdims=True).astype(I32)
    place_row = jnp.sum((same & (sub2 < lane2)).astype(F32), axis=0, keepdims=True).astype(I32)
    lane1 = iota((1, 128), 1)
    sub1 = iota((128, 1), 0)
    remote_row = owner_row != me
    slot_col = jnp.where((owner_col != me) & (sub1 < 64), owner_col * 2 + place_col, -1)
    line_col = (sub1 * 2 + (own_col & 1)).astype(F32)
    sent = jnp.sum(jnp.where(slot_col == lane2, line_col, 0.0), axis=0, keepdims=True).astype(I32)
    own_rim = (own & 511)
    own_rim = ((own_rim >> 3) & 7) * 8 + (own_rim & 7)
    in_own = lane1 < 64
    panel = jnp.where(remote_row, 64 + owner_row * 2 + place_row, own_rim)
    tab_ref[...] = jnp.zeros_like(tab_ref)
    tab_ref[0:1, :] = jnp.where(in_own, panel, 0)
    tab_ref[1:2, :] = jnp.where(in_own, sent, 0)
    tab_ref[2:3, :] = jnp.where(in_own, own_rim, (asked & 1023) >> 4)
    tab_ref[3:4, :] = jnp.where(in_own, (lane1 & 7) * 2 + (own & 1), asked & 15)
    tab_ref[4:5, :] = jnp.where(in_own, (~remote_row).astype(I32), asked >> 10)
    tab_ref[5:6, :] = jnp.where(in_own, lane1 * 2 + (own & 1), 0)
    copy = pltpu.make_async_copy(tab_ref, smem, sem)
    copy.start()
    arrive(2)
    for t in range(T):
        bank_rims(rims_ref, t, tile_of(states_ref, t), sel_ref)
    leave(2, 0, 64)
    arrive(3)
    for t in range(T):
        bank_lines(lines_ref, t, tile_of(cot_ref, t), sel_ref)
    copy.wait()
    gather_out(leave, 1, out_ref, rims_ref, lines_ref, smem)


def edge_cells():
    row = iota((CELLS, 1), 0)
    i, j = row >> 4, row & (S - 1)
    return (i == 0) | (i == S - 1) | (j == 0) | (j == S - 1)


def keep_lines(lines_ref, t, tile_ref):
    at = [pl.ds(0, S), pl.ds(S - 1, S, stride=S), pl.ds(S * (S - 1), S), pl.ds(0, S, stride=S)]
    for d in range(4):
        for h in range(2):
            lines_ref[pl.ds(pl.multiple_of(t * 64 + d * S, S), S), 128 * h : 128 * h + 128] = tile_ref[
                h, at[d], :
            ]


def put_halves(tile_ref, value):
    tile_ref[0] = value[:, 0:128]
    tile_ref[1] = value[:, 128:256]


def activation(hidden):
    cdf = 0.5 * (1.0 + lax.erf(hidden * SQRT_HALF))
    slope = cdf + hidden * jnp.exp(-0.5 * hidden * hidden) * INV_ROOT_TAU
    return (hidden * cdf).astype(BF16), slope


def inner_kernel(
    arrive, leave, tab_ref, states_ref, cot_ref, mixers_ref, stencils_ref, shifts_ref, shift_ref, sel_ref,
    back_ref, g_ref, c_ref, gl_ref, active_ref, first_ref, gh_ref, gc_ref,
    bank_ref, taps_ref, tile1_ref, tile2_ref,
):
    w0 = tap_rows(stencils_ref, 0)
    w1 = tap_rows(stencils_ref, 1)
    arrive(1)
    arrive(2)
    edge = edge_cells()

    def one(t, carry):
        x = tile_of(states_ref, t)
        bank_lines(bank_ref, t, tile_of(cot_ref, t), sel_ref)
        moved = dot(shift_ref[...], x)
        conv = conv_inner(moved[:CELLS], x.astype(F32), moved[CELLS:], w0)
        put_halves(tile1_ref, conv)
        keep_lines(back_ref, t + 2 * T, tile1_ref)
        first = conv.astype(BF16)
        put_tile(first_ref, t, first)
        leave(5, t * CELLS, CELLS)
        active, slope = activation(dot(first, mixers_ref[0]) + shifts_ref[0:1, :])
        put_tile(active_ref, t, jnp.where(edge, 0.0, active.astype(F32)).astype(BF16))
        leave(4, t * CELLS, CELLS)
        g = dot_t(tile_of(cot_ref, t), mixers_ref[1]).astype(BF16)
        put_tile(g_ref, t, g)
        leave(1, t * CELLS, CELLS)
        moved = dot(shift_ref[...], g)
        back = back_inner(moved[:CELLS], g.astype(F32), moved[CELLS:], w1)
        put_halves(tile2_ref, back)
        keep_lines(back_ref, t, tile2_ref)
        gh = jnp.where(edge, 0.0, back * slope).astype(BF16)
        put_tile(gh_ref, t, gh)
        leave(6, t * CELLS, CELLS)
        put_tile(gc_ref, t, dot_t(gh, mixers_ref[0]).astype(BF16))
        leave(7, t * CELLS, CELLS)
        return carry

    lax.fori_loop(0, T, one, 0)
    fill_tap_sets(taps_ref, stencils_ref, 1)
    live_lines(c_ref, 0, lambda i: bank_ref[tab_ref[5, i]], tab_ref, 0)
    leave(2, 0, 64)
    line_grads(gl_ref, c_ref, mixers_ref)
    leave(3, 0, 64)
    back_ref[2 * CELLS : 4 * CELLS] = jnp.zeros((2 * CELLS, 256), F32)
    rim_gradients(back_ref, 2 * CELLS, gl_ref, tab_ref, taps_ref, 0, 64)
    leave(0, 0, 6 * CELLS)


def middle_kernel(
    arrive, leave,
    tab_ref, in_ref, rims_in_ref, back_ref, mixers_ref, stencils_ref,
    shifts_ref, turn_ref, cross_ref,
    active_ref, first_ref, gh_ref, gc_ref, out_ref, c_ref, g_ref, panels_ref,
    rims_ref, lines_ref, split_ref, split2_ref, taps_ref,
):
    w0 = tap_rows(stencils_ref, 0)
    fill_tap_sets(taps_ref, stencils_ref, 1)
    live_lines(c_ref, 0, lambda i: in_ref[i, S : 2 * S], tab_ref, 64)
    leave(5, 0, 64)
    line_grads(g_ref, c_ref, mixers_ref)
    leave(6, 0, 64)
    arrive(2)
    forward_lines(split_ref, rims_in_ref, in_ref, tab_ref, w0, panels_ref)
    leave(7, 0, 64)
    arrive(3)
    rim_gradients(back_ref, 2 * CELLS, g_ref, tab_ref, taps_ref, 64, 64)
    split_rims(split2_ref, back_ref, 2 * CELLS)
    at = iota((CELLS, 1), 0)
    twice = (((at >> 4) & 1) == 1) & (((at & (S - 1)) == 0) | ((at & (S - 1)) == S - 1))

    def updates(ref, u):
        return jnp.concatenate([dot(cross_ref[...], ref[4 * u + q]) for q in range(4)], axis=0)

    for u in range(2):
        part = slice(u * CELLS, (u + 1) * CELLS)
        conv = back_ref[(u + 4) * CELLS : (u + 5) * CELLS]
        first = (conv + updates(split_ref, u)).astype(BF16)
        first_ref[part] = first
        active, slope = activation(dot(first, mixers_ref[0]) + shifts_ref[0:1, :])
        active_ref[part] = active
        grad = (back_ref[part] + updates(split2_ref, u)) * slope
        gh_ref[part] = jnp.where(twice, 0.0, grad).astype(BF16)
        gc = dot_t(grad.astype(BF16), mixers_ref[0]).astype(BF16)
        gc_ref[part] = gc
        for q in range(4):
            t = 4 * u + q
            rows = slice(64 * q, 64 * q + 64)
            edge_banks(rims_ref, lines_ref, t, active[rows], gc[rows], turn_ref)
        for k in range(4):
            leave(k, u * CELLS, CELLS)
    gather_out(leave, 4, out_ref, rims_ref, lines_ref, tab_ref)


def weight_kernel(
    arrive, leave,
    tab_ref, states_ref, cot_ref, active_ref, first_ref, gh_ref, gc_ref, g2_ref, panels_ref,
    c_own_ref, g_own_ref, c_in_ref, g_in_ref,
    active_edge_ref, first_edge_ref, gh_edge_ref, gc_edge_ref, stencils_ref, shift_ref, place_ref, turn_ref,
    pack_ref, conv_ref, gc_out_ref, rims_ref, lines_ref,
    second_ref, h_ref, taps_ref, acc1_ref, acc2_ref, accl_ref, sums_ref,
):
    w1 = tap_rows(stencils_ref, 1)
    acc1_ref[...] = jnp.zeros_like(acc1_ref)
    acc2_ref[...] = jnp.zeros_like(acc2_ref)
    accl_ref[...] = jnp.zeros_like(accl_ref)
    sums_ref[...] = jnp.zeros_like(sums_ref)
    fill_tap_sets(taps_ref, stencils_ref, 1)

    def folded(x):
        return jnp.sum(x.reshape(-1, 8, 256), axis=0)

    def taps_of(acc_ref, g, left, centre, right):
        for b, x in enumerate((left, centre, right)):
            acc_ref[b] += folded(g[S:] * x[: CELLS - S])
            acc_ref[3 + b] += folded(g * x)
            acc_ref[6 + b] += folded(g[: CELLS - S] * x[S:])

    def halves(x):
        return x[0:8] + x[8:16]

    def second_halo(source_ref):
        def one(i, carry):
            x = rims_ref[(tab_ref[2, i] >> 1) * 2].astype(F32)
            g = source_ref[i & 63].astype(F32)
            before, after = neighbours(x)
            kind = tab_ref[3, i]
            u = taps_ref[kind]
            h_ref[i] = (u[0:1] * before + u[1:2] * x + u[2:3] * after).astype(BF16)
            for m, y in enumerate((before, x, after)):
                accl_ref[kind, m] += halves(g * y)
            return carry

        return one

    arrive(13)
    arrive(16)
    for t in range(T):
        rows = slice(64 * t, 64 * t + 64)
        edge_banks(rims_ref, lines_ref, t, active_edge_ref[rows], gc_edge_ref[rows], turn_ref)
    leave(3, 0, 64)
    leave(4, 0, 128)
    arrive(10)
    lax.fori_loop(0, 64, second_halo(g_own_ref), 0, unroll=8)
    arrive(12)
    lax.fori_loop(64, 128, second_halo(g_in_ref), 0, unroll=8)

    for k in (8,):
        arrive(k)

    def first_halo(t, carry):
        for d in range(8):
            x = panels_ref[t * 8 + d].astype(F32)
            g = lines_ref[(t * 8 + d) * 2].astype(F32)
            if d < 4:
                before, after = neighbours(x)
                for k, y in zip(SIDE_TAPS[d], (before, x, after)):
                    acc1_ref[k] += halves(g * y)
            else:
                acc1_ref[CORNER_TAP[d]] += halves(g * x)
        return carry

    lax.fori_loop(0, T, first_halo, 0, unroll=2)

    for k in (6, 1, 3, 7, 5, 15, 2):
        arrive(k)

    def whole(inner_ref, edge_ref, t):
        edges = edge_ref[pl.ds(pl.multiple_of(t * 64, 64), 64), :]
        return tile_of(inner_ref, t).astype(F32) + dot(place_ref[...], edges)

    sums_ref[0] += folded(gh_edge_ref[...].astype(F32))

    def one(t, carry):
        gcf = whole(gc_ref, gc_edge_ref, t)
        put_tile(gc_out_ref, t, gcf.astype(BF16))
        leave(2, t * CELLS, CELLS)
        x = tile_of(states_ref, t)
        moved = dot(shift_ref[...], x)
        taps_of(acc1_ref, gcf, moved[:CELLS], x.astype(F32), moved[CELLS:])
        xf = whole(active_ref, active_edge_ref, t)
        moved = dot(shift_ref[...], xf.astype(BF16))
        second = conv_inner(moved[:CELLS], xf, moved[CELLS:], w1)
        put_tile(conv_ref, t, second)
        leave(1, t * CELLS, CELLS)
        put_tile(second_ref, t, second.astype(BF16))
        taps_of(acc2_ref, tile_of(g2_ref, t).astype(F32), moved[:CELLS], xf, moved[CELLS:])
        sums_ref[0] += folded(tile_of(gh_ref, t).astype(F32))
        sums_ref[1] += folded(tile_of(cot_ref, t).astype(F32))
        return carry

    lax.fori_loop(0, T, one, 0)
    for k in (4, 14, 9, 11):
        arrive(k)
    for d in range(8):
        for f in range(2):
            if d < 4:
                taps = SIDE_TAPS[d][::-1] if f else SIDE_TAPS[d]
                for m, k in enumerate(taps):
                    acc2_ref[k] += accl_ref[2 * d + f, m]
            else:
                acc2_ref[CORNER_TAP[d]] += accl_ref[2 * d + f, 1]

    rows = [jnp.sum(acc1_ref[k], axis=0, keepdims=True) for k in range(9)]
    rows += [jnp.sum(acc2_ref[k], axis=0, keepdims=True) for k in range(9)]
    rows += [jnp.sum(sums_ref[k], axis=0, keepdims=True) for k in range(2)]
    rows = [row[:, 128 * h : 128 * h + 128] for row in rows for h in range(2)]
    for r in range(5):
        pack_ref[r, 32:40] = jnp.concatenate(rows[8 * r : 8 * r + 8], axis=0).astype(BF16)
    for r in range(5, pack_ref.shape[0]):
        pack_ref[r, 32:40] = jnp.zeros((8, 128), BF16)
    half = pack_ref.shape[0] // 2

    def put_rows(r, rows16):
        for q in range(4):
            at = (q // 2) * 8, (q % 2) * 128
            pack_ref[r, 8 * q : 8 * q + 8] = rows16[at[0] : at[0] + 8, at[1] : at[1] + 128].astype(BF16)

    mixer_first = t_dot(first_ref[...], gh_ref[...]) + t_dot(first_edge_ref[...], gh_edge_ref[...])
    for r in range(half):
        put_rows(r, mixer_first[16 * r : 16 * r + 16])
    leave(0, 0, half)
    mixer_second = (
        t_dot(second_ref[...], cot_ref[...])
        + t_dot(h_ref[0:64].reshape(1024, 256), c_own_ref[...].reshape(1024, 256))
        + t_dot(h_ref[64:128].reshape(1024, 256), c_in_ref[...].reshape(1024, 256))
    )
    for r in range(half):
        put_rows(half + r, mixer_second[16 * r : 16 * r + 16])
    leave(0, half, half)


def outcome_kernel(
    arrive, leave,
    tab_ref, in_ref, rims_in_ref, bank_ref, conv_ref, states_ref, mixers_ref, stencils_ref, shifts_ref,
    spread_ref,
    outcome_ref, halo_ref,
    split_ref, rim_ref, taps_ref, lines_ref,
):
    w1 = tap_rows(stencils_ref, 1)
    arrive(2)
    arrive(1)
    forward_lines(split_ref, rims_in_ref, in_ref, tab_ref, w1)
    arrive(4)
    arrive(5)

    def one(t, carry):
        second = (tile_of(conv_ref, t) + dot(spread_ref[...], split_ref[t])).astype(BF16)
        out = tile_of(states_ref, t).astype(F32) + dot(second, mixers_ref[1]) + shifts_ref[1:2, :]
        put_tile(outcome_ref, t, out.astype(BF16))
        leave(0, t * CELLS, CELLS)
        return carry

    lax.fori_loop(0, T, one, 0, unroll=2)
    fill_tap_sets(taps_ref, stencils_ref, 0)
    rim_ref[...] = jnp.zeros_like(rim_ref)
    arrive(3)
    live_lines(lines_ref, 0, lambda i: bank_ref[tab_ref[5, i]], tab_ref, 0)
    live_lines(lines_ref, 64, lambda i: in_ref[i, S : 2 * S], tab_ref, 64)
    rim_gradients(rim_ref, 0, lines_ref, tab_ref, taps_ref, 0, 128)
    split_rims(halo_ref, rim_ref, 0)
    leave(1, 0, T)


def grad_kernel(
    arrive, leave,
    gc_ref, halo_ref, cot_ref, stencils_ref, shift_ref, spread_ref,
    grad_ref,
):
    w0 = tap_rows(stencils_ref, 0)
    for k in range(3):
        arrive(k)

    def one(t, carry):
        gc = tile_of(gc_ref, t)
        moved = dot(shift_ref[...], gc)
        grad = back_inner(moved[:CELLS], gc.astype(F32), moved[CELLS:], w0)
        grad = grad + dot(spread_ref[...], halo_ref[t]) + tile_of(cot_ref, t).astype(F32)
        put_tile(grad_ref, t, grad.astype(BF16))
        leave(0, t * CELLS, CELLS)
        return carry

    lax.fori_loop(0, T, one, 0)


def sum_kernel(arrive, leave, in_ref, out_ref):
    total = in_ref[0].astype(F32)
    for r in range(1, in_ref.shape[0]):
        total = total + in_ref[r].astype(F32)
    for r in range(out_ref.shape[0]):
        out_ref[r] = total.astype(BF16)


def spread_kernel(arrive, leave, in_ref, out_ref):
    total = in_ref[0].astype(F32)
    for r in range(1, in_ref.shape[0]):
        total = total + in_ref[r].astype(F32)
    value = total.astype(BF16)
    for r in range(out_ref.shape[0]):
        out_ref[r] = value


def unpack_kernel(scale, arrive, leave, in_ref, mixer_ref, stencil_ref, shift_ref):
    half = in_ref.shape[0] // 2
    for k in range(2):
        for r in range(half):
            for q in range(4):
                block = in_ref[k * half + r, 8 * q : 8 * q + 8].astype(F32) * scale
                row, col = 16 * r + (q // 2) * 8, (q % 2) * 128
                mixer_ref[k, row : row + 8, col : col + 128] = block
        leave(0, k, 1)
    rows = [in_ref[r, 32:40].astype(F32) * scale for r in range(5)]
    rows = [row for block in rows for row in jnp.split(block, 8, axis=0)]
    for k in range(2):
        for h in range(2):
            part = slice(128 * h, 128 * h + 128)
            for j in range(9):
                stencil_ref[j, k : k + 1, part] = rows[2 * (9 * k + j) + h]
            shift_ref[k : k + 1, part] = rows[2 * (18 + k) + h]


def shape_of(*dims, dtype=BF16):
    return jax.ShapeDtypeStruct(dims, dtype)


def call(body, ins, in_modes, outs, out_modes, scratch=(), limit=60.0, order=None):
    spaces = {"s": pltpu.SMEM, "v": pltpu.VMEM, "h": pltpu.HBM}
    ports_in = order or [k for k, mode in enumerate(in_modes) if mode == "h"]
    ports_out = [k for k, mode in enumerate(out_modes) if mode == "h"]
    n_in, n_out, n_own = len(ins), len(outs), len(scratch)

    def kernel(*refs):
        in_refs = list(refs[:n_in])
        out_refs = list(refs[n_in : n_in + n_out])
        rest = list(refs[n_in + n_out :])
        own, rest = rest[:n_own], rest[n_own:]
        sem_in, sem_out = rest[-2:]
        inward, outward = {}, {}
        for q, k in enumerate(ports_in):
            inward[k] = pltpu.make_async_copy(in_refs[k], rest[q], sem_in.at[q])
            inward[k].start()
            in_refs[k] = rest[q]
        for q, k in enumerate(ports_out):
            buffer = rest[len(ports_in) + q]
            outward[k] = (buffer, out_refs[k], sem_out.at[q])
            out_refs[k] = buffer

        def arrive(k):
            if k in inward:
                inward[k].wait()

        def leave(k, first, count):
            if k in outward:
                source, target, sem = outward[k]
                part = pl.ds(first, count)
                pltpu.make_async_copy(source.at[part], target.at[part], sem).start()

        body(arrive, leave, *in_refs, *out_refs, *own)
        for source, target, sem in outward.values():
            pltpu.make_async_copy(source, target, sem).wait()

    buffers = [pltpu.VMEM(ins[k].shape, ins[k].dtype) for k in ports_in]
    buffers += [pltpu.VMEM(outs[k].shape, outs[k].dtype) for k in ports_out]
    sems = [pltpu.SemaphoreType.DMA((max(1, len(p)),)) for p in (ports_in, ports_out)]
    return pl.pallas_call(
        kernel,
        out_shape=[
            pltpu.HBM(o.shape, o.dtype) if m == "h" else o for o, m in zip(outs, out_modes)
        ],
        in_specs=[pl.BlockSpec(memory_space=spaces[m]) for m in in_modes],
        out_specs=[pl.BlockSpec(memory_space=spaces[m]) for m in out_modes],
        scratch_shapes=list(scratch) + buffers + sems,
        compiler_params=pltpu.CompilerParams(vmem_limit_bytes=int(limit * 1024 * 1024)),
    )(*ins)


def exchange(array):
    return lax.all_to_all(array, TILE, split_axis=0, concat_axis=0, tiled=True)


def whole_block(states, cotangent, beside_slot, beside_code, mixers, stencils, shifts):
    groups = lax.axis_size(TILE)
    batch = lax.axis_size("batch")
    shape = states.shape
    x = states.reshape(T * CELLS, 256)
    cot = cotangent.reshape(T * CELLS, 256)
    sel = jnp.asarray(selection()[:128], BF16)
    spread = jnp.asarray(spreading(), BF16)
    shift = jnp.asarray(shifting(), BF16)
    taps = stencils.swapaxes(0, 1)
    lines16 = shape_of(128, S, 256)
    rims16 = shape_of(64, S, 256)
    sent16 = shape_of(64, 2 * S, 256)
    field = shape_of(T * CELLS, 256)
    wide = shape_of(T * CELLS, 256, dtype=F32)
    lines_scratch = pltpu.VMEM((128, S, 256), BF16)
    split_scratch = pltpu.VMEM((T, 128, 256), BF16)
    rim_scratch = pltpu.VMEM((2 * CELLS, 256), F32)
    taps_scratch = pltpu.VMEM((16, 3, 256), F32)
    rims_scratch = pltpu.VMEM((64, S, 256), BF16)
    tab, out1, rims1 = call(
        first_kernel,
        (beside_slot.astype(I32).T, beside_code.astype(I32).T, x, cot, sel),
        "vvhhv",
        [shape_of(8, 128, dtype=I32), sent16, rims16],
        "vhh",
        [
            lines_scratch,
            pltpu.VMEM((groups, 128), I32),
            pltpu.SMEM((8, 128), I32),
            pltpu.SemaphoreType.DMA,
        ],
    )
    in1 = exchange(out1.reshape(groups, 4 * S, 256)).reshape(64, 2 * S, 256)
    turn, cross, place = (jnp.asarray(m, BF16) for m in line_matrices())
    edge = shape_of(2 * CELLS, 256)
    tile_scratch = pltpu.VMEM((2, CELLS, 128), F32)
    back2, g2, c_own, g_own, active, first, gh, gc = call(
        inner_kernel,
        (tab, x, cot, mixers, taps, shifts, shift, sel),
        "shhvvvvv",
        [
            shape_of(6 * CELLS, 256, dtype=F32),
            field,
            rims16,
            rims16,
            field,
            field,
            field,
            field,
        ],
        "hhhhhhhh",
        [lines_scratch, taps_scratch, tile_scratch, tile_scratch],
    )
    active_e, first_e, gh_e, gc_e, out2, c_in, g_in, panels = call(
        middle_kernel,
        (tab, in1, rims1, back2, mixers, taps, shifts, turn, cross),
        "svhhvvvvv",
        [edge, edge, edge, edge, sent16, rims16, rims16, rims16],
        "hhhhhhhh",
        [rims_scratch, lines_scratch, split_scratch, split_scratch, taps_scratch],
        limit=51.0,
    )
    in2 = exchange(out2.reshape(groups, 4 * S, 256)).reshape(64, 2 * S, 256)
    pack, conv2, gc_all, rims2, lines2 = call(
        weight_kernel,
        (tab, x, cot, active, first, gh, gc, g2, panels, c_own, g_own, c_in, g_in,
         active_e, first_e, gh_e, gc_e, taps, shift, place, turn),
        "shhhhhhhhhhhhhhhhvvvv",
        [shape_of(groups, 40, 128), wide, field, rims16, lines16],
        "hhhhh",
        [
            pltpu.VMEM((T * CELLS, 256), BF16),
            lines_scratch,
            taps_scratch,
            pltpu.VMEM((9, 8, 256), F32),
            pltpu.VMEM((9, 8, 256), F32),
            pltpu.VMEM((16, 3, 8, 256), F32),
            pltpu.VMEM((2, 8, 256), F32),
        ],
        order=(13, 16, 10, 12, 8, 6, 1, 3, 7, 5, 15, 2, 4, 14, 9, 11),
    )
    parts = exchange(pack)
    outcome, halo = call(
        outcome_kernel,
        (tab, in2, rims2, lines2, conv2, x, mixers, taps, shifts, spread),
        "shhhhhvvvv",
        [field, shape_of(T, 128, 256)],
        "hh",
        [split_scratch, rim_scratch, taps_scratch, lines_scratch],
        order=(2, 1, 4, 5, 3),
    )
    (part,) = call(sum_kernel, (parts,), "v", [shape_of(batch, 40, 128)], "v", limit=4)
    part = lax.all_to_all(part, "batch", split_axis=0, concat_axis=0, tiled=True)
    (spread_out,) = call(spread_kernel, (part,), "v", [shape_of(groups, 40, 128)], "v", limit=4)
    whole = exchange(spread_out)
    (state_grad,) = call(
        grad_kernel, (gc_all, halo, cot, taps, shift, spread), "hhhvvv", [field], "h"
    )
    scale = 1.0 / math.sqrt(T * CELLS * groups * batch)

    def unpack(*refs):
        unpack_kernel(scale, *refs)

    mixer_grads, stencil_grads, shift_grads = call(
        unpack,
        (whole,),
        "v",
        [shape_of(2, 256, 256, dtype=F32), shape_of(9, 2, 256, dtype=F32), shape_of(2, 256, dtype=F32)],
        "hvv",
        limit=4,
    )
    stencil_grads = stencil_grads.swapaxes(0, 1)
    return (
        outcome.reshape(shape),
        state_grad.reshape(shape),
        mixer_grads,
        stencil_grads,
        shift_grads,
    )


def solution(mesh):
    torus = Mesh(
        mesh.devices.reshape(4, 4, 2, mesh.shape["batch"]), ("tile_0", "tile_1", "tile_2", "batch")
    )
    in_specs = (
        P("batch", TILE, None, None, None),
        P("batch", TILE, None, None, None),
        P(),
        P(),
        P(),
        P(),
        P(),
    )
    out_specs = (
        P("batch", TILE, None, None, None),
        P("batch", TILE, None, None, None),
        P(),
        P(),
        P(),
    )
    return jax.shard_map(
        whole_block, mesh=torus, in_specs=in_specs, out_specs=out_specs, check_vma=False
    )
```

```python
import math

import jax
import jax.numpy as jnp
import numpy as np
from jax import lax
from jax.experimental import pallas as pl
from jax.experimental.pallas import tpu as pltpu
from jax.sharding import Mesh
from jax.sharding import PartitionSpec as P


TILE = ("tile_0", "tile_1", "tile_2")
SQRT_HALF = 0.7071067811865476
INV_ROOT_TAU = 0.3989422804014327

F32 = jnp.float32
BF16 = jnp.bfloat16
I32 = jnp.int32

S = 16
T = 8
CELLS = S * S
SIDE_TAPS = {0: (0, 1, 2), 1: (2, 5, 8), 2: (6, 7, 8), 3: (0, 3, 6)}
CORNER_TAP = {4: 2, 5: 8, 6: 6, 7: 0}


def line_cell(d, i):
    if d == 0:
        return i
    if d == 1:
        return S * i + S - 1
    if d == 2:
        return S * (S - 1) + i
    if d == 3:
        return S * i
    if i != 0:
        return None
    return {4: S - 1, 5: CELLS - 1, 6: S * (S - 1), 7: 0}[d]


def selection():
    sel = np.zeros((256, CELLS), np.float32)
    for d in range(8):
        for f in range(2):
            for i in range(S):
                cell = line_cell(d, S - 1 - i if f else i)
                if cell is not None:
                    sel[(2 * d + f) * S + i, cell] = 1.0
    return sel


def spreading():
    out = np.zeros((CELLS, 128), np.float32)
    for d in range(4):
        for i in range(S):
            out[line_cell(d, i), d * S + i] = 1.0
            out[line_cell(d, i), 64 + d * S + i] = 1.0
    return out


def shifting():
    out = np.zeros((512, CELLS), np.float32)
    for i in range(S):
        for j in range(S):
            if j > 0:
                out[S * i + j, S * i + j - 1] = 1.0
            if j < S - 1:
                out[256 + S * i + j, S * i + j + 1] = 1.0
    return out


def line_matrices():
    sel = selection()
    lines = np.concatenate([sel[32 * d : 32 * d + S] for d in range(4)])
    turn = np.kron(np.eye(4), np.eye(S)[::-1]).astype(np.float32)
    place = np.zeros((CELLS, 64), np.float32)
    for cell in range(CELLS):
        at = np.flatnonzero(lines[:, cell])
        if at.size:
            home = [q for q in at if (q // S) % 2 == 0] or list(at)
            place[cell, home[0]] = 1.0
    return turn, lines @ spreading(), place


def dot(a, b):
    return jnp.dot(a, b, preferred_element_type=F32)


def dot_t(a, b):
    return lax.dot_general(a, b, (((1,), (1,)), ((), ())), preferred_element_type=F32)


def t_dot(a, b):
    return lax.dot_general(a, b, (((0,), (0,)), ((), ())), preferred_element_type=F32)


def iota(shape, axis):
    return lax.broadcasted_iota(I32, shape, axis)


def neighbours(x):
    place = iota(x.shape, 0)
    before = jnp.where(place == 0, 0.0, pltpu.roll(x, 1, 0))
    after = jnp.where(place == S - 1, 0.0, pltpu.roll(x, S - 1, 0))
    return before, after


def down(x):
    return jnp.concatenate([jnp.zeros((S, x.shape[1]), x.dtype), x[: CELLS - S]], axis=0)


def up(x):
    return jnp.concatenate([x[S:], jnp.zeros((S, x.shape[1]), x.dtype)], axis=0)


def conv_inner(left, centre, right, w):
    rows = [w[3 * a] * left + w[3 * a + 1] * centre + w[3 * a + 2] * right for a in range(3)]
    return rows[1] + down(rows[0]) + up(rows[2])


def back_inner(left, centre, right, w):
    rows = [w[3 * a] * right + w[3 * a + 1] * centre + w[3 * a + 2] * left for a in range(3)]
    return rows[1] + up(rows[0]) + down(rows[2])


def tap_rows(ref, layer):
    return [ref[k, layer : layer + 1, :] for k in range(9)]


def fill_tap_sets(taps_ref, stencil_ref, layer):
    w = tap_rows(stencil_ref, layer)
    zero = jnp.zeros_like(w[0])
    for d in range(8):
        if d < 4:
            three = [w[k] for k in SIDE_TAPS[d]]
        else:
            three = [zero, w[CORNER_TAP[d]], zero]
        for f in range(2):
            for m, row in enumerate(three[::-1] if f else three):
                taps_ref[2 * d + f, m : m + 1, :] = row


def tile_of(ref, t):
    return ref[pl.ds(pl.multiple_of(t * CELLS, CELLS), CELLS), :]


def put_tile(ref, t, value):
    ref[pl.ds(pl.multiple_of(t * CELLS, CELLS), CELLS), :] = value


def split_store(ref, t, first, value):
    high = value.astype(BF16)
    ref[t, pl.ds(first, value.shape[0]), :] = high
    ref[t, pl.ds(64 + first, value.shape[0]), :] = (value - high.astype(F32)).astype(BF16)


def forward_lines(split_ref, rims_ref, in_ref, tab_ref, w, panels_ref=None):
    def panel_of(k):
        place = tab_ref[0, k]
        own = rims_ref[jnp.minimum(place, 63)]
        sent = in_ref[jnp.maximum(place - 64, 0), 0:S]
        return jnp.where(place < 64, own, sent)

    def one(t, carry):
        corner = {}
        for d in range(4, 8):
            panel = panel_of(t * 8 + d)
            if panels_ref is not None:
                panels_ref[t * 8 + d] = panel
            row = panel[:8, :].astype(F32)[:1, :]
            corner[d] = w[CORNER_TAP[d]] * row
        for d in range(4):
            panel = panel_of(t * 8 + d)
            if panels_ref is not None:
                panels_ref[t * 8 + d] = panel
            x = panel.astype(F32)
            before, after = neighbours(x)
            a, b, c = SIDE_TAPS[d]
            line = w[a] * before + w[b] * x + w[c] * after
            at = iota(line.shape, 0)
            if d == 0:
                line = line + jnp.where(at == 0, corner[7], 0.0)
                line = line + jnp.where(at == S - 1, corner[4], 0.0)
            if d == 2:
                line = line + jnp.where(at == 0, corner[6], 0.0)
                line = line + jnp.where(at == S - 1, corner[5], 0.0)
            split_store(split_ref, t, d * S, line)
        return carry

    lax.fori_loop(0, T, one, 0, unroll=4)


def rim_rows_at(base, rim):
    return pl.ds(pl.multiple_of(base + rim * S, S), S)


def rim_gradients(rim_ref, base, lines_ref, tab_ref, taps_ref, first, count):
    def one(i, carry):
        x = lines_ref[i].astype(F32)
        before, after = neighbours(x)
        u = taps_ref[tab_ref[3, first + i]]
        rim = tab_ref[2, first + i] >> 1
        rim_ref[rim_rows_at(base, rim)] += u[0:1] * after + u[1:2] * x + u[2:3] * before
        return carry

    lax.fori_loop(0, count, one, 0, unroll=16)


def split_rims(split_ref, rim_ref, base):
    def split(t, carry):
        for e in range(4):
            split_store(split_ref, t, e * S, rim_ref[rim_rows_at(base, t * 4 + e)])
        return carry

    lax.fori_loop(0, T, split, 0, unroll=4)


def live_lines(dst_ref, dst_first, line_of, tab_ref, tab_first):
    def one(i, carry):
        live = tab_ref[4, tab_first + i] > 0
        dst_ref[dst_first + i] = jnp.where(live, line_of(i), jnp.zeros((S, 256), BF16))
        return carry

    lax.fori_loop(0, 64, one, 0, unroll=16)


def line_grads(g_ref, c_ref, mixers_ref):
    for b in range(4):
        part = c_ref[b * 16 : b * 16 + 16].reshape(256, 256)
        g_ref[b * 16 : b * 16 + 16] = dot_t(part, mixers_ref[1]).astype(BF16).reshape(16, S, 256)


def gather_out(leave, port, out_ref, rims_ref, lines_ref, tab_ref):
    def some(q, carry):
        for r in range(8):
            s = q * 8 + r
            out_ref[s, 0:S] = rims_ref[tab_ref[2, 64 + s]]
            out_ref[s, S : 2 * S] = lines_ref[tab_ref[1, s]]
        leave(port, q * 8, 8)
        return carry

    lax.fori_loop(0, 8, some, 0)


CORNER_SOURCE = {4: (0, 1), 5: (2, 1), 6: (2, 0), 7: (0, 0)}


def put_corners(lines_ref, t, sides):
    at = iota((S, 1), 0)
    for d, (side, flip) in CORNER_SOURCE.items():
        for f in range(2):
            value = jnp.where(at == (S - 1 if f else 0), sides[side][flip ^ f], 0.0)
            lines_ref[16 * t + 2 * d + f] = value.astype(BF16)


def bank_rims(rims_ref, t, tile, sel_ref):
    rims = dot(sel_ref[...], tile).astype(BF16)
    rims_ref[pl.ds(t * 8, 8)] = rims.reshape(8, S, 256)


def bank_lines(lines_ref, t, tile, sel_ref):
    lines = dot(sel_ref[...], tile)
    lines_ref[pl.ds(t * 16, 8)] = lines.astype(BF16).reshape(8, S, 256)
    groups = [lines[S * k : S * k + S] for k in range(8)]
    put_corners(lines_ref, t, [groups[2 * d : 2 * d + 2] for d in range(4)])


def edge_banks(rims_ref, lines_ref, t, active, gc, turn_ref):
    turned = dot(turn_ref[...], active).astype(BF16)
    back = dot(turn_ref[...], gc)
    sides = []
    for d in range(4):
        part = slice(S * d, S * d + S)
        rims_ref[8 * t + 2 * d] = active[part]
        rims_ref[8 * t + 2 * d + 1] = turned[part]
        lines_ref[16 * t + 2 * d] = gc[part]
        lines_ref[16 * t + 2 * d + 1] = back[part].astype(BF16)
        sides.append((gc[part].astype(F32), back[part]))
    put_corners(lines_ref, t, sides)


def own_position():
    a, b, c = (lax.axis_index(name) for name in TILE)
    return (a * lax.axis_size(TILE[1]) + b) * lax.axis_size(TILE[2]) + c


def first_kernel(
    arrive, leave, slot_ref, code_ref, states_ref, cot_ref, sel_ref, tab_ref, out_ref, rims_ref,
    lines_ref, comb_ref, smem, sem,
):
    me = own_position()
    entries = slot_ref.shape[1]
    groups = entries // T
    sub = iota((128, entries), 0)
    tile = iota((128, entries), 1)
    belongs = (tile & (T - 1)) == (sub >> 3)
    member = (iota((groups, entries), 0) == (iota((groups, entries), 1) >> 3)).astype(F32).astype(BF16)

    def by_block(ref):
        copies = jnp.concatenate([ref[...].astype(F32)] * 16, axis=0)
        return dot_t(member, jnp.where(belongs, copies, 0.0).astype(BF16)).astype(I32)

    comb = by_block(slot_ref) * 8 + by_block(code_ref)
    comb_ref[...] = comb
    lane = iota(comb.shape, 1)
    home = iota(comb.shape, 0)
    slot = comb >> 3
    wanted = (lane < 64) & ((slot >> 3) == me) & (home != me)
    wanted_f = wanted.astype(F32)
    before = (iota((128, 128), 0) < iota((128, 128), 1)).astype(F32).astype(BF16)
    place = dot(wanted_f.astype(BF16), before)
    code = comb & 7
    rim_code = (slot & 7) * 8 + code
    tap_set = (lane & 7) * 2 + (code & 1)
    packed = (rim_code * 16 + tap_set + 1024).astype(F32)
    asked = jnp.zeros((1, 128), F32)
    for k in range(2):
        value = jnp.sum(
            jnp.where(wanted & (place == k), packed, 0.0), axis=1, keepdims=True
        )
        at = (lane >= 64) & (((lane - 64) >> 1) == home) & ((lane & 1) == k)
        asked = asked + jnp.sum(jnp.where(at, value, 0.0), axis=0, keepdims=True)
    asked = asked.astype(I32)

    own = comb_ref[pl.ds(me, 1), :]
    sub2 = iota((128, 128), 0)
    lane2 = iota((128, 128), 1)
    own_wide = jnp.broadcast_to(own, (128, 128))
    own_col = jnp.sum(
        jnp.where(sub2 == lane2, own_wide, 0).astype(F32), axis=1, keepdims=True
    ).astype(I32)
    owner_col = own_col >> 6
    owner_row = own >> 6
    same = (owner_col == owner_row) & (sub2 < 64) & (lane2 < 64)
    place_col = jnp.sum((same & (lane2 < sub2)).astype(F32), axis=1, keepdims=True).astype(I32)
    place_row = jnp.sum((same & (sub2 < lane2)).astype(F32), axis=0, keepdims=True).astype(I32)
    lane1 = iota((1, 128), 1)
    sub1 = iota((128, 1), 0)
    remote_row = owner_row != me
    slot_col = jnp.where((owner_col != me) & (sub1 < 64), owner_col * 2 + place_col, -1)
    line_col = (sub1 * 2 + (own_col & 1)).astype(F32)
    sent = jnp.sum(jnp.where(slot_col == lane2, line_col, 0.0), axis=0, keepdims=True).astype(I32)
    own_rim = (own & 511)
    own_rim = ((own_rim >> 3) & 7) * 8 + (own_rim & 7)
    in_own = lane1 < 64
    panel = jnp.where(remote_row, 64 + owner_row * 2 + place_row, own_rim)
    tab_ref[...] = jnp.zeros_like(tab_ref)
    tab_ref[0:1, :] = jnp.where(in_own, panel, 0)
    tab_ref[1:2, :] = jnp.where(in_own, sent, 0)
    tab_ref[2:3, :] = jnp.where(in_own, own_rim, (asked & 1023) >> 4)
    tab_ref[3:4, :] = jnp.where(in_own, (lane1 & 7) * 2 + (own & 1), asked & 15)
    tab_ref[4:5, :] = jnp.where(in_own, (~remote_row).astype(I32), asked >> 10)
    tab_ref[5:6, :] = jnp.where(in_own, lane1 * 2 + (own & 1), 0)
    copy = pltpu.make_async_copy(tab_ref, smem, sem)
    copy.start()
    arrive(2)
    for t in range(T):
        bank_rims(rims_ref, t, tile_of(states_ref, t), sel_ref)
    leave(2, 0, 64)
    arrive(3)
    for t in range(T):
        bank_lines(lines_ref, t, tile_of(cot_ref, t), sel_ref)
    copy.wait()
    gather_out(leave, 1, out_ref, rims_ref, lines_ref, smem)


def edge_cells():
    row = iota((CELLS, 1), 0)
    i, j = row >> 4, row & (S - 1)
    return (i == 0) | (i == S - 1) | (j == 0) | (j == S - 1)


def keep_lines(lines_ref, t, tile_ref):
    at = [pl.ds(0, S), pl.ds(S - 1, S, stride=S), pl.ds(S * (S - 1), S), pl.ds(0, S, stride=S)]
    for d in range(4):
        for h in range(2):
            lines_ref[pl.ds(pl.multiple_of(t * 64 + d * S, S), S), 128 * h : 128 * h + 128] = tile_ref[
                h, at[d], :
            ]


def put_halves(tile_ref, value):
    tile_ref[0] = value[:, 0:128]
    tile_ref[1] = value[:, 128:256]


def activation(hidden):
    cdf = 0.5 * (1.0 + lax.erf(hidden * SQRT_HALF))
    slope = cdf + hidden * jnp.exp(-0.5 * hidden * hidden) * INV_ROOT_TAU
    return (hidden * cdf).astype(BF16), slope


def inner_kernel(
    arrive, leave, tab_ref, states_ref, cot_ref, mixers_ref, stencils_ref, shifts_ref, shift_ref, sel_ref,
    back_ref, g_ref, c_ref, gl_ref, active_ref, first_ref, gh_ref, gc_ref,
    bank_ref, taps_ref, tile1_ref, tile2_ref,
):
    w0 = tap_rows(stencils_ref, 0)
    w1 = tap_rows(stencils_ref, 1)
    arrive(1)
    arrive(2)
    edge = edge_cells()

    def one(t, carry):
        x = tile_of(states_ref, t)
        bank_lines(bank_ref, t, tile_of(cot_ref, t), sel_ref)
        moved = dot(shift_ref[...], x)
        conv = conv_inner(moved[:CELLS], x.astype(F32), moved[CELLS:], w0)
        put_halves(tile1_ref, conv)
        keep_lines(back_ref, t + 2 * T, tile1_ref)
        first = conv.astype(BF16)
        put_tile(first_ref, t, first)
        leave(5, t * CELLS, CELLS)
        active, slope = activation(dot(first, mixers_ref[0]) + shifts_ref[0:1, :])
        put_tile(active_ref, t, jnp.where(edge, 0.0, active.astype(F32)).astype(BF16))
        leave(4, t * CELLS, CELLS)
        g = dot_t(tile_of(cot_ref, t), mixers_ref[1]).astype(BF16)
        put_tile(g_ref, t, g)
        leave(1, t * CELLS, CELLS)
        moved = dot(shift_ref[...], g)
        back = back_inner(moved[:CELLS], g.astype(F32), moved[CELLS:], w1)
        put_halves(tile2_ref, back)
        keep_lines(back_ref, t, tile2_ref)
        gh = jnp.where(edge, 0.0, back * slope).astype(BF16)
        put_tile(gh_ref, t, gh)
        leave(6, t * CELLS, CELLS)
        put_tile(gc_ref, t, dot_t(gh, mixers_ref[0]).astype(BF16))
        leave(7, t * CELLS, CELLS)
        return carry

    lax.fori_loop(0, T, one, 0)
    fill_tap_sets(taps_ref, stencils_ref, 1)
    live_lines(c_ref, 0, lambda i: bank_ref[tab_ref[5, i]], tab_ref, 0)
    leave(2, 0, 64)
    line_grads(gl_ref, c_ref, mixers_ref)
    leave(3, 0, 64)
    back_ref[2 * CELLS : 4 * CELLS] = jnp.zeros((2 * CELLS, 256), F32)
    rim_gradients(back_ref, 2 * CELLS, gl_ref, tab_ref, taps_ref, 0, 64)
    leave(0, 0, 6 * CELLS)


def middle_kernel(
    arrive, leave,
    tab_ref, in_ref, rims_in_ref, back_ref, mixers_ref, stencils_ref,
    shifts_ref, turn_ref, cross_ref,
    active_ref, first_ref, gh_ref, gc_ref, out_ref, c_ref, g_ref, panels_ref,
    rims_ref, lines_ref, split_ref, split2_ref, taps_ref,
):
    w0 = tap_rows(stencils_ref, 0)
    fill_tap_sets(taps_ref, stencils_ref, 1)
    live_lines(c_ref, 0, lambda i: in_ref[i, S : 2 * S], tab_ref, 64)
    leave(5, 0, 64)
    line_grads(g_ref, c_ref, mixers_ref)
    leave(6, 0, 64)
    arrive(2)
    forward_lines(split_ref, rims_in_ref, in_ref, tab_ref, w0, panels_ref)
    leave(7, 0, 64)
    arrive(3)
    rim_gradients(back_ref, 2 * CELLS, g_ref, tab_ref, taps_ref, 64, 64)
    split_rims(split2_ref, back_ref, 2 * CELLS)
    at = iota((CELLS, 1), 0)
    twice = (((at >> 4) & 1) == 1) & (((at & (S - 1)) == 0) | ((at & (S - 1)) == S - 1))

    def updates(ref, u):
        return jnp.concatenate([dot(cross_ref[...], ref[4 * u + q]) for q in range(4)], axis=0)

    for u in range(2):
        part = slice(u * CELLS, (u + 1) * CELLS)
        conv = back_ref[(u + 4) * CELLS : (u + 5) * CELLS]
        first = (conv + updates(split_ref, u)).astype(BF16)
        first_ref[part] = first
        active, slope = activation(dot(first, mixers_ref[0]) + shifts_ref[0:1, :])
        active_ref[part] = active
        grad = (back_ref[part] + updates(split2_ref, u)) * slope
        gh_ref[part] = jnp.where(twice, 0.0, grad).astype(BF16)
        gc = dot_t(grad.astype(BF16), mixers_ref[0]).astype(BF16)
        gc_ref[part] = gc
        for q in range(4):
            t = 4 * u + q
            rows = slice(64 * q, 64 * q + 64)
            edge_banks(rims_ref, lines_ref, t, active[rows], gc[rows], turn_ref)
        for k in range(4):
            leave(k, u * CELLS, CELLS)
    gather_out(leave, 4, out_ref, rims_ref, lines_ref, tab_ref)


def weight_kernel(
    arrive, leave,
    tab_ref, states_ref, cot_ref, active_ref, first_ref, gh_ref, gc_ref, g2_ref, panels_ref,
    c_own_ref, g_own_ref, c_in_ref, g_in_ref,
    active_edge_ref, first_edge_ref, gh_edge_ref, gc_edge_ref, stencils_ref, shift_ref, place_ref, turn_ref,
    pack_ref, conv_ref, gc_out_ref, rims_ref, lines_ref,
    second_ref, h_ref, taps_ref, acc1_ref, acc2_ref, accl_ref, sums_ref,
):
    w1 = tap_rows(stencils_ref, 1)
    acc1_ref[...] = jnp.zeros_like(acc1_ref)
    acc2_ref[...] = jnp.zeros_like(acc2_ref)
    accl_ref[...] = jnp.zeros_like(accl_ref)
    sums_ref[...] = jnp.zeros_like(sums_ref)
    fill_tap_sets(taps_ref, stencils_ref, 1)

    def folded(x):
        return jnp.sum(x.reshape(-1, 8, 256), axis=0)

    def taps_of(acc_ref, g, left, centre, right):
        for b, x in enumerate((left, centre, right)):
            acc_ref[b] += folded(g[S:] * x[: CELLS - S])
            acc_ref[3 + b] += folded(g * x)
            acc_ref[6 + b] += folded(g[: CELLS - S] * x[S:])

    def halves(x):
        return x[0:8] + x[8:16]

    def second_halo(source_ref):
        def one(i, carry):
            x = rims_ref[(tab_ref[2, i] >> 1) * 2].astype(F32)
            g = source_ref[i & 63].astype(F32)
            before, after = neighbours(x)
            kind = tab_ref[3, i]
            u = taps_ref[kind]
            h_ref[i] = (u[0:1] * before + u[1:2] * x + u[2:3] * after).astype(BF16)
            for m, y in enumerate((before, x, after)):
                accl_ref[kind, m] += halves(g * y)
            return carry

        return one

    arrive(13)
    arrive(16)
    for t in range(T):
        rows = slice(64 * t, 64 * t + 64)
        edge_banks(rims_ref, lines_ref, t, active_edge_ref[rows], gc_edge_ref[rows], turn_ref)
    leave(3, 0, 64)
    leave(4, 0, 128)
    arrive(10)
    lax.fori_loop(0, 64, second_halo(g_own_ref), 0, unroll=8)
    arrive(12)
    lax.fori_loop(64, 128, second_halo(g_in_ref), 0, unroll=8)

    for k in (8,):
        arrive(k)

    def first_halo(t, carry):
        for d in range(8):
            x = panels_ref[t * 8 + d].astype(F32)
            g = lines_ref[(t * 8 + d) * 2].astype(F32)
            if d < 4:
                before, after = neighbours(x)
                for k, y in zip(SIDE_TAPS[d], (before, x, after)):
                    acc1_ref[k] += halves(g * y)
            else:
                acc1_ref[CORNER_TAP[d]] += halves(g * x)
        return carry

    lax.fori_loop(0, T, first_halo, 0, unroll=2)

    for k in (6, 1, 3, 7, 5, 15, 2):
        arrive(k)

    def whole(inner_ref, edge_ref, t):
        edges = edge_ref[pl.ds(pl.multiple_of(t * 64, 64), 64), :]
        return tile_of(inner_ref, t).astype(F32) + dot(place_ref[...], edges)

    sums_ref[0] += folded(gh_edge_ref[...].astype(F32))

    def one(t, carry):
        gcf = whole(gc_ref, gc_edge_ref, t)
        put_tile(gc_out_ref, t, gcf.astype(BF16))
        leave(2, t * CELLS, CELLS)
        x = tile_of(states_ref, t)
        moved = dot(shift_ref[...], x)
        taps_of(acc1_ref, gcf, moved[:CELLS], x.astype(F32), moved[CELLS:])
        xf = whole(active_ref, active_edge_ref, t)
        moved = dot(shift_ref[...], xf.astype(BF16))
        second = conv_inner(moved[:CELLS], xf, moved[CELLS:], w1)
        put_tile(conv_ref, t, second)
        leave(1, t * CELLS, CELLS)
        put_tile(second_ref, t, second.astype(BF16))
        taps_of(acc2_ref, tile_of(g2_ref, t).astype(F32), moved[:CELLS], xf, moved[CELLS:])
        sums_ref[0] += folded(tile_of(gh_ref, t).astype(F32))
        sums_ref[1] += folded(tile_of(cot_ref, t).astype(F32))
        return carry

    lax.fori_loop(0, T, one, 0)
    for k in (4, 14, 9, 11):
        arrive(k)
    for d in range(8):
        for f in range(2):
            if d < 4:
                taps = SIDE_TAPS[d][::-1] if f else SIDE_TAPS[d]
                for m, k in enumerate(taps):
                    acc2_ref[k] += accl_ref[2 * d + f, m]
            else:
                acc2_ref[CORNER_TAP[d]] += accl_ref[2 * d + f, 1]

    rows = [jnp.sum(acc1_ref[k], axis=0, keepdims=True) for k in range(9)]
    rows += [jnp.sum(acc2_ref[k], axis=0, keepdims=True) for k in range(9)]
    rows += [jnp.sum(sums_ref[k], axis=0, keepdims=True) for k in range(2)]
    rows = [row[:, 128 * h : 128 * h + 128] for row in rows for h in range(2)]
    for r in range(5):
        pack_ref[r, 32:40] = jnp.concatenate(rows[8 * r : 8 * r + 8], axis=0).astype(BF16)
    for r in range(5, pack_ref.shape[0]):
        pack_ref[r, 32:40] = jnp.zeros((8, 128), BF16)
    half = pack_ref.shape[0] // 2

    def put_rows(r, rows16):
        for q in range(4):
            at = (q // 2) * 8, (q % 2) * 128
            pack_ref[r, 8 * q : 8 * q + 8] = rows16[at[0] : at[0] + 8, at[1] : at[1] + 128].astype(BF16)

    mixer_first = t_dot(first_ref[...], gh_ref[...]) + t_dot(first_edge_ref[...], gh_edge_ref[...])
    for r in range(half):
        put_rows(r, mixer_first[16 * r : 16 * r + 16])
    leave(0, 0, half)
    mixer_second = (
        t_dot(second_ref[...], cot_ref[...])
        + t_dot(h_ref[0:64].reshape(1024, 256), c_own_ref[...].reshape(1024, 256))
        + t_dot(h_ref[64:128].reshape(1024, 256), c_in_ref[...].reshape(1024, 256))
    )
    for r in range(half):
        put_rows(half + r, mixer_second[16 * r : 16 * r + 16])
    leave(0, half, half)


def outcome_kernel(
    arrive, leave,
    tab_ref, in_ref, rims_in_ref, bank_ref, conv_ref, states_ref, mixers_ref, stencils_ref, shifts_ref,
    spread_ref,
    outcome_ref, halo_ref,
    split_ref, rim_ref, taps_ref, lines_ref,
):
    w1 = tap_rows(stencils_ref, 1)
    arrive(2)
    arrive(1)
    forward_lines(split_ref, rims_in_ref, in_ref, tab_ref, w1)
    arrive(4)
    arrive(5)

    def one(t, carry):
        second = (tile_of(conv_ref, t) + dot(spread_ref[...], split_ref[t])).astype(BF16)
        out = tile_of(states_ref, t).astype(F32) + dot(second, mixers_ref[1]) + shifts_ref[1:2, :]
        put_tile(outcome_ref, t, out.astype(BF16))
        leave(0, t * CELLS, CELLS)
        return carry

    lax.fori_loop(0, T, one, 0, unroll=2)
    fill_tap_sets(taps_ref, stencils_ref, 0)
    rim_ref[...] = jnp.zeros_like(rim_ref)
    arrive(3)
    live_lines(lines_ref, 0, lambda i: bank_ref[tab_ref[5, i]], tab_ref, 0)
    live_lines(lines_ref, 64, lambda i: in_ref[i, S : 2 * S], tab_ref, 64)
    rim_gradients(rim_ref, 0, lines_ref, tab_ref, taps_ref, 0, 128)
    split_rims(halo_ref, rim_ref, 0)
    leave(1, 0, T)


def grad_kernel(
    arrive, leave,
    gc_ref, halo_ref, cot_ref, stencils_ref, shift_ref, spread_ref,
    grad_ref,
):
    w0 = tap_rows(stencils_ref, 0)
    for k in range(3):
        arrive(k)

    def one(t, carry):
        gc = tile_of(gc_ref, t)
        moved = dot(shift_ref[...], gc)
        grad = back_inner(moved[:CELLS], gc.astype(F32), moved[CELLS:], w0)
        grad = grad + dot(spread_ref[...], halo_ref[t]) + tile_of(cot_ref, t).astype(F32)
        put_tile(grad_ref, t, grad.astype(BF16))
        leave(0, t * CELLS, CELLS)
        return carry

    lax.fori_loop(0, T, one, 0)


def sum_kernel(arrive, leave, in_ref, out_ref):
    total = in_ref[0].astype(F32)
    for r in range(1, in_ref.shape[0]):
        total = total + in_ref[r].astype(F32)
    for r in range(out_ref.shape[0]):
        out_ref[r] = total.astype(BF16)


def spread_kernel(arrive, leave, in_ref, out_ref):
    total = in_ref[0].astype(F32)
    for r in range(1, in_ref.shape[0]):
        total = total + in_ref[r].astype(F32)
    value = total.astype(BF16)
    for r in range(out_ref.shape[0]):
        out_ref[r] = value


def unpack_kernel(scale, arrive, leave, in_ref, mixer_ref, stencil_ref, shift_ref):
    half = in_ref.shape[0] // 2
    for k in range(2):
        for r in range(half):
            for q in range(4):
                block = in_ref[k * half + r, 8 * q : 8 * q + 8].astype(F32) * scale
                row, col = 16 * r + (q // 2) * 8, (q % 2) * 128
                mixer_ref[k, row : row + 8, col : col + 128] = block
        leave(0, k, 1)
    rows = [in_ref[r, 32:40].astype(F32) * scale for r in range(5)]
    rows = [row for block in rows for row in jnp.split(block, 8, axis=0)]
    for k in range(2):
        for h in range(2):
            part = slice(128 * h, 128 * h + 128)
            for j in range(9):
                stencil_ref[j, k : k + 1, part] = rows[2 * (9 * k + j) + h]
            shift_ref[k : k + 1, part] = rows[2 * (18 + k) + h]


def shape_of(*dims, dtype=BF16):
    return jax.ShapeDtypeStruct(dims, dtype)


def call(body, ins, in_modes, outs, out_modes, scratch=(), limit=60.0, order=None):
    spaces = {"s": pltpu.SMEM, "v": pltpu.VMEM, "h": pltpu.HBM}
    ports_in = order or [k for k, mode in enumerate(in_modes) if mode == "h"]
    ports_out = [k for k, mode in enumerate(out_modes) if mode == "h"]
    n_in, n_out, n_own = len(ins), len(outs), len(scratch)

    def kernel(*refs):
        in_refs = list(refs[:n_in])
        out_refs = list(refs[n_in : n_in + n_out])
        rest = list(refs[n_in + n_out :])
        own, rest = rest[:n_own], rest[n_own:]
        sem_in, sem_out = rest[-2:]
        inward, outward = {}, {}
        for q, k in enumerate(ports_in):
            inward[k] = pltpu.make_async_copy(in_refs[k], rest[q], sem_in.at[q])
            inward[k].start()
            in_refs[k] = rest[q]
        for q, k in enumerate(ports_out):
            buffer = rest[len(ports_in) + q]
            outward[k] = (buffer, out_refs[k], sem_out.at[q])
            out_refs[k] = buffer

        def arrive(k):
            if k in inward:
                inward[k].wait()

        def leave(k, first, count):
            if k in outward:
                source, target, sem = outward[k]
                part = pl.ds(first, count)
                pltpu.make_async_copy(source.at[part], target.at[part], sem).start()

        body(arrive, leave, *in_refs, *out_refs, *own)
        for source, target, sem in outward.values():
            pltpu.make_async_copy(source, target, sem).wait()

    buffers = [pltpu.VMEM(ins[k].shape, ins[k].dtype) for k in ports_in]
    buffers += [pltpu.VMEM(outs[k].shape, outs[k].dtype) for k in ports_out]
    sems = [pltpu.SemaphoreType.DMA((max(1, len(p)),)) for p in (ports_in, ports_out)]
    return pl.pallas_call(
        kernel,
        out_shape=[
            pltpu.HBM(o.shape, o.dtype) if m == "h" else o for o, m in zip(outs, out_modes)
        ],
        in_specs=[pl.BlockSpec(memory_space=spaces[m]) for m in in_modes],
        out_specs=[pl.BlockSpec(memory_space=spaces[m]) for m in out_modes],
        scratch_shapes=list(scratch) + buffers + sems,
        compiler_params=pltpu.CompilerParams(vmem_limit_bytes=int(limit * 1024 * 1024)),
    )(*ins)


def exchange(array):
    return lax.all_to_all(array, TILE, split_axis=0, concat_axis=0, tiled=True)


def whole_block(states, cotangent, beside_slot, beside_code, mixers, stencils, shifts):
    groups = lax.axis_size(TILE)
    batch = lax.axis_size("batch")
    shape = states.shape
    x = states.reshape(T * CELLS, 256)
    cot = cotangent.reshape(T * CELLS, 256)
    sel = jnp.asarray(selection()[:128], BF16)
    spread = jnp.asarray(spreading(), BF16)
    shift = jnp.asarray(shifting(), BF16)
    taps = stencils.swapaxes(0, 1)
    lines16 = shape_of(128, S, 256)
    rims16 = shape_of(64, S, 256)
    sent16 = shape_of(64, 2 * S, 256)
    field = shape_of(T * CELLS, 256)
    wide = shape_of(T * CELLS, 256, dtype=F32)
    lines_scratch = pltpu.VMEM((128, S, 256), BF16)
    split_scratch = pltpu.VMEM((T, 128, 256), BF16)
    rim_scratch = pltpu.VMEM((2 * CELLS, 256), F32)
    taps_scratch = pltpu.VMEM((16, 3, 256), F32)
    rims_scratch = pltpu.VMEM((64, S, 256), BF16)
    tab, out1, rims1 = call(
        first_kernel,
        (beside_slot.astype(I32).T, beside_code.astype(I32).T, x, cot, sel),
        "vvhhv",
        [shape_of(8, 128, dtype=I32), sent16, rims16],
        "vhh",
        [
            lines_scratch,
            pltpu.VMEM((groups, 128), I32),
            pltpu.SMEM((8, 128), I32),
            pltpu.SemaphoreType.DMA,
        ],
    )
    in1 = exchange(out1.reshape(groups, 4 * S, 256)).reshape(64, 2 * S, 256)
    turn, cross, place = (jnp.asarray(m, BF16) for m in line_matrices())
    edge = shape_of(2 * CELLS, 256)
    tile_scratch = pltpu.VMEM((2, CELLS, 128), F32)
    back2, g2, c_own, g_own, active, first, gh, gc = call(
        inner_kernel,
        (tab, x, cot, mixers, taps, shifts, shift, sel),
        "shhvvvvv",
        [
            shape_of(6 * CELLS, 256, dtype=F32),
            field,
            rims16,
            rims16,
            field,
            field,
            field,
            field,
        ],
        "hhhhhhhh",
        [lines_scratch, taps_scratch, tile_scratch, tile_scratch],
    )
    active_e, first_e, gh_e, gc_e, out2, c_in, g_in, panels = call(
        middle_kernel,
        (tab, in1, rims1, back2, mixers, taps, shifts, turn, cross),
        "svhhvvvvv",
        [edge, edge, edge, edge, sent16, rims16, rims16, rims16],
        "hhhhhhhh",
        [rims_scratch, lines_scratch, split_scratch, split_scratch, taps_scratch],
        limit=51.0,
    )
    in2 = exchange(out2.reshape(groups, 4 * S, 256)).reshape(64, 2 * S, 256)
    pack, conv2, gc_all, rims2, lines2 = call(
        weight_kernel,
        (tab, x, cot, active, first, gh, gc, g2, panels, c_own, g_own, c_in, g_in,
         active_e, first_e, gh_e, gc_e, taps, shift, place, turn),
        "shhhhhhhhhhhhhhhhvvvv",
        [shape_of(groups, 40, 128), wide, field, rims16, lines16],
        "hhhhh",
        [
            pltpu.VMEM((T * CELLS, 256), BF16),
            lines_scratch,
            taps_scratch,
            pltpu.VMEM((9, 8, 256), F32),
            pltpu.VMEM((9, 8, 256), F32),
            pltpu.VMEM((16, 3, 8, 256), F32),
            pltpu.VMEM((2, 8, 256), F32),
        ],
        order=(13, 16, 10, 12, 8, 6, 1, 3, 7, 5, 15, 2, 4, 14, 9, 11),
    )
    parts = exchange(pack)
    outcome, halo = call(
        outcome_kernel,
        (tab, in2, rims2, lines2, conv2, x, mixers, taps, shifts, spread),
        "shhhhhvvvv",
        [field, shape_of(T, 128, 256)],
        "hh",
        [split_scratch, rim_scratch, taps_scratch, lines_scratch],
        order=(2, 1, 4, 5, 3),
    )
    (part,) = call(sum_kernel, (parts,), "v", [shape_of(batch, 40, 128)], "v", limit=4)
    part = lax.all_to_all(part, "batch", split_axis=0, concat_axis=0, tiled=True)
    (spread_out,) = call(spread_kernel, (part,), "v", [shape_of(groups, 40, 128)], "v", limit=4)
    whole = exchange(spread_out)
    (state_grad,) = call(
        grad_kernel, (gc_all, halo, cot, taps, shift, spread), "hhhvvv", [field], "h"
    )
    scale = 1.0 / math.sqrt(T * CELLS * groups * batch)

    def unpack(*refs):
        unpack_kernel(scale, *refs)

    mixer_grads, stencil_grads, shift_grads = call(
        unpack,
        (whole,),
        "v",
        [shape_of(2, 256, 256, dtype=F32), shape_of(9, 2, 256, dtype=F32), shape_of(2, 256, dtype=F32)],
        "hvv",
        limit=4,
    )
    stencil_grads = stencil_grads.swapaxes(0, 1)
    return (
        outcome.reshape(shape),
        state_grad.reshape(shape),
        mixer_grads,
        stencil_grads,
        shift_grads,
    )


def solution(mesh):
    torus = Mesh(
        mesh.devices.reshape(4, 4, 2, mesh.shape["batch"]), ("tile_0", "tile_1", "tile_2", "batch")
    )
    in_specs = (
        P("batch", TILE, None, None, None),
        P("batch", TILE, None, None, None),
        P(),
        P(),
        P(),
        P(),
        P(),
    )
    out_specs = (
        P("batch", TILE, None, None, None),
        P("batch", TILE, None, None, None),
        P(),
        P(),
        P(),
    )
    return jax.shard_map(
        whole_block, mesh=torus, in_specs=in_specs, out_specs=out_specs, check_vma=False
    )
```
